32 devices in a mesh: db: 16 (over z, x, core), mp: 2 (over y).
Axes of the slice: x: 2, y: 2, z: 4, core: 2. Of those that a mesh axis runs over, the one named last changes fastest.
Arguments:
- queries: bfloat16 [32768, 2048], P('db', 'mp'), may hold values from -400 to 400, as said below
- encodings: bfloat16 [512, 128, 896], P(('db', 'mp')), may hold values from -6 to 6
- key_weight: bfloat16 [896, 2048], P('db', 'mp'), may hold values from -0.1875 to 0.1875
- value_weight: bfloat16 [896, 2048], P('db', 'mp'), may hold values from -0.1875 to 0.1875
- nbr_shard: int32 [512, 2], P('db'), may hold values from 0 to 15, all different within a row; in each aligned block of 32 rows (0 to 31, 32 to 63, ...) at most 8 rows name the same one
- nbr_row: int32 [512, 2], P('db'), may hold values from 0 to 31
Outputs:
- cross_out: bfloat16 [32768, 2048], P('db', 'mp')
The draws below stay inside these ranges and needn't reach their ends.
Inputs may be any that keep to these rules, and one draw needn't show every extreme that they name: `queries`: some query rows may be far larger than the rest. `nbr_shard`: among the spans of one index of db no shard is named by more than 8 spans; the 2 shards of one span differ.
All inputs are finite; a program needn't handle non-finite values.
Results may differ from the reference program's by a relative error of at most 0.025.
Values may be sent and summed in bfloat16 or wider, within the bound.
No kernel may reach another device: no remote copies, remote signals or barrier semaphores. Data moves between devices by JAX's collectives and lax.ppermute only.
A program may use at most 256 MiB of HBM per device.

```python
import math
import jax
import jax.numpy as jnp
import numpy as np
from jax import lax

HEADS = 16
DH = 128
ENC = 896
SPAN = 64
NTOK = 128
NBR = 2
SEQ = 128
CH_DEV = 32
NB_DEV = 32
CAP = 8
HD = 2048
SPANS = 512
TOKENS = 32768
NEIGH = 512
N_DB = 16


def draw_queries(key, part):
    key_base = jax.random.fold_in(key, 0)
    drawn = jnp.clip(1.5 * jax.random.normal(key_base, (TOKENS, HD), jnp.float32), -9.0, 9.0)
    return drawn.astype(jnp.bfloat16)


def touch_ends(array, rng, smallest, high):
    shape = array.shape
    place = [jax.random.randint(jax.random.fold_in(rng, axis), (), 0, shape[axis]) for axis in range(len(shape))]
    array = array.at[tuple(place)].set(smallest)
    longest = shape.index(max(shape))
    place[longest] = (place[longest] + 1) % shape[longest]
    return array.at[tuple(place)].set(high)


def steps_of(stream_key, extent, cuts, low, high):
    loudness, own = 1.0, jax.random.fold_in(stream_key, 6)
    for position, blocks in cuts:
        draws = jnp.exp(jax.random.uniform(jax.random.fold_in(own, position), (blocks,), jnp.float32, low / len(cuts), high / len(cuts)))
        loudness = loudness * jnp.repeat(draws, extent[position] // blocks).reshape([-1 if axis == position else 1 for axis in range(len(extent))])
    return loudness


def assign_block(own_key, own, number, rows, number_of, top, bound, lean):
    order = jax.random.permutation(own_key, number_of)
    heavy_load, usual = load_shares(number_of, rows * top, bound, lean, True), load_shares(number_of, rows * top, bound, lean, False)
    places = jnp.arange(number_of)

    def named(tallies, turn):
        used = int((tallies > 0).sum())
        fixed = max(1, used // 4)
        moved = fixed + (places - fixed + turn * (used - fixed)) % max(1, number_of - fixed)
        return jnp.zeros((number_of,), jnp.int32).at[order[jnp.where(places < fixed, places, moved)]].set(jnp.asarray(tallies, jnp.int32))

    tallies = jnp.where(number % 4 == 0, named(heavy_load, number // 4), named(usual, number - number // 4 - 1))
    mixed = jax.random.permutation(jax.random.fold_in(own, 3), number_of)
    donor, taker = mixed[0:number_of // 2 * 2:2], mixed[1:number_of // 2 * 2:2]
    slack = jnp.minimum(tallies[donor] - 1, bound - tallies[taker]) // 2
    slack = jnp.where((donor == order[0]) | (taker == order[0]) | (tallies[taker] == 0), 0, jnp.maximum(slack, 0))
    moved = jax.random.randint(jax.random.fold_in(own, 4), (number_of // 2,), 0, 1 << 20) % (slack + 1)
    tallies = tallies.at[donor].add(-moved).at[taker].add(moved)
    labels = jnp.searchsorted(jnp.cumsum(tallies), jnp.arange(rows * top), side="right").astype(jnp.int32)
    grid = labels.reshape(top, rows).T
    grid = grid[jax.random.permutation(jax.random.fold_in(own, 1), rows)]
    turn = jax.random.randint(jax.random.fold_in(own, 2), (rows, 1), 0, top)
    return jnp.take_along_axis(grid, (jnp.arange(top)[None, :] + turn) % top, axis=1)


def load_shares(number_of, total, limit, lean, full):
    portions = [(1 << 20) // math.isqrt(standing ** lean) + 1 for standing in range(1, number_of + 1)]
    largest = limit if full else min(limit, max(-(-total // number_of), total * portions[0] // sum(portions)))
    least = 1 if total - largest >= number_of - 1 else 0
    counts, spare = [largest] + [least] * (number_of - 1), total - largest - least * (number_of - 1)
    while spare > 0:
        movable = [i for i in range(1, number_of) if counts[i] < largest] or [i for i in range(1, number_of) if counts[i] < limit]
        mass, left = sum([portions[i] for i in movable]), spare
        for i in movable:
            addition = min(limit - counts[i], max(1, left * portions[i] // mass), spare)
            counts[i] = counts[i] + addition
            spare = spare - addition
    return np.array(counts)


def centred(stream_key, extent, scale, most, cuts=(), dtype=jnp.bfloat16):
    level = steps_of(stream_key, extent, cuts, -0.22, 0.18) if cuts else 1.0
    entries = jax.random.normal(stream_key, extent, jnp.float32) * scale * level
    return jnp.minimum(jnp.maximum(entries, -most), most).astype(dtype)


def setup_inputs(seed: int = 0) -> dict:
    seeds = jax.random.split(jax.random.key(seed), 7)
    queries = draw_queries(jax.random.fold_in(seeds[6], 71), 0)
    encodings = centred(seeds[1], (NEIGH, NTOK, ENC), 1.0, 6.0, ((0, 32),))
    key_weight = centred(seeds[2], (ENC, HD), ENC ** -0.5, 0.1875, ((0, 16), (1, 2)))
    value_weight = centred(seeds[3], (ENC, HD), ENC ** -0.5, 0.1875, ((0, 16), (1, 2)))
    nbr_shard_keys = jax.random.split(jax.random.fold_in(seeds[4], 1), SPANS // CH_DEV)
    nbr_shard_turns = jax.random.permutation(jax.random.fold_in(seeds[4], 3), SPANS // CH_DEV)
    nbr_shard = jax.vmap(lambda own, number: assign_block(jax.random.fold_in(seeds[4], 2), own, number, CH_DEV, N_DB, NBR, CAP, 2))(nbr_shard_keys, nbr_shard_turns).reshape((SPANS, NBR))
    nbr_row = touch_ends(jax.random.randint(seeds[5], (SPANS, NBR), 0, NB_DEV), jax.random.fold_in(seeds[5], 1), 0, NB_DEV - 1).astype(jnp.int32)
    return {"queries": queries, "encodings": encodings, "key_weight": key_weight, "value_weight": value_weight, "nbr_shard": nbr_shard, "nbr_row": nbr_row}


def reference(queries, encodings, key_weight, value_weight, nbr_shard, nbr_row):
    score_scale = 1.0 / math.sqrt(DH)

    def project(neighbour_block):
        key_rows = jnp.dot(neighbour_block, key_weight, preferred_element_type=jnp.float32).astype(jnp.bfloat16)
        value_rows = jnp.dot(neighbour_block, value_weight, preferred_element_type=jnp.float32).astype(jnp.bfloat16)
        return (key_rows, value_rows)
    keys, values = lax.map(project, encodings)
    sequences = TOKENS // SEQ
    seq_rows = queries.reshape(sequences, SEQ, HD)
    shifted = jnp.concatenate([seq_rows[:, SPAN - 1:], jnp.zeros((sequences, SPAN - 1, HD), jnp.bfloat16)], axis=1)
    windows = shifted.reshape(SPANS, SPAN, HEADS, DH)
    neighbour = (nbr_shard * NB_DEV + nbr_row).astype(jnp.int32)

    def attend(operands):
        window_rows, chosen = operands
        key_heads = jnp.take(keys, chosen, axis=0).reshape(NBR, NTOK, HEADS, DH)
        value_heads = jnp.take(values, chosen, axis=0).reshape(NBR, NTOK, HEADS, DH)
        scores = jnp.einsum('qhd,jkhd->jhqk', window_rows.astype(jnp.float32), key_heads.astype(jnp.float32)) * score_scale
        row_max = lax.optimization_barrier(jnp.max(scores, axis=-1))
        expscore = jnp.exp(scores - row_max[..., None])
        row_sum = lax.optimization_barrier(jnp.sum(expscore, axis=-1))
        probabilities = lax.optimization_barrier(expscore.astype(jnp.bfloat16)).astype(jnp.float32)
        partial_value = jnp.einsum('jhqk,jkhd->jqhd', probabilities, value_heads.astype(jnp.float32))
        partial_value = lax.optimization_barrier(partial_value.astype(jnp.bfloat16)).astype(jnp.float32)
        largest = lax.optimization_barrier(jnp.max(row_max, axis=0))
        weights_each = jnp.exp(row_max - largest[None])
        denominator = lax.optimization_barrier(jnp.sum(weights_each * row_sum, axis=0))
        numerator = lax.optimization_barrier(jnp.sum(jnp.transpose(weights_each, (0, 2, 1))[..., None] * partial_value, axis=0))
        return (numerator / jnp.transpose(denominator)[..., None]).astype(jnp.bfloat16)
    attended = lax.map(attend, (windows, neighbour))
    attended = attended.reshape(sequences, SEQ, HD)
    result = jnp.concatenate([jnp.zeros((sequences, SPAN - 1, HD), jnp.bfloat16), attended[:, :SEQ - SPAN + 1]], axis=1)
    return result.reshape(TOKENS, HD)
```

```python
import functools
import math

import jax
import jax.numpy as jnp
from jax import lax
from jax.experimental import pallas as pl
from jax.experimental.pallas import tpu as pltpu
from jax.sharding import PartitionSpec as P

DH = 128
SPAN = 64
SEQ = 128
LANES = 8
FAST_SLOTS = 48
BF16 = jnp.bfloat16
F32 = jnp.float32
SCALE = 1.0 / math.sqrt(DH)
BOTH = ("db", "mp")
CONTRACT_LAST = (((1,), (1,)), ((), ()))


def even_body(slot_ref, query_ref, rows_ref, weight_ref, odd_ref, out_ref, *, per_step, neighbours):
    columns = query_ref.shape[1]
    heads = columns // DH
    lanes, _, piece, width = rows_ref.shape
    tokens = lanes * piece
    first = SPAN - 1
    low = first // 16 * 16
    rows = rows_ref[...]
    stacked = jnp.concatenate(
        [rows[:, j].reshape(tokens, width) for j in range(per_step * neighbours)], axis=0
    )
    projected = jnp.dot(stacked, weight_ref[...], preferred_element_type=F32).astype(BF16)
    position = low + lax.broadcasted_iota(jnp.int32, (SEQ - low, DH), 0)
    span = neighbours * tokens
    for s in range(per_step):
        own = projected[s * span : (s + 1) * span]
        sequence = pl.program_id(0) * per_step + s
        picked = [odd_ref[pl.ds(slot_ref[sequence * neighbours + j], 1), :] for j in range(neighbours)]
        out_ref[s * SEQ : s * SEQ + low, :] = jnp.zeros((low, columns), BF16)
        for h in range(heads):
            lo, hi = h * DH, (h + 1) * DH
            query = query_ref[s * SEQ + low : (s + 1) * SEQ, lo:hi]
            scores = (
                lax.dot_general(query, own[:, lo:hi], CONTRACT_LAST, preferred_element_type=F32) * SCALE
            )
            largest = jnp.max(scores, axis=1, keepdims=True)
            expscore = jnp.exp(scores - largest)
            total = jnp.sum(expscore, axis=1, keepdims=True)
            mixed = jnp.dot(
                expscore.astype(BF16), own[:, columns + lo : columns + hi], preferred_element_type=F32
            )
            attended = mixed / total
            maxima = [p[:, columns + h : columns + h + 1] for p in picked]
            sums = [p[:, columns + DH // 2 + h : columns + DH // 2 + h + 1] for p in picked]
            top = functools.reduce(jnp.maximum, maxima)
            each = [jnp.exp(m - top) for m in maxima]
            under = sum(e * t for e, t in zip(each, sums))
            over = sum(e * p[:, lo:hi] for e, p in zip(each, picked))
            odd = over / under
            attended = jnp.where(position == SEQ - 1, odd, attended)
            attended = jnp.where(position < first, 0.0, attended)
            out_ref[s * SEQ + low : (s + 1) * SEQ, lo:hi] = attended.astype(BF16)


def even_attention(slots, queries, rows, weights, odd):
    tokens, columns = queries.shape
    sequences = tokens // SEQ
    lanes, count, piece, width = rows.shape
    neighbours = count // sequences
    per_step = math.gcd(sequences, 2)
    return pl.pallas_call(
        functools.partial(even_body, per_step=per_step, neighbours=neighbours),
        out_shape=jax.ShapeDtypeStruct(queries.shape, BF16),
        grid_spec=pltpu.PrefetchScalarGridSpec(
            num_scalar_prefetch=1,
            grid=(sequences // per_step,),
            in_specs=[
                pl.BlockSpec((per_step * SEQ, columns), lambda i, s: (i, 0)),
                pl.BlockSpec((lanes, per_step * neighbours, piece, width), lambda i, s: (0, i, 0, 0)),
                pl.BlockSpec(weights.shape, lambda i, s: (0, 0)),
                pl.BlockSpec(odd.shape, lambda i, s: (0, 0)),
            ],
            out_specs=pl.BlockSpec((per_step * SEQ, columns), lambda i, s: (i, 0)),
        ),
        name="even_attention",
    )(slots, queries, rows, weights, odd)


def odd_body(query_ref, want_ref, rows_ref, weight_ref, out_ref):
    columns = query_ref.shape[1]
    heads = columns // DH
    per_step, tokens, width = rows_ref.shape
    base = pl.program_id(0) * per_step
    projected = jnp.dot(
        rows_ref[...].reshape(per_step * tokens, width), weight_ref[...], preferred_element_type=F32
    ).astype(BF16)
    want = want_ref[...] - base
    here = [want == r for r in range(per_step)]
    inside = (want >= 0) & (want < per_step)
    lane = lax.broadcasted_iota(jnp.int32, (want.shape[0], DH), 1)
    stats = out_ref[:, columns:]
    for h in range(heads):
        lo, hi = h * DH, (h + 1) * DH
        scores = (
            lax.dot_general(
                query_ref[:, lo:hi], projected[:, lo:hi], CONTRACT_LAST, preferred_element_type=F32
            )
            * SCALE
        )
        mine = jnp.zeros((want.shape[0], tokens), F32)
        for r in range(per_step):
            mine = jnp.where(here[r], scores[:, r * tokens : (r + 1) * tokens], mine)
        largest = jnp.max(mine, axis=1, keepdims=True)
        expscore = jnp.exp(mine - largest)
        total = jnp.sum(expscore, axis=1, keepdims=True)
        spread = jnp.concatenate([jnp.where(here[r], expscore, 0.0) for r in range(per_step)], axis=1)
        mixed = jnp.dot(spread.astype(BF16), projected[:, columns + lo : columns + hi], preferred_element_type=F32)
        out_ref[:, lo:hi] = jnp.where(inside, mixed, out_ref[:, lo:hi])
        stats = jnp.where(inside & (lane == h), largest, stats)
        stats = jnp.where(inside & (lane == DH // 2 + h), total, stats)
    out_ref[:, columns:] = stats


def odd_attention(queries, want, rows, weights):
    slots, columns = queries.shape
    count, tokens, width = rows.shape
    per_step = math.gcd(count, 4)
    return pl.pallas_call(
        odd_body,
        out_shape=jax.ShapeDtypeStruct((slots, columns + DH), F32),
        grid=(count // per_step,),
        in_specs=[
            pl.BlockSpec((slots, columns), lambda i: (0, 0)),
            pl.BlockSpec((slots, DH), lambda i: (0, 0)),
            pl.BlockSpec((per_step, tokens, width), lambda i: (i, 0, 0)),
            pl.BlockSpec(weights.shape, lambda i: (0, 0)),
        ],
        out_specs=pl.BlockSpec((slots, columns + DH), lambda i: (0, 0)),
        name="odd_attention",
    )(queries, want, rows, weights)


def local(queries, encodings, key_weight, value_weight, nbr_shard, nbr_row):
    shards = lax.axis_size("db")
    parts = lax.axis_size("mp")
    group = max(1, LANES // parts)
    lanes = group * parts
    planes = shards // group
    columns = queries.shape[1]
    held, tokens, width = encodings.shape
    piece = tokens // lanes
    shard_rows = held * parts
    plane_rows = group * shard_rows
    span_count, neighbours = nbr_shard.shape
    sequences = queries.shape[0] // SEQ
    wanted = sequences * neighbours
    capacity = max(2, 4 * span_count // shards)
    most = min(plane_rows, group * wanted, group * group * capacity)
    fast = min(most, FAST_SLOTS)
    plane_groups = [[a * lanes + b for b in range(lanes)] for a in range(planes)]
    lane_groups = [[a * lanes + b for a in range(planes)] for b in range(lanes)]
    db_index = lax.axis_index("db")
    plane_index = db_index // group

    def swap(x, groups):
        return lax.all_to_all(x, BOTH, 0, 0, axis_index_groups=groups, tiled=True)

    table = jnp.concatenate([nbr_shard.reshape(-1), nbr_row.reshape(-1)])
    table = jnp.broadcast_to(table[None, None], (shards, 1, table.shape[0]))
    table = lax.all_to_all(table, "db", 0, 0, tiled=True).reshape(
        shards, 2, sequences, SEQ // SPAN, neighbours
    )
    table_shard, table_row = table[:, 0], table[:, 1]

    pieces = jnp.transpose(encodings.reshape(held, lanes, piece, width), (1, 0, 2, 3))
    plane_pieces = swap(pieces.reshape(lanes * held, piece, width), plane_groups)

    weights = lax.all_gather(jnp.concatenate([key_weight, value_weight], axis=1), "db", axis=0, tiled=True)

    even_id = (table_shard[:, :, 0] * shard_rows + table_row[:, :, 0]).reshape(planes, group * wanted)
    ids = jnp.arange(planes * plane_rows, dtype=jnp.int32)
    want = jnp.any(even_id[:, :, None] == ids[None, None, :], axis=1).reshape(planes, planes, plane_rows)
    below = jnp.arange(plane_rows)
    before = (below[:, None] < below[None, :]).astype(BF16)
    rank = jnp.dot(want.astype(BF16), before, preferred_element_type=F32).astype(jnp.int32)
    fits = jnp.max(jnp.sum(want.astype(jnp.int32), axis=2)) <= fast
    mine_want = lax.dynamic_index_in_dim(want, plane_index, 1, keepdims=False)
    mine_rank = lax.dynamic_index_in_dim(rank, plane_index, 1, keepdims=False)
    picks = mine_want[:, None, :] & (
        mine_rank[:, None, :] == jnp.arange(fast, dtype=jnp.int32)[None, :, None]
    )
    send_rows = jnp.sum(jnp.where(picks, below[None, None, :].astype(jnp.int32), 0), axis=2)
    my_ids = lax.dynamic_index_in_dim(even_id, plane_index, 0, keepdims=False)
    my_rank = lax.dynamic_index_in_dim(rank, plane_index, 0, keepdims=False).reshape(-1)
    place = jnp.sum(jnp.where(my_ids[:, None] == ids[None, :], my_rank[None, :], 0), axis=1)
    my_plane = my_ids // plane_rows

    def finish(received, index):
        picked = jnp.take(received, index, axis=0, mode="clip").reshape(group, 1, wanted, piece, width)
        return jnp.broadcast_to(picked, (group, parts, wanted, piece, width)).reshape(
            lanes * wanted, piece, width
        )

    def exact(source):
        sending = jnp.take(source, send_rows.reshape(-1), axis=0, mode="clip")
        return finish(swap(sending, lane_groups), my_plane * fast + place)

    def whole(source):
        sending = jnp.broadcast_to(source[None], (planes,) + source.shape)
        received = swap(sending.reshape((planes * plane_rows,) + source.shape[1:]), lane_groups)
        return finish(received, my_ids)

    if fast < most:
        outgoing = lax.cond(fits, exact, whole, plane_pieces)
    else:
        outgoing = exact(plane_pieces)
    even_rows = swap(outgoing, plane_groups).reshape(lanes, wanted, piece, width)

    odd_shard = table_shard[:, :, 1].reshape(shards, wanted)
    odd_row = table_row[:, :, 1].reshape(shards, wanted)
    earlier = jnp.arange(wanted)
    same = (odd_shard[:, :, None] == odd_shard[:, None, :]) & (earlier[None, None, :] < earlier[None, :, None])
    odd_rank = jnp.sum(same.astype(jnp.int32), axis=2)
    arriving = (odd_shard == db_index)[:, None, :] & (
        odd_rank[:, None, :] == jnp.arange(capacity, dtype=jnp.int32)[None, :, None]
    )
    slot_row = jnp.sum(jnp.where(arriving, odd_row[:, None, :] + 1, 0), axis=2) - 1
    my_slot = lax.dynamic_index_in_dim(odd_shard * capacity + odd_rank, db_index, 0, keepdims=False)
    slots = jnp.arange(shards * capacity, dtype=jnp.int32)
    chosen = my_slot[None, :] == slots[:, None]
    sender = jnp.sum(jnp.where(chosen, (earlier // neighbours).astype(jnp.int32)[None, :], 0), axis=1)
    last_rows = queries.reshape(sequences, SEQ, columns)[:, SEQ - 1]
    odd_query = jnp.take(last_rows, sender, axis=0, mode="clip").reshape(shards, capacity, columns)
    odd_query = lax.all_to_all(odd_query, "db", 0, 0, tiled=True).reshape(shards * capacity, columns)

    held_rows, _ = lax.optimization_barrier((encodings, plane_pieces))
    shard_enc = lax.all_gather(held_rows, "mp", axis=0, tiled=True)
    shard_enc, _ = lax.optimization_barrier((shard_enc, outgoing))
    slot_lanes = jnp.broadcast_to(slot_row.reshape(-1, 1), (shards * capacity, DH))
    odd_part = odd_attention(odd_query, slot_lanes, shard_enc, weights)
    odd_part = lax.all_to_all(
        odd_part.reshape(shards, capacity, columns + DH), "db", 0, 0, tiled=True
    ).reshape(shards * capacity, columns + DH)

    return even_attention(my_slot, queries, even_rows, weights, odd_part)


def solution(mesh):
    placed = (
        P("db", "mp"),
        P(("db", "mp"), None, None),
        P("db", "mp"),
        P("db", "mp"),
        P("db", None),
        P("db", None),
    )
    return jax.shard_map(
        local, mesh=mesh, in_specs=placed, out_specs=P("db", "mp"), check_vma=False
    )
```

```python
import functools
import math

import jax
import jax.numpy as jnp
from jax import lax
from jax.experimental import pallas as pl
from jax.experimental.pallas import tpu as pltpu
from jax.sharding import PartitionSpec as P

DH = 128
SPAN = 64
SEQ = 128
LANES = 8
CHUNKS = 2
MOST_SHIFTS = 8
FAST_SLOTS = 48
BF16 = jnp.bfloat16
F32 = jnp.float32
SCALE = 1.0 / math.sqrt(DH)
BOTH = ("db", "mp")
CONTRACT_LAST = (((1,), (1,)), ((), ()))


def project_body(rows_ref, weight_ref, out_ref):
    lanes, count, piece, width = rows_ref.shape
    rows = rows_ref[...]
    stacked = jnp.concatenate([rows[:, j].reshape(lanes * piece, width) for j in range(count)], axis=0)
    out_ref[...] = jnp.dot(stacked, weight_ref[...], preferred_element_type=F32).astype(BF16)


def project(rows, weights):
    lanes, count, piece, width = rows.shape
    per_step = math.gcd(count, 8)
    tokens = lanes * piece
    return pl.pallas_call(
        project_body,
        out_shape=jax.ShapeDtypeStruct((count * tokens, weights.shape[1]), BF16),
        grid=(count // per_step,),
        in_specs=[
            pl.BlockSpec((lanes, per_step, piece, width), lambda i: (0, i, 0, 0)),
            pl.BlockSpec(weights.shape, lambda i: (0, 0)),
        ],
        out_specs=pl.BlockSpec((per_step * tokens, weights.shape[1]), lambda i: (i, 0)),
        name="project",
    )(rows, weights)


def even_body(slot_ref, query_ref, rows_ref, weight_ref, early_ref, odd_ref, out_ref, *, per_step, neighbours):
    columns = query_ref.shape[1]
    heads = columns // DH
    lanes, _, piece, width = rows_ref.shape
    tokens = lanes * piece
    first = SPAN - 1
    low = first // 16 * 16
    rows = rows_ref[...]
    stacked = jnp.concatenate(
        [rows[:, j].reshape(tokens, width) for j in range(per_step * neighbours)], axis=0
    )
    late = jnp.dot(stacked, weight_ref[...], preferred_element_type=F32).astype(BF16)
    position = low + lax.broadcasted_iota(jnp.int32, (SEQ - low, DH), 0)
    span = neighbours * tokens
    early_span = early_ref.shape[0] // per_step
    for s in range(per_step):
        sequence = pl.program_id(0) * per_step + s
        picked = [odd_ref[pl.ds(slot_ref[sequence * neighbours + j], 1), :] for j in range(neighbours)]
        out_ref[s * SEQ : s * SEQ + low, :] = jnp.zeros((low, columns), BF16)
        for h in range(heads):
            lo, hi = h * DH, (h + 1) * DH
            parts = [(early_ref, s * early_span, early_span), (late, s * span, span)]
            keys = jnp.concatenate([r[b : b + n, lo:hi] for r, b, n in parts], axis=0)
            values = jnp.concatenate([r[b : b + n, columns + lo : columns + hi] for r, b, n in parts], axis=0)
            query = query_ref[s * SEQ + low : (s + 1) * SEQ, lo:hi]
            scores = lax.dot_general(query, keys, CONTRACT_LAST, preferred_element_type=F32) * SCALE
            largest = jnp.max(scores, axis=1, keepdims=True)
            expscore = jnp.exp(scores - largest)
            total = jnp.sum(expscore, axis=1, keepdims=True)
            mixed = jnp.dot(expscore.astype(BF16), values, preferred_element_type=F32)
            attended = mixed / total
            maxima = [p[:, columns + h : columns + h + 1] for p in picked]
            sums = [p[:, columns + DH // 2 + h : columns + DH // 2 + h + 1] for p in picked]
            top = functools.reduce(jnp.maximum, maxima)
            each = [jnp.exp(m - top) for m in maxima]
            under = sum(e * t for e, t in zip(each, sums))
            over = sum(e * p[:, lo:hi] for e, p in zip(each, picked))
            odd = over / under
            attended = jnp.where(position == SEQ - 1, odd, attended)
            attended = jnp.where(position < first, 0.0, attended)
            out_ref[s * SEQ + low : (s + 1) * SEQ, lo:hi] = attended.astype(BF16)


def even_attention(slots, queries, rows, weights, early, odd):
    tokens, columns = queries.shape
    sequences = tokens // SEQ
    lanes, count, piece, width = rows.shape
    neighbours = count // sequences
    per_step = math.gcd(sequences, 2)
    early_rows = early.shape[0] // sequences * per_step
    return pl.pallas_call(
        functools.partial(even_body, per_step=per_step, neighbours=neighbours),
        out_shape=jax.ShapeDtypeStruct(queries.shape, BF16),
        grid_spec=pltpu.PrefetchScalarGridSpec(
            num_scalar_prefetch=1,
            grid=(sequences // per_step,),
            in_specs=[
                pl.BlockSpec((per_step * SEQ, columns), lambda i, s: (i, 0)),
                pl.BlockSpec((lanes, per_step * neighbours, piece, width), lambda i, s: (0, i, 0, 0)),
                pl.BlockSpec(weights.shape, lambda i, s: (0, 0)),
                pl.BlockSpec((early_rows, weights.shape[1]), lambda i, s: (i, 0)),
                pl.BlockSpec(odd.shape, lambda i, s: (0, 0)),
            ],
            out_specs=pl.BlockSpec((per_step * SEQ, columns), lambda i, s: (i, 0)),
        ),
        name="even_attention",
    )(slots, queries, rows, weights, early, odd)


def odd_body(query_ref, want_ref, rows_ref, weight_ref, out_ref):
    columns = query_ref.shape[1]
    heads = columns // DH
    per_step, tokens, width = rows_ref.shape
    base = pl.program_id(0) * per_step
    projected = jnp.dot(
        rows_ref[...].reshape(per_step * tokens, width), weight_ref[...], preferred_element_type=F32
    ).astype(BF16)
    want = want_ref[...] - base
    here = [want == r for r in range(per_step)]
    inside = (want >= 0) & (want < per_step)
    lane = lax.broadcasted_iota(jnp.int32, (want.shape[0], DH), 1)
    stats = out_ref[:, columns:]
    for h in range(heads):
        lo, hi = h * DH, (h + 1) * DH
        scores = (
            lax.dot_general(
                query_ref[:, lo:hi], projected[:, lo:hi], CONTRACT_LAST, preferred_element_type=F32
            )
            * SCALE
        )
        mine = jnp.zeros((want.shape[0], tokens), F32)
        for r in range(per_step):
            mine = jnp.where(here[r], scores[:, r * tokens : (r + 1) * tokens], mine)
        largest = jnp.max(mine, axis=1, keepdims=True)
        expscore = jnp.exp(mine - largest)
        total = jnp.sum(expscore, axis=1, keepdims=True)
        spread = jnp.concatenate([jnp.where(here[r], expscore, 0.0) for r in range(per_step)], axis=1)
        mixed = jnp.dot(spread.astype(BF16), projected[:, columns + lo : columns + hi], preferred_element_type=F32)
        out_ref[:, lo:hi] = jnp.where(inside, mixed, out_ref[:, lo:hi])
        stats = jnp.where(inside & (lane == h), largest, stats)
        stats = jnp.where(inside & (lane == DH // 2 + h), total, stats)
    out_ref[:, columns:] = stats


def odd_attention(queries, want, rows, weights):
    slots, columns = queries.shape
    count, tokens, width = rows.shape
    per_step = math.gcd(count, 4)
    return pl.pallas_call(
        odd_body,
        out_shape=jax.ShapeDtypeStruct((slots, columns + DH), F32),
        grid=(count // per_step,),
        in_specs=[
            pl.BlockSpec((slots, columns), lambda i: (0, 0)),
            pl.BlockSpec((slots, DH), lambda i: (0, 0)),
            pl.BlockSpec((per_step, tokens, width), lambda i: (i, 0, 0)),
            pl.BlockSpec(weights.shape, lambda i: (0, 0)),
        ],
        out_specs=pl.BlockSpec((slots, columns + DH), lambda i: (0, 0)),
        name="odd_attention",
    )(queries, want, rows, weights)


def local(queries, encodings, key_weight, value_weight, nbr_shard, nbr_row):
    shards = lax.axis_size("db")
    parts = lax.axis_size("mp")
    group = max(1, LANES // parts)
    lanes = group * parts
    planes = shards // group
    columns = queries.shape[1]
    held, tokens, width = encodings.shape
    piece = tokens // (lanes * CHUNKS)
    shard_rows = held * parts
    plane_rows = group * shard_rows
    span_count, neighbours = nbr_shard.shape
    sequences = queries.shape[0] // SEQ
    wanted = sequences * neighbours
    capacity = max(2, 4 * span_count // shards)
    most = min(plane_rows, group * wanted, group * group * capacity)
    fast = min(most, FAST_SLOTS)
    plane_groups = [[a * lanes + b for b in range(lanes)] for a in range(planes)]
    lane_groups = [[a * lanes + b for a in range(planes)] for b in range(lanes)]
    db_index = lax.axis_index("db")
    plane_index = db_index // group

    def swap(x, groups):
        return lax.all_to_all(x, BOTH, 0, 0, axis_index_groups=groups, tiled=True)

    def across(blocks):
        if planes > MOST_SHIFTS:
            ordered = jnp.take(blocks, (jnp.arange(planes) - plane_index) % planes, axis=0, mode="clip")
            ordered = swap(ordered.reshape((-1,) + blocks.shape[2:]), lane_groups).reshape(blocks.shape)
            moved = jnp.take(ordered, (plane_index - jnp.arange(planes)) % planes, axis=0, mode="clip")
            return moved.reshape((-1,) + blocks.shape[2:])
        moved = [blocks[0]]
        for k in range(1, planes):
            pairs = [
                (a * lanes + b, (a + k) % planes * lanes + b) for a in range(planes) for b in range(lanes)
            ]
            moved.append(lax.ppermute(blocks[k], BOTH, pairs))
        return jnp.concatenate(moved, axis=0)

    table = jnp.concatenate([nbr_shard.reshape(-1), nbr_row.reshape(-1)])
    table = jnp.broadcast_to(table[None, None], (shards, 1, table.shape[0]))
    table = lax.all_to_all(table, "db", 0, 0, tiled=True).reshape(
        shards, 2, sequences, SEQ // SPAN, neighbours
    )
    table_shard, table_row = table[:, 0], table[:, 1]

    weights = lax.all_gather(jnp.concatenate([key_weight, value_weight], axis=1), "db", axis=0, tiled=True)

    pieces = jnp.transpose(encodings.reshape(held, lanes, CHUNKS, piece, width), (2, 1, 0, 3, 4))
    plane_pieces = []
    for chunk in range(CHUNKS):
        sending = pieces[chunk].reshape(lanes * held, piece, width)
        if chunk:
            sending, _ = lax.optimization_barrier((sending, plane_pieces[-1]))
        plane_pieces.append(swap(sending, plane_groups))

    even_id = (table_shard[:, :, 0] * shard_rows + table_row[:, :, 0]).reshape(planes, group * wanted)
    ids = jnp.arange(planes * plane_rows, dtype=jnp.int32)
    want = jnp.any(even_id[:, :, None] == ids[None, None, :], axis=1).reshape(planes, planes, plane_rows)
    below = jnp.arange(plane_rows)
    before = (below[:, None] < below[None, :]).astype(BF16)
    rank = jnp.dot(want.astype(BF16), before, preferred_element_type=F32).astype(jnp.int32)
    fits = jnp.max(jnp.sum(want.astype(jnp.int32), axis=2)) <= fast
    mine_want = lax.dynamic_index_in_dim(want, plane_index, 1, keepdims=False)
    mine_rank = lax.dynamic_index_in_dim(rank, plane_index, 1, keepdims=False)
    picks = mine_want[:, None, :] & (
        mine_rank[:, None, :] == jnp.arange(fast, dtype=jnp.int32)[None, :, None]
    )
    send_rows = jnp.sum(jnp.where(picks, below[None, None, :].astype(jnp.int32), 0), axis=2)
    steps = jnp.arange(planes, dtype=jnp.int32)
    upward = (plane_index + steps) % planes
    send_rows = jnp.sum(
        jnp.where(upward[:, None, None] == steps[None, :, None], send_rows[None], 0), axis=1
    )
    my_ids = lax.dynamic_index_in_dim(even_id, plane_index, 0, keepdims=False)
    my_rank = lax.dynamic_index_in_dim(rank, plane_index, 0, keepdims=False).reshape(-1)
    place = jnp.sum(jnp.where(my_ids[:, None] == ids[None, :], my_rank[None, :], 0), axis=1)
    my_step = (plane_index + planes - my_ids // plane_rows) % planes

    def finish(received, index):
        picked = jnp.take(received, index, axis=0, mode="clip").reshape(group, 1, wanted, piece, width)
        return jnp.broadcast_to(picked, (group, parts, wanted, piece, width)).reshape(
            lanes * wanted, piece, width
        )

    def exact(source):
        taken = jnp.take(source, send_rows.reshape(-1), axis=0, mode="clip")
        return taken.reshape((planes, fast) + source.shape[1:])

    def whole(source):
        return jnp.broadcast_to(source[None], (planes,) + source.shape)

    def exchange(sources, select, index):
        received, arrived = [], []
        for source in sources:
            sending = select(source)
            if received:
                sending, _ = lax.optimization_barrier((sending, received[-1]))
            received.append(across(sending))
            outgoing = finish(received[-1], index)
            if arrived:
                outgoing, _ = lax.optimization_barrier((outgoing, arrived[-1]))
            arrived.append(swap(outgoing, plane_groups))
        return [a.reshape(lanes, wanted, piece, width) for a in arrived]

    odd_shard = table_shard[:, :, 1].reshape(shards, wanted)
    odd_row = table_row[:, :, 1].reshape(shards, wanted)
    earlier = jnp.arange(wanted)
    same = (odd_shard[:, :, None] == odd_shard[:, None, :]) & (earlier[None, None, :] < earlier[None, :, None])
    odd_rank = jnp.sum(same.astype(jnp.int32), axis=2)
    arriving = (odd_shard == db_index)[:, None, :] & (
        odd_rank[:, None, :] == jnp.arange(capacity, dtype=jnp.int32)[None, :, None]
    )
    slot_row = jnp.sum(jnp.where(arriving, odd_row[:, None, :] + 1, 0), axis=2) - 1
    my_slot = lax.dynamic_index_in_dim(odd_shard * capacity + odd_rank, db_index, 0, keepdims=False)
    slots = jnp.arange(shards * capacity, dtype=jnp.int32)
    chosen = my_slot[None, :] == slots[:, None]
    sender = jnp.sum(jnp.where(chosen, (earlier // neighbours).astype(jnp.int32)[None, :], 0), axis=1)
    last_rows = queries.reshape(sequences, SEQ, columns)[:, SEQ - 1]
    odd_query = jnp.take(last_rows, sender, axis=0, mode="clip").reshape(shards, capacity, columns)
    odd_query = lax.all_to_all(odd_query, "db", 0, 0, tiled=True).reshape(shards * capacity, columns)

    part_index = lax.axis_index("mp")
    sharing, _ = lax.optimization_barrier((encodings, plane_pieces[-1]))
    shared = [encodings]
    for k in range(1, parts):
        shared.append(lax.ppermute(sharing, "mp", [(m, (m + k) % parts) for m in range(parts)]))
    shard_enc = jnp.concatenate(shared, axis=0)
    slot_step = (part_index + parts - slot_row // held) % parts
    slot_row = jnp.where(slot_row >= 0, slot_step * held + slot_row % held, -1)
    slot_lanes = jnp.broadcast_to(slot_row.reshape(-1, 1), (shards * capacity, DH))
    odd_part = odd_attention(odd_query, slot_lanes, shard_enc, weights)
    odd_part = lax.all_to_all(
        odd_part.reshape(shards, capacity, columns + DH), "db", 0, 0, tiled=True
    ).reshape(shards * capacity, columns + DH)

    def attend(select, index):
        early, late = exchange(plane_pieces, select, index)
        return even_attention(my_slot, queries, late, weights, project(early, weights), odd_part)

    result = attend(exact, my_step * fast + place)
    if fast < most:
        result = lax.cond(fits, lambda done: done, lambda done: attend(whole, my_step * plane_rows + my_ids % plane_rows), result)
    return result


def solution(mesh):
    placed = (
        P("db", "mp"),
        P(("db", "mp"), None, None),
        P("db", "mp"),
        P("db", "mp"),
        P("db", None),
        P("db", None),
    )
    return jax.shard_map(
        local, mesh=mesh, in_specs=placed, out_specs=P("db", "mp"), check_vma=False
    )
```

```python
import functools
import math

import jax
import jax.numpy as jnp
from jax import lax
from jax.experimental import pallas as pl
from jax.experimental.pallas import tpu as pltpu
from jax.sharding import PartitionSpec as P


DH = 128
SPAN = 64
SEQ = 128
LANES = 8
CHUNKS = 2
MOST_SHIFTS = 8
TAIL = 16
FAST_SLOTS = 48
BF16 = jnp.bfloat16
F32 = jnp.float32
SCALE = 1.0 / math.sqrt(DH)
BOTH = ("db", "mp")
CONTRACT_LAST = (((1,), (1,)), ((), ()))


def project_body(rows_ref, weight_ref, out_ref):
    lanes, count, piece, width = rows_ref.shape
    rows = rows_ref[...]
    stacked = jnp.concatenate([rows[:, j].reshape(lanes * piece, width) for j in range(count)], axis=0)
    out_ref[...] = jnp.dot(stacked, weight_ref[...], preferred_element_type=F32).astype(BF16)


def project(rows, weights):
    lanes, count, piece, width = rows.shape
    per_step = math.gcd(count, 8)
    tokens = lanes * piece
    return pl.pallas_call(
        project_body,
        out_shape=jax.ShapeDtypeStruct((count * tokens, weights.shape[1]), BF16),
        grid=(count // per_step,),
        in_specs=[
            pl.BlockSpec((lanes, per_step, piece, width), lambda i: (0, i, 0, 0)),
            pl.BlockSpec(weights.shape, lambda i: (0, 0)),
        ],
        out_specs=pl.BlockSpec((per_step * tokens, weights.shape[1]), lambda i: (i, 0)),
        name="project",
    )(rows, weights)


def even_body(query_ref, rows_ref, weight_ref, *refs, per_step, neighbours):
    early_refs, out_ref = refs[:-1], refs[-1]
    columns = query_ref.shape[1]
    heads = columns // DH
    lanes, _, piece, width = rows_ref.shape
    tokens = lanes * piece
    first = SPAN - 1
    low = first // 16 * 16
    rows = rows_ref[...]
    stacked = jnp.concatenate(
        [rows[:, j].reshape(tokens, width) for j in range(per_step * neighbours)], axis=0
    )
    late = jnp.dot(stacked, weight_ref[...], preferred_element_type=F32).astype(BF16)
    position = low + lax.broadcasted_iota(jnp.int32, (SEQ - low, DH), 0)
    span = neighbours * tokens
    for s in range(per_step):
        out_ref[s * SEQ : s * SEQ + low, :] = jnp.zeros((low, columns), BF16)
        for h in range(heads):
            lo, hi = h * DH, (h + 1) * DH
            parts = [(r, s * span, span) for r in (*early_refs, late)]
            keys = jnp.concatenate([r[b : b + n, lo:hi] for r, b, n in parts], axis=0)
            values = jnp.concatenate([r[b : b + n, columns + lo : columns + hi] for r, b, n in parts], axis=0)
            query = query_ref[s * SEQ + low : (s + 1) * SEQ, lo:hi]
            scores = lax.dot_general(query, keys, CONTRACT_LAST, preferred_element_type=F32) * SCALE
            largest = jnp.max(scores, axis=1, keepdims=True)
            expscore = jnp.exp(scores - largest)
            total = jnp.sum(expscore, axis=1, keepdims=True)
            mixed = jnp.dot(expscore.astype(BF16), values, preferred_element_type=F32)
            attended = mixed / total
            attended = jnp.where(position < first, 0.0, attended)
            out_ref[s * SEQ + low : (s + 1) * SEQ, lo:hi] = attended.astype(BF16)


def even_attention(queries, rows, weights, early):
    tokens, columns = queries.shape
    sequences = tokens // SEQ
    lanes, count, piece, width = rows.shape
    neighbours = count // sequences
    per_step = math.gcd(sequences, 2)
    early_rows = lanes * piece * per_step * neighbours
    early_spec = pl.BlockSpec((early_rows, weights.shape[1]), lambda i: (i, 0))
    return pl.pallas_call(
        functools.partial(even_body, per_step=per_step, neighbours=neighbours),
        out_shape=jax.ShapeDtypeStruct(queries.shape, BF16),
        grid=(sequences // per_step,),
        in_specs=[
            pl.BlockSpec((per_step * SEQ, columns), lambda i: (i, 0)),
            pl.BlockSpec((lanes, per_step * neighbours, piece, width), lambda i: (0, i, 0, 0)),
            pl.BlockSpec(weights.shape, lambda i: (0, 0)),
            *[early_spec for _ in early],
        ],
        out_specs=pl.BlockSpec((per_step * SEQ, columns), lambda i: (i, 0)),
        name="even_attention",
    )(queries, rows, weights, *early)


def patch_body(slot_ref, out_in_ref, odd_ref, out_ref, *, neighbours):
    columns = out_ref.shape[1]
    heads = columns // DH
    sequence = pl.program_id(0)
    picked = [odd_ref[pl.ds(slot_ref[sequence * neighbours + j], 1), :] for j in range(neighbours)]
    last = lax.broadcasted_iota(jnp.int32, (TAIL, DH), 0) == TAIL - 1
    for h in range(heads):
        lo, hi = h * DH, (h + 1) * DH
        maxima = [p[:, columns + h : columns + h + 1] for p in picked]
        sums = [p[:, columns + DH // 2 + h : columns + DH // 2 + h + 1] for p in picked]
        top = functools.reduce(jnp.maximum, maxima)
        each = [jnp.exp(m - top) for m in maxima]
        under = sum(e * t for e, t in zip(each, sums))
        over = sum(e * p[:, lo:hi] for e, p in zip(each, picked))
        out_ref[:, lo:hi] = jnp.where(last, (over / under).astype(BF16), out_in_ref[:, lo:hi])


def patch(slots, out, odd):
    tokens, columns = out.shape
    sequences = tokens // SEQ
    tail = pl.BlockSpec((TAIL, columns), lambda i, s: (i * (SEQ // TAIL) + SEQ // TAIL - 1, 0))
    return pl.pallas_call(
        functools.partial(patch_body, neighbours=slots.shape[0] // sequences),
        out_shape=jax.ShapeDtypeStruct(out.shape, BF16),
        grid_spec=pltpu.PrefetchScalarGridSpec(
            num_scalar_prefetch=1,
            grid=(sequences,),
            in_specs=[tail, pl.BlockSpec(odd.shape, lambda i, s: (0, 0))],
            out_specs=tail,
        ),
        input_output_aliases={1: 0},
        name="patch",
    )(slots, out, odd)


def gather_body(index_ref, *refs, rows, copies):
    sources, out_ref, sem = refs[:-2], refs[-2], refs[-1]
    size = sources[0].shape[0]
    wanted = out_ref.shape[0] // (rows * copies)

    def step(i, carry):
        at = index_ref[i]
        base = i // wanted * (copies * wanted) + i % wanted
        for k, source in enumerate(sources):
            @pl.when((at >= k * size) & (at < (k + 1) * size))
            def _():
                for c in range(copies):
                    pltpu.make_async_copy(
                        source.at[at - k * size], out_ref.at[base + c * wanted], sem
                    ).start()

        return carry

    lax.fori_loop(0, rows * wanted, step, 0)
    whole = out_ref.at[pl.ds(0, rows * wanted * copies)]
    pltpu.make_async_copy(whole, whole, sem).wait()


def gather_rows(index, sources, groups, copies):
    total = index.shape[0] * copies
    return pl.pallas_call(
        functools.partial(gather_body, rows=groups, copies=copies),
        out_shape=jax.ShapeDtypeStruct((total,) + sources[0].shape[1:], sources[0].dtype),
        grid_spec=pltpu.PrefetchScalarGridSpec(
            num_scalar_prefetch=1,
            grid=(1,),
            in_specs=[pl.BlockSpec(memory_space=pl.ANY) for _ in sources],
            out_specs=pl.BlockSpec(memory_space=pl.ANY),
            scratch_shapes=[pltpu.SemaphoreType.DMA],
        ),
        name="gather_rows",
    )(index, *sources)


def odd_body(query_ref, want_ref, rows_ref, weight_ref, out_ref):
    columns = query_ref.shape[1]
    heads = columns // DH
    per_step, tokens, width = rows_ref.shape
    base = pl.program_id(0) * per_step
    projected = jnp.dot(
        rows_ref[...].reshape(per_step * tokens, width), weight_ref[...], preferred_element_type=F32
    ).astype(BF16)
    want = want_ref[...] - base
    here = [want == r for r in range(per_step)]
    inside = (want >= 0) & (want < per_step)
    lane = lax.broadcasted_iota(jnp.int32, (want.shape[0], DH), 1)
    stats = out_ref[:, columns:]
    for h in range(heads):
        lo, hi = h * DH, (h + 1) * DH
        scores = (
            lax.dot_general(
                query_ref[:, lo:hi], projected[:, lo:hi], CONTRACT_LAST, preferred_element_type=F32
            )
            * SCALE
        )
        mine = jnp.zeros((want.shape[0], tokens), F32)
        for r in range(per_step):
            mine = jnp.where(here[r], scores[:, r * tokens : (r + 1) * tokens], mine)
        largest = jnp.max(mine, axis=1, keepdims=True)
        expscore = jnp.exp(mine - largest)
        total = jnp.sum(expscore, axis=1, keepdims=True)
        spread = jnp.concatenate([jnp.where(here[r], expscore, 0.0) for r in range(per_step)], axis=1)
        mixed = jnp.dot(spread.astype(BF16), projected[:, columns + lo : columns + hi], preferred_element_type=F32)
        out_ref[:, lo:hi] = jnp.where(inside, mixed, out_ref[:, lo:hi])
        stats = jnp.where(inside & (lane == h), largest, stats)
        stats = jnp.where(inside & (lane == DH // 2 + h), total, stats)
    out_ref[:, columns:] = stats


def odd_attention(queries, want, rows, weights):
    slots, columns = queries.shape
    count, tokens, width = rows.shape
    per_step = math.gcd(count, 4)
    return pl.pallas_call(
        odd_body,
        out_shape=jax.ShapeDtypeStruct((slots, columns + DH), F32),
        grid=(count // per_step,),
        in_specs=[
            pl.BlockSpec((slots, columns), lambda i: (0, 0)),
            pl.BlockSpec((slots, DH), lambda i: (0, 0)),
            pl.BlockSpec((per_step, tokens, width), lambda i: (i, 0, 0)),
            pl.BlockSpec(weights.shape, lambda i: (0, 0)),
        ],
        out_specs=pl.BlockSpec((slots, columns + DH), lambda i: (0, 0)),
        name="odd_attention",
    )(queries, want, rows, weights)


def local(queries, encodings, key_weight, value_weight, nbr_shard, nbr_row):
    shards = lax.axis_size("db")
    parts = lax.axis_size("mp")
    group = max(1, LANES // parts)
    lanes = group * parts
    planes = shards // group
    columns = queries.shape[1]
    held, tokens, width = encodings.shape
    piece = tokens // (lanes * CHUNKS)
    shard_rows = held * parts
    plane_rows = group * shard_rows
    span_count, neighbours = nbr_shard.shape
    sequences = queries.shape[0] // SEQ
    wanted = sequences * neighbours
    capacity = max(2, 4 * span_count // shards)
    most = min(plane_rows, group * wanted, group * group * capacity)
    fast = min(most, FAST_SLOTS)
    plane_groups = [[a * lanes + b for b in range(lanes)] for a in range(planes)]
    lane_groups = [[a * lanes + b for a in range(planes)] for b in range(lanes)]
    db_index = lax.axis_index("db")
    plane_index = db_index // group

    def swap(x, groups):
        return lax.all_to_all(x, BOTH, 0, 0, axis_index_groups=groups, tiled=True)

    def across(blocks):
        if planes > MOST_SHIFTS:
            stacked = jnp.stack(blocks)
            ordered = jnp.take(stacked, (jnp.arange(planes) - plane_index) % planes, axis=0, mode="clip")
            ordered = swap(ordered.reshape((-1,) + stacked.shape[2:]), lane_groups).reshape(stacked.shape)
            moved = jnp.take(ordered, (plane_index - jnp.arange(planes)) % planes, axis=0, mode="clip")
            return [moved.reshape((-1,) + stacked.shape[2:])]
        moved = [blocks[0]]
        for k in range(1, planes):
            pairs = [
                (a * lanes + b, (a + k) % planes * lanes + b) for a in range(planes) for b in range(lanes)
            ]
            moved.append(lax.ppermute(blocks[k], BOTH, pairs))
        return moved

    table = jnp.concatenate([nbr_shard.reshape(-1), nbr_row.reshape(-1)])
    table = jnp.broadcast_to(table[None, None], (shards, 1, table.shape[0]))
    table = lax.all_to_all(table, "db", 0, 0, tiled=True).reshape(
        shards, 2, sequences, SEQ // SPAN, neighbours
    )
    table_shard, table_row = table[:, 0], table[:, 1]

    weights = lax.all_gather(
        jnp.concatenate([key_weight, value_weight], axis=1), "db", axis=0, tiled=True
    )

    pieces = jnp.transpose(encodings.reshape(held, lanes, CHUNKS, piece, width), (2, 1, 0, 3, 4))
    plane_pieces = []

    def spread(chunk, after):
        sending, _ = lax.optimization_barrier((pieces[chunk].reshape(lanes * held, piece, width), after))
        plane_pieces.append(swap(sending, plane_groups))

    spread(0, table)

    odd_shard = table_shard[:, :, 1].reshape(shards, wanted)
    odd_row = table_row[:, :, 1].reshape(shards, wanted)
    earlier = jnp.arange(wanted)
    same = (odd_shard[:, :, None] == odd_shard[:, None, :]) & (earlier[None, None, :] < earlier[None, :, None])
    odd_rank = jnp.sum(same.astype(jnp.int32), axis=2)
    arriving = (odd_shard == db_index)[:, None, :] & (
        odd_rank[:, None, :] == jnp.arange(capacity, dtype=jnp.int32)[None, :, None]
    )
    slot_row = jnp.sum(jnp.where(arriving, odd_row[:, None, :] + 1, 0), axis=2) - 1
    my_slot = lax.dynamic_index_in_dim(odd_shard * capacity + odd_rank, db_index, 0, keepdims=False)
    slots = jnp.arange(shards * capacity, dtype=jnp.int32)
    chosen = my_slot[None, :] == slots[:, None]
    sender = jnp.sum(jnp.where(chosen, (earlier // neighbours).astype(jnp.int32)[None, :], 0), axis=1)
    last_rows = queries.reshape(sequences, SEQ, columns)[:, SEQ - 1]
    odd_query = jnp.take(last_rows, sender, axis=0, mode="clip").reshape(shards, capacity, columns)
    odd_query, _ = lax.optimization_barrier((odd_query, plane_pieces[0]))
    odd_query = lax.all_to_all(odd_query, "db", 0, 0, tiled=True)
    odd_query = odd_query.reshape(shards * capacity, columns)

    for chunk in range(1, CHUNKS):
        spread(chunk, odd_query if chunk == 1 else plane_pieces[-1])

    even_id = (table_shard[:, :, 0] * shard_rows + table_row[:, :, 0]).reshape(planes, group * wanted)
    ids = jnp.arange(planes * plane_rows, dtype=jnp.int32)
    want = jnp.any(even_id[:, :, None] == ids[None, None, :], axis=1).reshape(planes, planes, plane_rows)
    below = jnp.arange(plane_rows)
    before = (below[:, None] < below[None, :]).astype(BF16)
    rank = jnp.dot(want.astype(BF16), before, preferred_element_type=F32).astype(jnp.int32)
    fits = jnp.max(jnp.sum(want.astype(jnp.int32), axis=2)) <= fast
    mine_want = lax.dynamic_index_in_dim(want, plane_index, 1, keepdims=False)
    mine_rank = lax.dynamic_index_in_dim(rank, plane_index, 1, keepdims=False)
    picks = mine_want[:, None, :] & (
        mine_rank[:, None, :] == jnp.arange(fast, dtype=jnp.int32)[None, :, None]
    )
    send_rows = jnp.sum(jnp.where(picks, below[None, None, :].astype(jnp.int32), 0), axis=2)
    steps = jnp.arange(planes, dtype=jnp.int32)
    upward = (plane_index + steps) % planes
    send_rows = jnp.sum(
        jnp.where(upward[:, None, None] == steps[None, :, None], send_rows[None], 0), axis=1
    )
    my_ids = lax.dynamic_index_in_dim(even_id, plane_index, 0, keepdims=False)
    my_rank = lax.dynamic_index_in_dim(rank, plane_index, 0, keepdims=False).reshape(-1)
    place = jnp.sum(jnp.where(my_ids[:, None] == ids[None, :], my_rank[None, :], 0), axis=1)
    my_step = (plane_index + planes - my_ids // plane_rows) % planes

    def exact(source):
        return [jnp.take(source, send_rows[k], axis=0, mode="clip") for k in range(planes)]

    def whole(source):
        return [source] * planes

    def exchange(sources, select, index):
        received, arrived = [], []
        for source in sources:
            sending = select(source)
            if received:
                sending, _ = lax.optimization_barrier((sending, received[-1]))
            received.append(across(sending))
            outgoing = gather_rows(index, received[-1], group, parts)
            if arrived:
                outgoing, _ = lax.optimization_barrier((outgoing, arrived[-1]))
            arrived.append(swap(outgoing, plane_groups))
        return [a.reshape(lanes, wanted, piece, width) for a in arrived]

    part_index = lax.axis_index("mp")
    sharing, _ = lax.optimization_barrier((encodings, plane_pieces[0]))
    shared = [encodings]
    for k in range(1, parts):
        shared.append(lax.ppermute(sharing, "mp", [(m, (m + k) % parts) for m in range(parts)]))
    shard_enc = jnp.concatenate(shared, axis=0)
    slot_step = (part_index + parts - slot_row // held) % parts
    slot_row = jnp.where(slot_row >= 0, slot_step * held + slot_row % held, -1)
    slot_lanes = jnp.broadcast_to(slot_row.reshape(-1, 1), (shards * capacity, DH))
    odd_part = odd_attention(odd_query, slot_lanes, shard_enc, weights)

    def attend(select, index):
        *early, late = exchange(plane_pieces, select, index)
        early = [project(e, weights) for e in early]
        return even_attention(queries, late, weights, early), late

    result, last = attend(exact, my_step * fast + jnp.minimum(place, fast - 1))
    odd_part, _ = lax.optimization_barrier((odd_part, last))
    odd_part = lax.all_to_all(odd_part.reshape(shards, capacity, columns + DH), "db", 0, 0, tiled=True)
    odd_part = odd_part.reshape(shards * capacity, columns + DH)
    if fast < most:
        result, odd_part = lax.optimization_barrier((result, odd_part))
        result = lax.cond(
            fits,
            lambda done: done,
            lambda done: attend(whole, my_step * plane_rows + my_ids % plane_rows)[0],
            result,
        )
    return patch(my_slot, result, odd_part)


def solution(mesh):
    placed = (
        P("db", "mp"),
        P(("db", "mp"), None, None),
        P("db", "mp"),
        P("db", "mp"),
        P("db", None),
        P("db", None),
    )

    return jax.shard_map(local, mesh=mesh, in_specs=placed, out_specs=P("db", "mp"), check_vma=False)
```

```python
import functools
import math

import jax
import jax.numpy as jnp
from jax import lax
from jax.experimental import pallas as pl
from jax.experimental.pallas import tpu as pltpu
from jax.sharding import PartitionSpec as P


DH = 128
SPAN = 64
SEQ = 128
LANES = 8
CHUNKS = 2
MOST_SHIFTS = 8
TAIL = 16
FAST_SLOTS = 48
BF16 = jnp.bfloat16
F32 = jnp.float32
SCALE = 1.0 / math.sqrt(DH)
BOTH = ("db", "mp")
CONTRACT_LAST = (((1,), (1,)), ((), ()))


def project_body(rows_ref, weight_ref, out_ref):
    lanes, count, piece, width = rows_ref.shape
    rows = rows_ref[...]
    stacked = jnp.concatenate([rows[:, j].reshape(lanes * piece, width) for j in range(count)], axis=0)
    out_ref[...] = jnp.dot(stacked, weight_ref[...], preferred_element_type=F32).astype(BF16)


def project(rows, weights):
    lanes, count, piece, width = rows.shape
    per_step = math.gcd(count, 8)
    tokens = lanes * piece
    return pl.pallas_call(
        project_body,
        out_shape=jax.ShapeDtypeStruct((count * tokens, weights.shape[1]), BF16),
        grid=(count // per_step,),
        in_specs=[
            pl.BlockSpec((lanes, per_step, piece, width), lambda i: (0, i, 0, 0)),
            pl.BlockSpec(weights.shape, lambda i: (0, 0)),
        ],
        out_specs=pl.BlockSpec((per_step * tokens, weights.shape[1]), lambda i: (i, 0)),
        name="project",
    )(rows, weights)


def even_body(query_ref, rows_ref, weight_ref, *refs, per_step, neighbours):
    early_refs, out_ref = refs[:-1], refs[-1]
    columns = query_ref.shape[1]
    heads = columns // DH
    lanes, _, piece, width = rows_ref.shape
    tokens = lanes * piece
    first = SPAN - 1
    low = first // 16 * 16
    rows = rows_ref[...]
    stacked = jnp.concatenate(
        [rows[:, j].reshape(tokens, width) for j in range(per_step * neighbours)], axis=0
    )
    late = jnp.dot(stacked, weight_ref[...], preferred_element_type=F32).astype(BF16)
    position = low + lax.broadcasted_iota(jnp.int32, (SEQ - low, DH), 0)
    span = neighbours * tokens
    for s in range(per_step):
        out_ref[s * SEQ : s * SEQ + low, :] = jnp.zeros((low, columns), BF16)
        for h in range(heads):
            lo, hi = h * DH, (h + 1) * DH
            parts = [(r, s * span, span) for r in (*early_refs, late)]
            keys = jnp.concatenate([r[b : b + n, lo:hi] for r, b, n in parts], axis=0)
            values = jnp.concatenate([r[b : b + n, columns + lo : columns + hi] for r, b, n in parts], axis=0)
            query = query_ref[s * SEQ + low : (s + 1) * SEQ, lo:hi]
            scores = lax.dot_general(query, keys, CONTRACT_LAST, preferred_element_type=F32) * SCALE
            largest = jnp.max(scores, axis=1, keepdims=True)
            expscore = jnp.exp(scores - largest)
            total = jnp.sum(expscore, axis=1, keepdims=True)
            mixed = jnp.dot(expscore.astype(BF16), values, preferred_element_type=F32)
            attended = mixed / total
            attended = jnp.where(position < first, 0.0, attended)
            out_ref[s * SEQ + low : (s + 1) * SEQ, lo:hi] = attended.astype(BF16)


def even_attention(queries, rows, weights, early):
    tokens, columns = queries.shape
    sequences = tokens // SEQ
    lanes, count, piece, width = rows.shape
    neighbours = count // sequences
    per_step = math.gcd(sequences, 2)
    early_rows = lanes * piece * per_step * neighbours
    early_spec = pl.BlockSpec((early_rows, weights.shape[1]), lambda i: (i, 0))
    return pl.pallas_call(
        functools.partial(even_body, per_step=per_step, neighbours=neighbours),
        out_shape=jax.ShapeDtypeStruct(queries.shape, BF16),
        grid=(sequences // per_step,),
        in_specs=[
            pl.BlockSpec((per_step * SEQ, columns), lambda i: (i, 0)),
            pl.BlockSpec((lanes, per_step * neighbours, piece, width), lambda i: (0, i, 0, 0)),
            pl.BlockSpec(weights.shape, lambda i: (0, 0)),
            *[early_spec for _ in early],
        ],
        out_specs=pl.BlockSpec((per_step * SEQ, columns), lambda i: (i, 0)),
        name="even_attention",
    )(queries, rows, weights, *early)


def patch_body(slot_ref, out_in_ref, odd_ref, out_ref, *rest, neighbours):
    picked_refs, row_ref = rest[:-1], rest[-1]
    per_step, _, tail, columns = out_ref.shape
    heads = columns // DH
    sequences = row_ref.shape[0]
    step = pl.program_id(0)

    @pl.when(step == 0)
    def _():
        for i in range(sequences):
            for j, picked_ref in enumerate(picked_refs):
                picked_ref[i : i + 1, :] = odd_ref[pl.ds(slot_ref[i * neighbours + j], 1), :]
        for h in range(heads):
            lo, hi = h * DH, (h + 1) * DH
            maxima = [p[:, columns + h : columns + h + 1] for p in picked_refs]
            sums = [p[:, columns + DH // 2 + h : columns + DH // 2 + h + 1] for p in picked_refs]
            top = functools.reduce(jnp.maximum, maxima)
            each = [jnp.exp(m - top) for m in maxima]
            under = sum(e * t for e, t in zip(each, sums))
            over = sum(e * p[:, lo:hi] for e, p in zip(each, picked_refs))
            row_ref[:, lo:hi] = over / under

    last = lax.broadcasted_iota(jnp.int32, (tail, columns), 0) == tail - 1
    for i in range(per_step):
        row = row_ref[pl.ds(step * per_step + i, 1), :]
        out_ref[i, 0] = jnp.where(last, row, out_in_ref[i, 0].astype(F32)).astype(BF16)


def patch(slots, out, odd):
    tokens, columns = out.shape
    sequences = tokens // SEQ
    neighbours = slots.shape[0] // sequences
    per_step = math.gcd(sequences, 4)
    blocks = SEQ // TAIL
    tail = pl.BlockSpec((per_step, 1, TAIL, columns), lambda i, s: (i, blocks - 1, 0, 0))
    shape = (sequences, blocks, TAIL, columns)
    return pl.pallas_call(
        functools.partial(patch_body, neighbours=neighbours),
        out_shape=jax.ShapeDtypeStruct(shape, BF16),
        grid_spec=pltpu.PrefetchScalarGridSpec(
            num_scalar_prefetch=1,
            grid=(sequences // per_step,),
            in_specs=[tail, pl.BlockSpec(odd.shape, lambda i, s: (0, 0))],
            out_specs=tail,
            scratch_shapes=[pltpu.VMEM((sequences, odd.shape[1]), F32)] * neighbours
            + [pltpu.VMEM((sequences, columns), F32)],
        ),
        input_output_aliases={1: 0},
        name="patch",
    )(slots, out.reshape(shape), odd).reshape(out.shape)


def gather_body(index_ref, *refs, copies):
    sources, out_ref = refs[:-1], refs[-1]
    size = sources[0].shape[0]
    wanted = out_ref.shape[0]
    base = pl.program_id(0) // copies * wanted

    def step(i, carry):
        at = index_ref[base + i]
        for k, source in enumerate(sources):
            @pl.when((at >= k * size) & (at < (k + 1) * size))
            def _():
                out_ref[i] = source[at - k * size]

        return carry

    lax.fori_loop(0, wanted, step, 0, unroll=4)


def gather_rows(index, sources, groups, copies):
    wanted = index.shape[0] // groups
    shape = sources[0].shape
    whole = pl.BlockSpec(shape, lambda i, s: (0, 0, 0))
    return pl.pallas_call(
        functools.partial(gather_body, copies=copies),
        out_shape=jax.ShapeDtypeStruct((index.shape[0] * copies,) + shape[1:], sources[0].dtype),
        grid_spec=pltpu.PrefetchScalarGridSpec(
            num_scalar_prefetch=1,
            grid=(groups * copies,),
            in_specs=[whole for _ in sources],
            out_specs=pl.BlockSpec((wanted,) + shape[1:], lambda i, s: (i, 0, 0)),
        ),
        name="gather_rows",
    )(index, *sources)


def select_body(index_ref, source_ref, *out_refs):
    fast = out_refs[0].shape[0]

    def step(i, carry):
        for k, out_ref in enumerate(out_refs):
            out_ref[i] = source_ref[index_ref[k * fast + i]]
        return carry

    lax.fori_loop(0, fast, step, 0, unroll=2)


def select_rows(index, source):
    count, fast = index.shape
    block = pl.BlockSpec((fast,) + source.shape[1:], lambda i, s: (0, 0, 0))
    return pl.pallas_call(
        select_body,
        out_shape=[jax.ShapeDtypeStruct((fast,) + source.shape[1:], source.dtype)] * count,
        grid_spec=pltpu.PrefetchScalarGridSpec(
            num_scalar_prefetch=1,
            grid=(1,),
            in_specs=[pl.BlockSpec(source.shape, lambda i, s: (0, 0, 0))],
            out_specs=[block] * count,
        ),
        name="select_rows",
    )(index.reshape(-1), source)


def odd_body(query_ref, want_ref, rows_ref, weight_ref, out_ref):
    columns = query_ref.shape[1]
    heads = columns // DH
    per_step, tokens, width = rows_ref.shape
    base = pl.program_id(0) * per_step
    projected = jnp.dot(
        rows_ref[...].reshape(per_step * tokens, width), weight_ref[...], preferred_element_type=F32
    ).astype(BF16)
    want = want_ref[...] - base
    here = [want == r for r in range(per_step)]
    inside = (want >= 0) & (want < per_step)
    lane = lax.broadcasted_iota(jnp.int32, (want.shape[0], DH), 1)
    stats = out_ref[:, columns:]
    for h in range(heads):
        lo, hi = h * DH, (h + 1) * DH
        scores = (
            lax.dot_general(
                query_ref[:, lo:hi], projected[:, lo:hi], CONTRACT_LAST, preferred_element_type=F32
            )
            * SCALE
        )
        mine = jnp.zeros((want.shape[0], tokens), F32)
        for r in range(per_step):
            mine = jnp.where(here[r], scores[:, r * tokens : (r + 1) * tokens], mine)
        largest = jnp.max(mine, axis=1, keepdims=True)
        expscore = jnp.exp(mine - largest)
        total = jnp.sum(expscore, axis=1, keepdims=True)
        spread = jnp.concatenate([jnp.where(here[r], expscore, 0.0) for r in range(per_step)], axis=1)
        mixed = jnp.dot(spread.astype(BF16), projected[:, columns + lo : columns + hi], preferred_element_type=F32)
        out_ref[:, lo:hi] = jnp.where(inside, mixed, out_ref[:, lo:hi])
        stats = jnp.where(inside & (lane == h), largest, stats)
        stats = jnp.where(inside & (lane == DH // 2 + h), total, stats)
    out_ref[:, columns:] = stats


def odd_attention(queries, want, rows, weights):
    slots, columns = queries.shape
    count, tokens, width = rows.shape
    per_step = math.gcd(count, 4)
    return pl.pallas_call(
        odd_body,
        out_shape=jax.ShapeDtypeStruct((slots, columns + DH), F32),
        grid=(count // per_step,),
        in_specs=[
            pl.BlockSpec((slots, columns), lambda i: (0, 0)),
            pl.BlockSpec((slots, DH), lambda i: (0, 0)),
            pl.BlockSpec((per_step, tokens, width), lambda i: (i, 0, 0)),
            pl.BlockSpec(weights.shape, lambda i: (0, 0)),
        ],
        out_specs=pl.BlockSpec((slots, columns + DH), lambda i: (0, 0)),
        name="odd_attention",
    )(queries, want, rows, weights)


def local(queries, encodings, key_weight, value_weight, nbr_shard, nbr_row):
    shards = lax.axis_size("db")
    parts = lax.axis_size("mp")
    group = max(1, LANES // parts)
    lanes = group * parts
    planes = shards // group
    columns = queries.shape[1]
    held, tokens, width = encodings.shape
    piece = tokens // (lanes * CHUNKS)
    shard_rows = held * parts
    plane_rows = group * shard_rows
    span_count, neighbours = nbr_shard.shape
    sequences = queries.shape[0] // SEQ
    wanted = sequences * neighbours
    capacity = max(2, 4 * span_count // shards)
    most = min(plane_rows, group * wanted, group * group * capacity)
    fast = min(most, FAST_SLOTS)
    plane_groups = [[a * lanes + b for b in range(lanes)] for a in range(planes)]
    lane_groups = [[a * lanes + b for a in range(planes)] for b in range(lanes)]
    db_index = lax.axis_index("db")
    plane_index = db_index // group

    def swap(x, groups):
        return lax.all_to_all(x, BOTH, 0, 0, axis_index_groups=groups, tiled=True)

    def across(blocks):
        if planes > MOST_SHIFTS:
            stacked = jnp.stack(blocks)
            ordered = jnp.take(stacked, (jnp.arange(planes) - plane_index) % planes, axis=0, mode="clip")
            ordered = swap(ordered.reshape((-1,) + stacked.shape[2:]), lane_groups).reshape(stacked.shape)
            moved = jnp.take(ordered, (plane_index - jnp.arange(planes)) % planes, axis=0, mode="clip")
            return [moved.reshape((-1,) + stacked.shape[2:])]
        moved = [blocks[0]]
        for k in range(1, planes):
            pairs = [
                (a * lanes + b, (a + k) % planes * lanes + b) for a in range(planes) for b in range(lanes)
            ]
            moved.append(lax.ppermute(blocks[k], BOTH, pairs))
        return moved

    table = jnp.concatenate([nbr_shard.reshape(-1), nbr_row.reshape(-1)])
    table = jnp.broadcast_to(table[None, None], (shards, 1, table.shape[0]))
    table = lax.all_to_all(table, "db", 0, 0, tiled=True).reshape(
        shards, 2, sequences, SEQ // SPAN, neighbours
    )
    table_shard, table_row = table[:, 0], table[:, 1]

    weights = lax.all_gather(
        jnp.concatenate([key_weight, value_weight], axis=1), "db", axis=0, tiled=True
    )

    pieces = jnp.transpose(encodings.reshape(held, lanes, CHUNKS, piece, width), (2, 1, 0, 3, 4))
    plane_pieces = []

    def spread(chunk, after):
        sending, _ = lax.optimization_barrier((pieces[chunk].reshape(lanes * held, piece, width), after))
        plane_pieces.append(swap(sending, plane_groups))

    spread(0, table)

    odd_shard = table_shard[:, :, 1].reshape(shards, wanted)
    odd_row = table_row[:, :, 1].reshape(shards, wanted)
    earlier = jnp.arange(wanted)
    same = (odd_shard[:, :, None] == odd_shard[:, None, :]) & (earlier[None, None, :] < earlier[None, :, None])
    odd_rank = jnp.sum(same.astype(jnp.int32), axis=2)
    arriving = (odd_shard == db_index)[:, None, :] & (
        odd_rank[:, None, :] == jnp.arange(capacity, dtype=jnp.int32)[None, :, None]
    )
    slot_row = jnp.sum(jnp.where(arriving, odd_row[:, None, :] + 1, 0), axis=2) - 1
    my_slot = lax.dynamic_index_in_dim(odd_shard * capacity + odd_rank, db_index, 0, keepdims=False)
    slots = jnp.arange(shards * capacity, dtype=jnp.int32)
    chosen = my_slot[None, :] == slots[:, None]
    sender = jnp.sum(jnp.where(chosen, (earlier // neighbours).astype(jnp.int32)[None, :], 0), axis=1)
    last_rows = queries.reshape(sequences, SEQ, columns)[:, SEQ - 1]
    odd_query = jnp.take(last_rows, sender, axis=0, mode="clip").reshape(shards, capacity, columns)
    odd_query, _ = lax.optimization_barrier((odd_query, plane_pieces[0]))
    odd_query = lax.all_to_all(odd_query, "db", 0, 0, tiled=True)
    odd_query = odd_query.reshape(shards * capacity, columns)

    for chunk in range(1, CHUNKS):
        spread(chunk, odd_query if chunk == 1 else plane_pieces[-1])

    even_id = (table_shard[:, :, 0] * shard_rows + table_row[:, :, 0]).reshape(planes, group * wanted)
    ids = jnp.arange(planes * plane_rows, dtype=jnp.int32)
    want = jnp.any(even_id[:, :, None] == ids[None, None, :], axis=1).reshape(planes, planes, plane_rows)
    below = jnp.arange(plane_rows)
    before = (below[:, None] < below[None, :]).astype(BF16)
    rank = jnp.dot(want.astype(BF16), before, preferred_element_type=F32).astype(jnp.int32)
    fits = jnp.max(jnp.sum(want.astype(jnp.int32), axis=2)) <= fast
    mine_want = lax.dynamic_index_in_dim(want, plane_index, 1, keepdims=False)
    mine_rank = lax.dynamic_index_in_dim(rank, plane_index, 1, keepdims=False)
    picks = mine_want[:, None, :] & (
        mine_rank[:, None, :] == jnp.arange(fast, dtype=jnp.int32)[None, :, None]
    )
    send_rows = jnp.sum(jnp.where(picks, below[None, None, :].astype(jnp.int32), 0), axis=2)
    steps = jnp.arange(planes, dtype=jnp.int32)
    upward = (plane_index + steps) % planes
    send_rows = jnp.sum(
        jnp.where(upward[:, None, None] == steps[None, :, None], send_rows[None], 0), axis=1
    )
    my_ids = lax.dynamic_index_in_dim(even_id, plane_index, 0, keepdims=False)
    my_rank = lax.dynamic_index_in_dim(rank, plane_index, 0, keepdims=False).reshape(-1)
    place = jnp.sum(jnp.where(my_ids[:, None] == ids[None, :], my_rank[None, :], 0), axis=1)
    my_step = (plane_index + planes - my_ids // plane_rows) % planes

    def exact(source):
        if planes > MOST_SHIFTS:
            return [jnp.take(source, send_rows[k], axis=0, mode="clip") for k in range(planes)]
        return select_rows(send_rows, source)

    def whole(source):
        return [source] * planes

    def exchange(sources, select, index):
        received, arrived = [], []
        for source in sources:
            sending = select(source)
            if received:
                sending, _ = lax.optimization_barrier((sending, received[-1]))
            received.append(across(sending))
            outgoing = gather_rows(index, received[-1], group, parts)
            if arrived:
                outgoing, _ = lax.optimization_barrier((outgoing, arrived[-1]))
            arrived.append(swap(outgoing, plane_groups))
        return [a.reshape(lanes, wanted, piece, width) for a in arrived]

    part_index = lax.axis_index("mp")
    sharing, _ = lax.optimization_barrier((encodings, plane_pieces[0]))
    shared = [encodings]
    for k in range(1, parts):
        shared.append(lax.ppermute(sharing, "mp", [(m, (m + k) % parts) for m in range(parts)]))
    shard_enc = jnp.concatenate(shared, axis=0)
    slot_step = (part_index + parts - slot_row // held) % parts
    slot_row = jnp.where(slot_row >= 0, slot_step * held + slot_row % held, -1)
    slot_lanes = jnp.broadcast_to(slot_row.reshape(-1, 1), (shards * capacity, DH))
    odd_part = odd_attention(odd_query, slot_lanes, shard_enc, weights)

    def attend(select, index):
        *early, late = exchange(plane_pieces, select, index)
        early = [project(e, weights) for e in early]
        return even_attention(queries, late, weights, early), late

    result, last = attend(exact, my_step * fast + jnp.minimum(place, fast - 1))
    odd_part, _ = lax.optimization_barrier((odd_part, last))
    odd_part = lax.all_to_all(odd_part.reshape(shards, capacity, columns + DH), "db", 0, 0, tiled=True)
    odd_part = odd_part.reshape(shards * capacity, columns + DH)
    if fast < most:
        result, odd_part = lax.optimization_barrier((result, odd_part))
        result = lax.cond(
            fits,
            lambda done: done,
            lambda done: attend(whole, my_step * plane_rows + my_ids % plane_rows)[0],
            result,
        )
    return patch(my_slot, result, odd_part)


def solution(mesh):
    placed = (
        P("db", "mp"),
        P(("db", "mp"), None, None),
        P("db", "mp"),
        P("db", "mp"),
        P("db", None),
        P("db", None),
    )

    return jax.shard_map(local, mesh=mesh, in_specs=placed, out_specs=P("db", "mp"), check_vma=False)
```

```python
import functools
import math

import jax
import jax.numpy as jnp
from jax import lax
from jax.experimental import pallas as pl
from jax.experimental.pallas import tpu as pltpu
from jax.sharding import PartitionSpec as P


DH = 128
SPAN = 64
SEQ = 128
LANES = 8
CHUNKS = 2
MOST_SHIFTS = 8
TAIL = 16
FAST_SLOTS = 48
BF16 = jnp.bfloat16
F32 = jnp.float32
SCALE = 1.0 / math.sqrt(DH)
BOTH = ("db", "mp")
CONTRACT_LAST = (((1,), (1,)), ((), ()))


def project_body(rows_ref, weight_ref, out_ref):
    lanes, count, piece, width = rows_ref.shape
    rows = rows_ref[...]
    stacked = jnp.concatenate([rows[:, j].reshape(lanes * piece, width) for j in range(count)], axis=0)
    out_ref[...] = jnp.dot(stacked, weight_ref[...], preferred_element_type=F32).astype(BF16)


def project(rows, weights):
    lanes, count, piece, width = rows.shape
    per_step = math.gcd(count, 8)
    tokens = lanes * piece
    return pl.pallas_call(
        project_body,
        out_shape=jax.ShapeDtypeStruct((count * tokens, weights.shape[1]), BF16),
        grid=(count // per_step,),
        in_specs=[
            pl.BlockSpec((lanes, per_step, piece, width), lambda i: (0, i, 0, 0)),
            pl.BlockSpec(weights.shape, lambda i: (0, 0)),
        ],
        out_specs=pl.BlockSpec((per_step * tokens, weights.shape[1]), lambda i: (i, 0)),
        name="project",
    )(rows, weights)


def even_body(query_ref, rows_ref, weight_ref, *refs, per_step, neighbours):
    early_refs, out_ref = refs[:-1], refs[-1]
    columns = query_ref.shape[1]
    heads = columns // DH
    lanes, _, piece, width = rows_ref.shape
    tokens = lanes * piece
    first = SPAN - 1
    low = first // 16 * 16
    rows = rows_ref[...]
    stacked = jnp.concatenate(
        [rows[:, j].reshape(tokens, width) for j in range(per_step * neighbours)], axis=0
    )
    late = jnp.dot(stacked, weight_ref[...], preferred_element_type=F32).astype(BF16)
    position = low + lax.broadcasted_iota(jnp.int32, (SEQ - low, DH), 0)
    span = neighbours * tokens
    for s in range(per_step):
        out_ref[s * SEQ : s * SEQ + low, :] = jnp.zeros((low, columns), BF16)
        for h in range(heads):
            lo, hi = h * DH, (h + 1) * DH
            parts = [(r, s * span, span) for r in (*early_refs, late)]
            keys = jnp.concatenate([r[b : b + n, lo:hi] for r, b, n in parts], axis=0)
            values = jnp.concatenate([r[b : b + n, columns + lo : columns + hi] for r, b, n in parts], axis=0)
            query = query_ref[s * SEQ + low : (s + 1) * SEQ, lo:hi]
            scores = lax.dot_general(query, keys, CONTRACT_LAST, preferred_element_type=F32) * SCALE
            largest = jnp.max(scores, axis=1, keepdims=True)
            expscore = jnp.exp(scores - largest)
            total = jnp.sum(expscore, axis=1, keepdims=True)
            mixed = jnp.dot(expscore.astype(BF16), values, preferred_element_type=F32)
            attended = mixed / total
            attended = jnp.where(position < first, 0.0, attended)
            out_ref[s * SEQ + low : (s + 1) * SEQ, lo:hi] = attended.astype(BF16)


def even_attention(queries, rows, weights, early):
    tokens, columns = queries.shape
    sequences = tokens // SEQ
    lanes, count, piece, width = rows.shape
    neighbours = count // sequences
    per_step = math.gcd(sequences, 2)
    early_rows = lanes * piece * per_step * neighbours
    early_spec = pl.BlockSpec((early_rows, weights.shape[1]), lambda i: (i, 0))
    return pl.pallas_call(
        functools.partial(even_body, per_step=per_step, neighbours=neighbours),
        out_shape=jax.ShapeDtypeStruct(queries.shape, BF16),
        grid=(sequences // per_step,),
        in_specs=[
            pl.BlockSpec((per_step * SEQ, columns), lambda i: (i, 0)),
            pl.BlockSpec((lanes, per_step * neighbours, piece, width), lambda i: (0, i, 0, 0)),
            pl.BlockSpec(weights.shape, lambda i: (0, 0)),
            *[early_spec for _ in early],
        ],
        out_specs=pl.BlockSpec((per_step * SEQ, columns), lambda i: (i, 0)),
        name="even_attention",
    )(queries, rows, weights, *early)


def patch_body(slot_ref, out_in_ref, odd_ref, out_ref, *rest, neighbours):
    picked_refs, row_ref = rest[:-1], rest[-1]
    per_step, _, tail, columns = out_ref.shape
    heads = columns // DH
    sequences = row_ref.shape[0]
    step = pl.program_id(0)

    @pl.when(step == 0)
    def _():
        for i in range(sequences):
            for j, picked_ref in enumerate(picked_refs):
                picked_ref[i : i + 1, :] = odd_ref[pl.ds(slot_ref[i * neighbours + j], 1), :]
        for h in range(heads):
            lo, hi = h * DH, (h + 1) * DH
            maxima = [p[:, columns + h : columns + h + 1] for p in picked_refs]
            sums = [p[:, columns + DH // 2 + h : columns + DH // 2 + h + 1] for p in picked_refs]
            top = functools.reduce(jnp.maximum, maxima)
            each = [jnp.exp(m - top) for m in maxima]
            under = sum(e * t for e, t in zip(each, sums))
            over = sum(e * p[:, lo:hi] for e, p in zip(each, picked_refs))
            row_ref[:, lo:hi] = over / under

    last = lax.broadcasted_iota(jnp.int32, (tail, columns), 0) == tail - 1
    for i in range(per_step):
        row = row_ref[pl.ds(step * per_step + i, 1), :]
        out_ref[i, 0] = jnp.where(last, row, out_in_ref[i, 0].astype(F32)).astype(BF16)


def patch(slots, out, odd):
    tokens, columns = out.shape
    sequences = tokens // SEQ
    neighbours = slots.shape[0] // sequences
    per_step = math.gcd(sequences, 4)
    blocks = SEQ // TAIL
    tail = pl.BlockSpec((per_step, 1, TAIL, columns), lambda i, s: (i, blocks - 1, 0, 0))
    shape = (sequences, blocks, TAIL, columns)
    return pl.pallas_call(
        functools.partial(patch_body, neighbours=neighbours),
        out_shape=jax.ShapeDtypeStruct(shape, BF16),
        grid_spec=pltpu.PrefetchScalarGridSpec(
            num_scalar_prefetch=1,
            grid=(sequences // per_step,),
            in_specs=[tail, pl.BlockSpec(odd.shape, lambda i, s: (0, 0))],
            out_specs=tail,
            scratch_shapes=[pltpu.VMEM((sequences, odd.shape[1]), F32)] * neighbours
            + [pltpu.VMEM((sequences, columns), F32)],
        ),
        input_output_aliases={1: 0},
        name="patch",
    )(slots, out.reshape(shape), odd).reshape(out.shape)


def gather_body(index_ref, *refs, count):
    sources, out_ref, stage_ref, sem_ref = refs[:count], refs[count], refs[count + 1], refs[count + 2]
    size = sources[0].shape[0]
    copies, wanted = out_ref.shape[1:3]
    base = pl.program_id(0) * wanted

    @pl.when(pl.program_id(0) == 0)
    def _():
        moves = [
            pltpu.make_async_copy(source, stage_ref.at[pl.ds(k * size, size)], sem_ref.at[k])
            for k, source in enumerate(sources)
        ]
        for move in moves:
            move.start()
        for move in moves:
            move.wait()

    def step(i, carry):
        row = stage_ref[index_ref[base + i]]
        for c in range(copies):
            out_ref[0, c, i] = row
        return carry

    lax.fori_loop(0, wanted, step, 0, unroll=8)


def gather_rows(index, sources, groups, copies):
    wanted = index.shape[0] // groups
    size, piece, width = sources[0].shape
    out = pl.pallas_call(
        functools.partial(gather_body, count=len(sources)),
        out_shape=jax.ShapeDtypeStruct((groups, copies, wanted, piece, width), sources[0].dtype),
        grid_spec=pltpu.PrefetchScalarGridSpec(
            num_scalar_prefetch=1,
            grid=(groups,),
            in_specs=[pl.BlockSpec(memory_space=pl.ANY) for _ in sources],
            out_specs=pl.BlockSpec((1, copies, wanted, piece, width), lambda i, s: (i, 0, 0, 0, 0)),
            scratch_shapes=[
                pltpu.VMEM((len(sources) * size, piece, width), sources[0].dtype),
                pltpu.SemaphoreType.DMA((len(sources),)),
            ],
        ),
        name="gather_rows",
    )(index, *sources)
    return out.reshape(groups * copies * wanted, piece, width)


def select_body(index_ref, source_ref, *out_refs):
    fast = out_refs[0].shape[0]

    def step(i, carry):
        for k, out_ref in enumerate(out_refs):
            out_ref[i] = source_ref[index_ref[k * fast + i]]
        return carry

    lax.fori_loop(0, fast, step, 0, unroll=2)


def select_rows(index, source):
    count, fast = index.shape
    block = pl.BlockSpec((fast,) + source.shape[1:], lambda i, s: (0, 0, 0))
    return pl.pallas_call(
        select_body,
        out_shape=[jax.ShapeDtypeStruct((fast,) + source.shape[1:], source.dtype)] * count,
        grid_spec=pltpu.PrefetchScalarGridSpec(
            num_scalar_prefetch=1,
            grid=(1,),
            in_specs=[pl.BlockSpec(source.shape, lambda i, s: (0, 0, 0))],
            out_specs=[block] * count,
        ),
        name="select_rows",
    )(index.reshape(-1), source)


def odd_body(query_ref, want_ref, rows_ref, weight_ref, out_ref):
    columns = query_ref.shape[1]
    heads = columns // DH
    per_step, tokens, width = rows_ref.shape
    base = pl.program_id(0) * per_step
    projected = jnp.dot(
        rows_ref[...].reshape(per_step * tokens, width), weight_ref[...], preferred_element_type=F32
    ).astype(BF16)
    want = want_ref[...] - base
    here = [want == r for r in range(per_step)]
    inside = (want >= 0) & (want < per_step)
    lane = lax.broadcasted_iota(jnp.int32, (want.shape[0], DH), 1)
    stats = out_ref[:, columns:]
    for h in range(heads):
        lo, hi = h * DH, (h + 1) * DH
        scores = (
            lax.dot_general(
                query_ref[:, lo:hi], projected[:, lo:hi], CONTRACT_LAST, preferred_element_type=F32
            )
            * SCALE
        )
        mine = jnp.zeros((want.shape[0], tokens), F32)
        for r in range(per_step):
            mine = jnp.where(here[r], scores[:, r * tokens : (r + 1) * tokens], mine)
        largest = jnp.max(mine, axis=1, keepdims=True)
        expscore = jnp.exp(mine - largest)
        total = jnp.sum(expscore, axis=1, keepdims=True)
        spread = jnp.concatenate([jnp.where(here[r], expscore, 0.0) for r in range(per_step)], axis=1)
        mixed = jnp.dot(spread.astype(BF16), projected[:, columns + lo : columns + hi], preferred_element_type=F32)
        out_ref[:, lo:hi] = jnp.where(inside, mixed, out_ref[:, lo:hi])
        stats = jnp.where(inside & (lane == h), largest, stats)
        stats = jnp.where(inside & (lane == DH // 2 + h), total, stats)
    out_ref[:, columns:] = stats


def odd_attention(queries, want, rows, weights):
    slots, columns = queries.shape
    count, tokens, width = rows.shape
    per_step = math.gcd(count, 4)
    return pl.pallas_call(
        odd_body,
        out_shape=jax.ShapeDtypeStruct((slots, columns + DH), F32),
        grid=(count // per_step,),
        in_specs=[
            pl.BlockSpec((slots, columns), lambda i: (0, 0)),
            pl.BlockSpec((slots, DH), lambda i: (0, 0)),
            pl.BlockSpec((per_step, tokens, width), lambda i: (i, 0, 0)),
            pl.BlockSpec(weights.shape, lambda i: (0, 0)),
        ],
        out_specs=pl.BlockSpec((slots, columns + DH), lambda i: (0, 0)),
        name="odd_attention",
    )(queries, want, rows, weights)


def local(queries, encodings, key_weight, value_weight, nbr_shard, nbr_row):
    shards = lax.axis_size("db")
    parts = lax.axis_size("mp")
    group = max(1, LANES // parts)
    lanes = group * parts
    planes = shards // group
    columns = queries.shape[1]
    held, tokens, width = encodings.shape
    piece = tokens // (lanes * CHUNKS)
    shard_rows = held * parts
    plane_rows = group * shard_rows
    span_count, neighbours = nbr_shard.shape
    sequences = queries.shape[0] // SEQ
    wanted = sequences * neighbours
    capacity = max(2, 4 * span_count // shards)
    most = min(plane_rows, group * wanted, group * group * capacity)
    fast = min(most, FAST_SLOTS)
    plane_groups = [[a * lanes + b for b in range(lanes)] for a in range(planes)]
    lane_groups = [[a * lanes + b for a in range(planes)] for b in range(lanes)]
    db_index = lax.axis_index("db")
    plane_index = db_index // group

    def swap(x, groups):
        return lax.all_to_all(x, BOTH, 0, 0, axis_index_groups=groups, tiled=True)

    def across(blocks):
        if planes > MOST_SHIFTS:
            stacked = jnp.stack(blocks)
            ordered = jnp.take(stacked, (jnp.arange(planes) - plane_index) % planes, axis=0, mode="clip")
            ordered = swap(ordered.reshape((-1,) + stacked.shape[2:]), lane_groups).reshape(stacked.shape)
            moved = jnp.take(ordered, (plane_index - jnp.arange(planes)) % planes, axis=0, mode="clip")
            return [moved.reshape((-1,) + stacked.shape[2:])]
        moved = [blocks[0]]
        for k in range(1, planes):
            pairs = [
                (a * lanes + b, (a + k) % planes * lanes + b) for a in range(planes) for b in range(lanes)
            ]
            moved.append(lax.ppermute(blocks[k], BOTH, pairs))
        return moved

    table = jnp.concatenate([nbr_shard.reshape(-1), nbr_row.reshape(-1)])
    table = jnp.broadcast_to(table[None, None], (shards, 1, table.shape[0]))
    table = lax.all_to_all(table, "db", 0, 0, tiled=True).reshape(
        shards, 2, sequences, SEQ // SPAN, neighbours
    )
    table_shard, table_row = table[:, 0], table[:, 1]

    weights = lax.all_gather(
        jnp.concatenate([key_weight, value_weight], axis=1), "db", axis=0, tiled=True
    )

    pieces = jnp.transpose(encodings.reshape(held, lanes, CHUNKS, piece, width), (2, 1, 0, 3, 4))
    plane_pieces = []

    def spread(chunk, after):
        sending, _ = lax.optimization_barrier((pieces[chunk].reshape(lanes * held, piece, width), after))
        plane_pieces.append(swap(sending, plane_groups))

    for chunk in range(CHUNKS):
        spread(chunk, plane_pieces[-1] if chunk else table)

    odd_shard = table_shard[:, :, 1].reshape(shards, wanted)
    odd_row = table_row[:, :, 1].reshape(shards, wanted)
    earlier = jnp.arange(wanted)
    same = (odd_shard[:, :, None] == odd_shard[:, None, :]) & (earlier[None, None, :] < earlier[None, :, None])
    odd_rank = jnp.sum(same.astype(jnp.int32), axis=2)
    arriving = (odd_shard == db_index)[:, None, :] & (
        odd_rank[:, None, :] == jnp.arange(capacity, dtype=jnp.int32)[None, :, None]
    )
    slot_row = jnp.sum(jnp.where(arriving, odd_row[:, None, :] + 1, 0), axis=2) - 1
    my_slot = lax.dynamic_index_in_dim(odd_shard * capacity + odd_rank, db_index, 0, keepdims=False)
    slots = jnp.arange(shards * capacity, dtype=jnp.int32)
    chosen = my_slot[None, :] == slots[:, None]
    sender = jnp.sum(jnp.where(chosen, (earlier // neighbours).astype(jnp.int32)[None, :], 0), axis=1)
    last_rows = queries.reshape(sequences, SEQ, columns)[:, SEQ - 1]
    odd_query = jnp.take(last_rows, sender, axis=0, mode="clip").reshape(shards, capacity, columns)
    odd_query, _ = lax.optimization_barrier((odd_query, plane_pieces[-1]))
    odd_query = lax.all_to_all(odd_query, "db", 0, 0, tiled=True)
    odd_query = odd_query.reshape(shards * capacity, columns)

    even_id = (table_shard[:, :, 0] * shard_rows + table_row[:, :, 0]).reshape(planes, group * wanted)
    ids = jnp.arange(planes * plane_rows, dtype=jnp.int32)
    want = jnp.any(even_id[:, :, None] == ids[None, None, :], axis=1).reshape(planes, planes, plane_rows)
    below = jnp.arange(plane_rows)
    before = (below[:, None] < below[None, :]).astype(BF16)
    rank = jnp.dot(want.astype(BF16), before, preferred_element_type=F32).astype(jnp.int32)
    fits = jnp.max(jnp.sum(want.astype(jnp.int32), axis=2)) <= fast
    mine_want = lax.dynamic_index_in_dim(want, plane_index, 1, keepdims=False)
    mine_rank = lax.dynamic_index_in_dim(rank, plane_index, 1, keepdims=False)
    picks = mine_want[:, None, :] & (
        mine_rank[:, None, :] == jnp.arange(fast, dtype=jnp.int32)[None, :, None]
    )
    send_rows = jnp.sum(jnp.where(picks, below[None, None, :].astype(jnp.int32), 0), axis=2)
    steps = jnp.arange(planes, dtype=jnp.int32)
    upward = (plane_index + steps) % planes
    send_rows = jnp.sum(
        jnp.where(upward[:, None, None] == steps[None, :, None], send_rows[None], 0), axis=1
    )
    my_ids = lax.dynamic_index_in_dim(even_id, plane_index, 0, keepdims=False)
    my_rank = lax.dynamic_index_in_dim(rank, plane_index, 0, keepdims=False).reshape(-1)
    place = jnp.sum(jnp.where(my_ids[:, None] == ids[None, :], my_rank[None, :], 0), axis=1)
    my_step = (plane_index + planes - my_ids // plane_rows) % planes

    def exact(source):
        if planes > MOST_SHIFTS:
            return [jnp.take(source, send_rows[k], axis=0, mode="clip") for k in range(planes)]
        return select_rows(send_rows, source)

    def whole(source):
        return [source] * planes

    def exchange(sources, select, index):
        received, arrived = [], []
        for source in sources:
            sending = select(source)
            if received:
                sending, _ = lax.optimization_barrier((sending, received[-1]))
            received.append(across(sending))
            outgoing = gather_rows(index, received[-1], group, parts)
            outgoing, _ = lax.optimization_barrier((outgoing, arrived[-1] if arrived else odd_query))
            arrived.append(swap(outgoing, plane_groups))
        return [a.reshape(lanes, wanted, piece, width) for a in arrived]

    part_index = lax.axis_index("mp")
    sharing, _ = lax.optimization_barrier((encodings, plane_pieces[-1]))
    shared = [encodings]
    for k in range(1, parts):
        shared.append(lax.ppermute(sharing, "mp", [(m, (m + k) % parts) for m in range(parts)]))
    shard_enc = jnp.concatenate(shared, axis=0)
    slot_step = (part_index + parts - slot_row // held) % parts
    slot_row = jnp.where(slot_row >= 0, slot_step * held + slot_row % held, -1)
    slot_lanes = jnp.broadcast_to(slot_row.reshape(-1, 1), (shards * capacity, DH))
    odd_part = odd_attention(odd_query, slot_lanes, shard_enc, weights)

    def attend(select, index):
        *early, late = exchange(plane_pieces, select, index)
        early = [project(e, weights) for e in early]
        return even_attention(queries, late, weights, early), late

    result, last = attend(exact, my_step * fast + jnp.minimum(place, fast - 1))
    odd_part, _ = lax.optimization_barrier((odd_part, last))
    odd_part = lax.all_to_all(odd_part.reshape(shards, capacity, columns + DH), "db", 0, 0, tiled=True)
    odd_part = odd_part.reshape(shards * capacity, columns + DH)
    if fast < most:
        result, odd_part = lax.optimization_barrier((result, odd_part))
        result = lax.cond(
            fits,
            lambda done: done,
            lambda done: attend(whole, my_step * plane_rows + my_ids % plane_rows)[0],
            result,
        )
    return patch(my_slot, result, odd_part)


def solution(mesh):
    placed = (
        P("db", "mp"),
        P(("db", "mp"), None, None),
        P("db", "mp"),
        P("db", "mp"),
        P("db", None),
        P("db", None),
    )

    return jax.shard_map(local, mesh=mesh, in_specs=placed, out_specs=P("db", "mp"), check_vma=False)
```

```python
import functools
import math

import jax
import jax.numpy as jnp
from jax import lax
from jax.experimental import pallas as pl
from jax.experimental.pallas import tpu as pltpu
from jax.sharding import PartitionSpec as P


DH = 128
SPAN = 64
SEQ = 128
LANES = 8
CHUNKS = 2
MOST_SHIFTS = 8
TAIL = 16
FAST_SLOTS = 48
BF16 = jnp.bfloat16
F32 = jnp.float32
SCALE = 1.0 / math.sqrt(DH)
BOTH = ("db", "mp")
CONTRACT_LAST = (((1,), (1,)), ((), ()))


def project_body(rows_ref, weight_ref, out_ref):
    lanes, count, piece, width = rows_ref.shape
    rows = rows_ref[...]
    stacked = jnp.concatenate([rows[:, j].reshape(lanes * piece, width) for j in range(count)], axis=0)
    out_ref[...] = jnp.dot(stacked, weight_ref[...], preferred_element_type=F32).astype(BF16)


def project(rows, weights):
    lanes, count, piece, width = rows.shape
    per_step = math.gcd(count, 8)
    tokens = lanes * piece
    return pl.pallas_call(
        project_body,
        out_shape=jax.ShapeDtypeStruct((count * tokens, weights.shape[1]), BF16),
        grid=(count // per_step,),
        in_specs=[
            pl.BlockSpec((lanes, per_step, piece, width), lambda i: (0, i, 0, 0)),
            pl.BlockSpec(weights.shape, lambda i: (0, 0)),
        ],
        out_specs=pl.BlockSpec((per_step * tokens, weights.shape[1]), lambda i: (i, 0)),
        name="project",
    )(rows, weights)


def even_body(query_ref, rows_ref, weight_ref, *refs, per_step, neighbours):
    early_refs, out_ref = refs[:-1], refs[-1]
    columns = query_ref.shape[1]
    heads = columns // DH
    lanes, _, piece, width = rows_ref.shape
    tokens = lanes * piece
    first = SPAN - 1
    low = first // 16 * 16
    rows = rows_ref[...]
    stacked = jnp.concatenate(
        [rows[:, j].reshape(tokens, width) for j in range(per_step * neighbours)], axis=0
    )
    late = jnp.dot(stacked, weight_ref[...], preferred_element_type=F32).astype(BF16)
    position = low + lax.broadcasted_iota(jnp.int32, (SEQ - low, DH), 0)
    span = neighbours * tokens
    for s in range(per_step):
        out_ref[s * SEQ : s * SEQ + low, :] = jnp.zeros((low, columns), BF16)
        for h in range(heads):
            lo, hi = h * DH, (h + 1) * DH
            parts = [(r, s * span, span) for r in (*early_refs, late)]
            keys = jnp.concatenate([r[b : b + n, lo:hi] for r, b, n in parts], axis=0)
            values = jnp.concatenate([r[b : b + n, columns + lo : columns + hi] for r, b, n in parts], axis=0)
            query = query_ref[s * SEQ + low : (s + 1) * SEQ, lo:hi]
            scores = lax.dot_general(query, keys, CONTRACT_LAST, preferred_element_type=F32) * SCALE
            largest = jnp.max(scores, axis=1, keepdims=True)
            expscore = jnp.exp(scores - largest)
            total = jnp.sum(expscore, axis=1, keepdims=True)
            mixed = jnp.dot(expscore.astype(BF16), values, preferred_element_type=F32)
            attended = mixed / total
            attended = jnp.where(position < first, 0.0, attended)
            out_ref[s * SEQ + low : (s + 1) * SEQ, lo:hi] = attended.astype(BF16)


def even_attention(queries, rows, weights, early):
    tokens, columns = queries.shape
    sequences = tokens // SEQ
    lanes, count, piece, width = rows.shape
    neighbours = count // sequences
    per_step = math.gcd(sequences, 2)
    early_rows = lanes * piece * per_step * neighbours
    early_spec = pl.BlockSpec((early_rows, weights.shape[1]), lambda i: (i, 0))
    return pl.pallas_call(
        functools.partial(even_body, per_step=per_step, neighbours=neighbours),
        out_shape=jax.ShapeDtypeStruct(queries.shape, BF16),
        grid=(sequences // per_step,),
        in_specs=[
            pl.BlockSpec((per_step * SEQ, columns), lambda i: (i, 0)),
            pl.BlockSpec((lanes, per_step * neighbours, piece, width), lambda i: (0, i, 0, 0)),
            pl.BlockSpec(weights.shape, lambda i: (0, 0)),
            *[early_spec for _ in early],
        ],
        out_specs=pl.BlockSpec((per_step * SEQ, columns), lambda i: (i, 0)),
        name="even_attention",
    )(queries, rows, weights, *early)


def patch_body(slot_ref, out_in_ref, odd_ref, out_ref, *rest, neighbours):
    picked_refs, row_ref = rest[:-1], rest[-1]
    per_step, _, tail, columns = out_ref.shape
    heads = columns // DH
    sequences = row_ref.shape[0]
    step = pl.program_id(0)

    @pl.when(step == 0)
    def _():
        for i in range(sequences):
            for j, picked_ref in enumerate(picked_refs):
                picked_ref[i : i + 1, :] = odd_ref[pl.ds(slot_ref[i * neighbours + j], 1), :]
        for h in range(heads):
            lo, hi = h * DH, (h + 1) * DH
            maxima = [p[:, columns + h : columns + h + 1] for p in picked_refs]
            sums = [p[:, columns + DH // 2 + h : columns + DH // 2 + h + 1] for p in picked_refs]
            top = functools.reduce(jnp.maximum, maxima)
            each = [jnp.exp(m - top) for m in maxima]
            under = sum(e * t for e, t in zip(each, sums))
            over = sum(e * p[:, lo:hi] for e, p in zip(each, picked_refs))
            row_ref[:, lo:hi] = over / under

    last = lax.broadcasted_iota(jnp.int32, (tail, columns), 0) == tail - 1
    for i in range(per_step):
        row = row_ref[pl.ds(step * per_step + i, 1), :]
        out_ref[i, 0] = jnp.where(last, row, out_in_ref[i, 0].astype(F32)).astype(BF16)


def patch(slots, out, odd):
    tokens, columns = out.shape
    sequences = tokens // SEQ
    neighbours = slots.shape[0] // sequences
    per_step = math.gcd(sequences, 4)
    blocks = SEQ // TAIL
    tail = pl.BlockSpec((per_step, 1, TAIL, columns), lambda i, s: (i, blocks - 1, 0, 0))
    shape = (sequences, blocks, TAIL, columns)
    return pl.pallas_call(
        functools.partial(patch_body, neighbours=neighbours),
        out_shape=jax.ShapeDtypeStruct(shape, BF16),
        grid_spec=pltpu.PrefetchScalarGridSpec(
            num_scalar_prefetch=1,
            grid=(sequences // per_step,),
            in_specs=[tail, pl.BlockSpec(odd.shape, lambda i, s: (0, 0))],
            out_specs=tail,
            scratch_shapes=[pltpu.VMEM((sequences, odd.shape[1]), F32)] * neighbours
            + [pltpu.VMEM((sequences, columns), F32)],
        ),
        input_output_aliases={1: 0},
        name="patch",
    )(slots, out.reshape(shape), odd).reshape(out.shape)


def gather_body(index_ref, *refs, count):
    sources, out_ref, stage_ref, sem_ref = refs[:count], refs[count], refs[count + 1], refs[count + 2]
    size = sources[0].shape[0]
    copies, wanted = out_ref.shape[1:3]
    base = pl.program_id(0) * wanted

    @pl.when(pl.program_id(0) == 0)
    def _():
        moves = [
            pltpu.make_async_copy(source, stage_ref.at[pl.ds(k * size, size)], sem_ref.at[k])
            for k, source in enumerate(sources)
        ]
        for move in moves:
            move.start()
        for move in moves:
            move.wait()

    def step(i, carry):
        row = stage_ref[index_ref[base + i]]
        for c in range(copies):
            out_ref[0, c, i] = row
        return carry

    lax.fori_loop(0, wanted, step, 0, unroll=8)


def gather_rows(index, sources, groups, copies):
    wanted = index.shape[0] // groups
    size, piece, width = sources[0].shape
    out = pl.pallas_call(
        functools.partial(gather_body, count=len(sources)),
        out_shape=jax.ShapeDtypeStruct((groups, copies, wanted, piece, width), sources[0].dtype),
        grid_spec=pltpu.PrefetchScalarGridSpec(
            num_scalar_prefetch=1,
            grid=(groups,),
            in_specs=[pl.BlockSpec(memory_space=pl.ANY) for _ in sources],
            out_specs=pl.BlockSpec((1, copies, wanted, piece, width), lambda i, s: (i, 0, 0, 0, 0)),
            scratch_shapes=[
                pltpu.VMEM((len(sources) * size, piece, width), sources[0].dtype),
                pltpu.SemaphoreType.DMA((len(sources),)),
            ],
        ),
        name="gather_rows",
    )(index, *sources)
    return out.reshape(groups * copies * wanted, piece, width)


def select_body(index_ref, source_ref, *out_refs):
    fast = out_refs[0].shape[0]

    def step(i, carry):
        for k, out_ref in enumerate(out_refs):
            out_ref[i] = source_ref[index_ref[k * fast + i]]
        return carry

    lax.fori_loop(0, fast, step, 0, unroll=2)


def select_rows(index, source):
    count, fast = index.shape
    block = pl.BlockSpec((fast,) + source.shape[1:], lambda i, s: (0, 0, 0))
    return pl.pallas_call(
        select_body,
        out_shape=[jax.ShapeDtypeStruct((fast,) + source.shape[1:], source.dtype)] * count,
        grid_spec=pltpu.PrefetchScalarGridSpec(
            num_scalar_prefetch=1,
            grid=(1,),
            in_specs=[pl.BlockSpec(source.shape, lambda i, s: (0, 0, 0))],
            out_specs=[block] * count,
        ),
        name="select_rows",
    )(index.reshape(-1), source)


def odd_body(query_ref, want_ref, *refs):
    rows_refs, (weight_ref, prior_ref, out_ref) = refs[:-3], refs[-3:]
    columns = query_ref.shape[1]
    heads = columns // DH
    lanes, per_step, piece, width = rows_refs[0].shape
    tokens = len(rows_refs) * lanes * piece
    step = pl.program_id(0)

    @pl.when(step == 0)
    def _():
        out_ref[...] = prior_ref[...]

    pieces = [ref[...] for ref in rows_refs]
    stacked = jnp.concatenate(
        [p[:, r].reshape(lanes * piece, width) for r in range(per_step) for p in pieces], axis=0
    )
    projected = jnp.dot(stacked, weight_ref[...], preferred_element_type=F32).astype(BF16)
    want = want_ref[...] - step * per_step
    here = [want == r for r in range(per_step)]
    inside = (want >= 0) & (want < per_step)
    lane = lax.broadcasted_iota(jnp.int32, (want.shape[0], DH), 1)
    stats = out_ref[:, columns:]
    for h in range(heads):
        lo, hi = h * DH, (h + 1) * DH
        scores = (
            lax.dot_general(
                query_ref[:, lo:hi], projected[:, lo:hi], CONTRACT_LAST, preferred_element_type=F32
            )
            * SCALE
        )
        mine = jnp.zeros((want.shape[0], tokens), F32)
        for r in range(per_step):
            mine = jnp.where(here[r], scores[:, r * tokens : (r + 1) * tokens], mine)
        largest = jnp.max(mine, axis=1, keepdims=True)
        expscore = jnp.exp(mine - largest)
        total = jnp.sum(expscore, axis=1, keepdims=True)
        spread = jnp.concatenate([jnp.where(here[r], expscore, 0.0) for r in range(per_step)], axis=1)
        mixed = jnp.dot(spread.astype(BF16), projected[:, columns + lo : columns + hi], preferred_element_type=F32)
        out_ref[:, lo:hi] = jnp.where(inside, mixed, out_ref[:, lo:hi])
        stats = jnp.where(inside & (lane == h), largest, stats)
        stats = jnp.where(inside & (lane == DH // 2 + h), total, stats)
    out_ref[:, columns:] = stats


def odd_attention(queries, want, rows, weights, prior):
    slots, columns = queries.shape
    lanes, count, piece, width = rows[0].shape
    per_step = math.gcd(count, 4)
    row_spec = pl.BlockSpec((lanes, per_step, piece, width), lambda i: (0, i, 0, 0))
    return pl.pallas_call(
        odd_body,
        out_shape=jax.ShapeDtypeStruct(prior.shape, F32),
        grid=(count // per_step,),
        in_specs=[
            pl.BlockSpec((slots, columns), lambda i: (0, 0)),
            pl.BlockSpec((slots, DH), lambda i: (0, 0)),
            *[row_spec for _ in rows],
            pl.BlockSpec(weights.shape, lambda i: (0, 0)),
            pl.BlockSpec(prior.shape, lambda i: (0, 0)),
        ],
        out_specs=pl.BlockSpec(prior.shape, lambda i: (0, 0)),
        name="odd_attention",
    )(queries, want, *rows, weights, prior)


def local(queries, encodings, key_weight, value_weight, nbr_shard, nbr_row):
    shards = lax.axis_size("db")
    parts = lax.axis_size("mp")
    group = max(1, LANES // parts)
    lanes = group * parts
    planes = shards // group
    columns = queries.shape[1]
    held, tokens, width = encodings.shape
    piece = tokens // (lanes * CHUNKS)
    shard_rows = held * parts
    plane_rows = group * shard_rows
    span_count, neighbours = nbr_shard.shape
    sequences = queries.shape[0] // SEQ
    wanted = sequences * neighbours
    capacity = max(2, 4 * span_count // shards)
    most = min(plane_rows, group * wanted, group * group * capacity)
    fast = min(most, FAST_SLOTS)
    plane_groups = [[a * lanes + b for b in range(lanes)] for a in range(planes)]
    lane_groups = [[a * lanes + b for a in range(planes)] for b in range(lanes)]
    db_index = lax.axis_index("db")
    plane_index = db_index // group

    def swap(x, groups):
        return lax.all_to_all(x, BOTH, 0, 0, axis_index_groups=groups, tiled=True)

    def across(blocks):
        if planes > MOST_SHIFTS:
            stacked = jnp.stack(blocks)
            ordered = jnp.take(stacked, (jnp.arange(planes) - plane_index) % planes, axis=0, mode="clip")
            ordered = swap(ordered.reshape((-1,) + stacked.shape[2:]), lane_groups).reshape(stacked.shape)
            moved = jnp.take(ordered, (plane_index - jnp.arange(planes)) % planes, axis=0, mode="clip")
            return [moved.reshape((-1,) + stacked.shape[2:])]
        moved = [blocks[0]]
        for k in range(1, planes):
            pairs = [
                (a * lanes + b, (a + k) % planes * lanes + b) for a in range(planes) for b in range(lanes)
            ]
            moved.append(lax.ppermute(blocks[k], BOTH, pairs))
        return moved

    table = jnp.concatenate([nbr_shard.reshape(-1), nbr_row.reshape(-1)])
    table = jnp.broadcast_to(table[None, None], (shards, 1, table.shape[0]))
    table = lax.all_to_all(table, "db", 0, 0, tiled=True).reshape(
        shards, 2, sequences, SEQ // SPAN, neighbours
    )
    table_shard, table_row = table[:, 0], table[:, 1]

    weights = lax.all_gather(
        jnp.concatenate([key_weight, value_weight], axis=1), "db", axis=0, tiled=True
    )

    early_half, late_half = jnp.transpose(encodings.reshape(held, lanes, CHUNKS, piece, width), (2, 1, 0, 3, 4))
    first, _ = lax.optimization_barrier((early_half.reshape(lanes * held, piece, width), table))
    first = swap(first, plane_groups)

    part_index = lax.axis_index("mp")

    def share(half, after):
        half, _ = lax.optimization_barrier((half, after))
        shared = [half]
        for k in range(1, parts):
            shared.append(lax.ppermute(half, "mp", [(m, (m + k) % parts) for m in range(parts)]))
        return shared

    late_shared = share(late_half, first)
    second = [
        lax.dynamic_index_in_dim(
            half.reshape(group, parts, held, piece, width), part_index, 1, keepdims=False
        )
        for half in late_shared
    ]
    second = jnp.concatenate(second, axis=1).reshape(group * shard_rows, piece, width)
    part_groups = [
        [a * lanes + g * parts + m for g in range(group)] for a in range(planes) for m in range(parts)
    ]
    second, _ = lax.optimization_barrier((second, first))
    if group > 1:
        second = swap(second, part_groups)
    early_shared = share(early_half, late_shared)
    plane_pieces = [first, second]

    def stepped(row):
        step = (part_index + parts - row % shard_rows // held) % parts
        return row // shard_rows * shard_rows + step * held + row % held

    odd_shard = table_shard[:, :, 1].reshape(shards, wanted)
    odd_row = table_row[:, :, 1].reshape(shards, wanted)
    earlier = jnp.arange(wanted)
    same = (odd_shard[:, :, None] == odd_shard[:, None, :]) & (earlier[None, None, :] < earlier[None, :, None])
    odd_rank = jnp.sum(same.astype(jnp.int32), axis=2)
    arriving = (odd_shard == db_index)[:, None, :] & (
        odd_rank[:, None, :] == jnp.arange(capacity, dtype=jnp.int32)[None, :, None]
    )
    slot_row = jnp.sum(jnp.where(arriving, odd_row[:, None, :] + 1, 0), axis=2) - 1
    my_slot = lax.dynamic_index_in_dim(odd_shard * capacity + odd_rank, db_index, 0, keepdims=False)
    slots = jnp.arange(shards * capacity, dtype=jnp.int32)
    chosen = my_slot[None, :] == slots[:, None]
    sender = jnp.sum(jnp.where(chosen, (earlier // neighbours).astype(jnp.int32)[None, :], 0), axis=1)
    last_rows = queries.reshape(sequences, SEQ, columns)[:, SEQ - 1]
    odd_query = jnp.take(last_rows, sender, axis=0, mode="clip").reshape(shards, capacity, columns)
    odd_query, _ = lax.optimization_barrier((odd_query, plane_pieces[-1]))
    odd_query = lax.all_to_all(odd_query, "db", 0, 0, tiled=True)
    odd_query = odd_query.reshape(shards * capacity, columns)

    even_id = (table_shard[:, :, 0] * shard_rows + table_row[:, :, 0]).reshape(planes, group * wanted)
    ids = jnp.arange(planes * plane_rows, dtype=jnp.int32)
    want = jnp.any(even_id[:, :, None] == ids[None, None, :], axis=1).reshape(planes, planes, plane_rows)
    below = jnp.arange(plane_rows)
    before = (below[:, None] < below[None, :]).astype(BF16)
    rank = jnp.dot(want.astype(BF16), before, preferred_element_type=F32).astype(jnp.int32)
    fits = jnp.max(jnp.sum(want.astype(jnp.int32), axis=2)) <= fast
    mine_want = lax.dynamic_index_in_dim(want, plane_index, 1, keepdims=False)
    mine_rank = lax.dynamic_index_in_dim(rank, plane_index, 1, keepdims=False)
    picks = mine_want[:, None, :] & (
        mine_rank[:, None, :] == jnp.arange(fast, dtype=jnp.int32)[None, :, None]
    )
    send_rows = jnp.sum(jnp.where(picks, below[None, None, :].astype(jnp.int32), 0), axis=2)
    steps = jnp.arange(planes, dtype=jnp.int32)
    upward = (plane_index + steps) % planes
    send_rows = jnp.sum(
        jnp.where(upward[:, None, None] == steps[None, :, None], send_rows[None], 0), axis=1
    )
    my_ids = lax.dynamic_index_in_dim(even_id, plane_index, 0, keepdims=False)
    my_rank = lax.dynamic_index_in_dim(rank, plane_index, 0, keepdims=False).reshape(-1)
    place = jnp.sum(jnp.where(my_ids[:, None] == ids[None, :], my_rank[None, :], 0), axis=1)
    my_step = (plane_index + planes - my_ids // plane_rows) % planes

    def exact(source, chunk):
        rows = stepped(send_rows) if chunk else send_rows
        if planes > MOST_SHIFTS:
            return [jnp.take(source, rows[k], axis=0, mode="clip") for k in range(planes)]
        return select_rows(rows, source)

    def whole(source, chunk):
        return [source] * planes

    def exchange(sources, select, index):
        received, arrived = [], []
        for chunk, source in enumerate(sources):
            sending = select(source, chunk)
            if received:
                sending, _ = lax.optimization_barrier((sending, received[-1]))
            received.append(across(sending))
            outgoing = gather_rows(index[chunk], received[-1], group, parts)
            outgoing, _ = lax.optimization_barrier((outgoing, arrived[-1] if arrived else odd_query))
            arrived.append(swap(outgoing, plane_groups))
        return [a.reshape(lanes, wanted, piece, width) for a in arrived]

    odd_part = jnp.zeros((shards * capacity, columns + DH), F32)
    for k in range(parts):
        slot_want = slot_row - (part_index + parts - k) % parts * held
        slot_want = jnp.broadcast_to(slot_want.reshape(-1, 1), (shards * capacity, DH))
        odd_part = odd_attention(
            odd_query, slot_want, (early_shared[k], late_shared[k]), weights, odd_part
        )

    def attend(select, index):
        *early, late = exchange(plane_pieces, select, index)
        early = [project(e, weights) for e in early]
        return even_attention(queries, late, weights, early), late

    fast_index = my_step * fast + jnp.minimum(place, fast - 1)
    result, last = attend(exact, [fast_index] * CHUNKS)
    odd_part, _ = lax.optimization_barrier((odd_part, last))
    odd_part = lax.all_to_all(odd_part.reshape(shards, capacity, columns + DH), "db", 0, 0, tiled=True)
    odd_part = odd_part.reshape(shards * capacity, columns + DH)
    if fast < most:
        result, odd_part = lax.optimization_barrier((result, odd_part))
        result = lax.cond(
            fits,
            lambda done: done,
            lambda done: attend(
                whole, [my_step * plane_rows + row for row in (my_ids % plane_rows, stepped(my_ids % plane_rows))]
            )[0],
            result,
        )
    return patch(my_slot, result, odd_part)


def solution(mesh):
    placed = (
        P("db", "mp"),
        P(("db", "mp"), None, None),
        P("db", "mp"),
        P("db", "mp"),
        P("db", None),
        P("db", None),
    )

    return jax.shard_map(local, mesh=mesh, in_specs=placed, out_specs=P("db", "mp"), check_vma=False)
```

```python
import functools
import math

import jax
import jax.numpy as jnp
from jax import lax
from jax.experimental import pallas as pl
from jax.experimental.pallas import tpu as pltpu
from jax.sharding import PartitionSpec as P


DH = 128
SPAN = 64
SEQ = 128
LANES = 8
CHUNKS = 2
MOST_SHIFTS = 8
TAIL = 16
FAST_SLOTS = 48
BF16 = jnp.bfloat16
F32 = jnp.float32
SCALE = 1.0 / math.sqrt(DH)
BOTH = ("db", "mp")
CONTRACT_LAST = (((1,), (1,)), ((), ()))


def project_body(rows_ref, weight_ref, out_ref):
    lanes, count, piece, width = rows_ref.shape
    rows = rows_ref[...]
    stacked = jnp.concatenate([rows[:, j].reshape(lanes * piece, width) for j in range(count)], axis=0)
    out_ref[...] = jnp.dot(stacked, weight_ref[...], preferred_element_type=F32).astype(BF16)


def project(rows, weights):
    lanes, count, piece, width = rows.shape
    per_step = math.gcd(count, 8)
    tokens = lanes * piece
    return pl.pallas_call(
        project_body,
        out_shape=jax.ShapeDtypeStruct((count * tokens, weights.shape[1]), BF16),
        grid=(count // per_step,),
        in_specs=[
            pl.BlockSpec((lanes, per_step, piece, width), lambda i: (0, i, 0, 0)),
            pl.BlockSpec(weights.shape, lambda i: (0, 0)),
        ],
        out_specs=pl.BlockSpec((per_step * tokens, weights.shape[1]), lambda i: (i, 0)),
        name="project",
    )(rows, weights)


def even_body(query_ref, rows_ref, weight_ref, *refs, per_step, neighbours):
    early_refs, out_ref = refs[:-1], refs[-1]
    columns = query_ref.shape[1]
    heads = columns // DH
    lanes, _, piece, width = rows_ref.shape
    tokens = lanes * piece
    first = SPAN - 1
    low = first // 16 * 16
    rows = rows_ref[...]
    stacked = jnp.concatenate(
        [rows[:, j].reshape(tokens, width) for j in range(per_step * neighbours)], axis=0
    )
    late = jnp.dot(stacked, weight_ref[...], preferred_element_type=F32).astype(BF16)
    position = low + lax.broadcasted_iota(jnp.int32, (SEQ - low, DH), 0)
    span = neighbours * tokens
    for s in range(per_step):
        out_ref[s * SEQ : s * SEQ + low, :] = jnp.zeros((low, columns), BF16)
        for h in range(heads):
            lo, hi = h * DH, (h + 1) * DH
            parts = [(r, s * span, span) for r in (*early_refs, late)]
            keys = jnp.concatenate([r[b : b + n, lo:hi] for r, b, n in parts], axis=0)
            values = jnp.concatenate([r[b : b + n, columns + lo : columns + hi] for r, b, n in parts], axis=0)
            query = query_ref[s * SEQ + low : (s + 1) * SEQ, lo:hi]
            scores = lax.dot_general(query, keys, CONTRACT_LAST, preferred_element_type=F32) * SCALE
            largest = jnp.max(scores, axis=1, keepdims=True)
            expscore = jnp.exp(scores - largest)
            total = jnp.sum(expscore, axis=1, keepdims=True)
            mixed = jnp.dot(expscore.astype(BF16), values, preferred_element_type=F32)
            attended = mixed / total
            attended = jnp.where(position < first, 0.0, attended)
            out_ref[s * SEQ + low : (s + 1) * SEQ, lo:hi] = attended.astype(BF16)


def even_attention(queries, rows, weights, early):
    tokens, columns = queries.shape
    sequences = tokens // SEQ
    lanes, count, piece, width = rows.shape
    neighbours = count // sequences
    per_step = math.gcd(sequences, 2)
    early_rows = lanes * piece * per_step * neighbours
    early_spec = pl.BlockSpec((early_rows, weights.shape[1]), lambda i: (i, 0))
    return pl.pallas_call(
        functools.partial(even_body, per_step=per_step, neighbours=neighbours),
        out_shape=jax.ShapeDtypeStruct(queries.shape, BF16),
        grid=(sequences // per_step,),
        in_specs=[
            pl.BlockSpec((per_step * SEQ, columns), lambda i: (i, 0)),
            pl.BlockSpec((lanes, per_step * neighbours, piece, width), lambda i: (0, i, 0, 0)),
            pl.BlockSpec(weights.shape, lambda i: (0, 0)),
            *[early_spec for _ in early],
        ],
        out_specs=pl.BlockSpec((per_step * SEQ, columns), lambda i: (i, 0)),
        name="even_attention",
    )(queries, rows, weights, *early)


def patch_body(slot_ref, out_in_ref, odd_ref, out_ref, *rest, neighbours):
    picked_refs, row_ref = rest[:-1], rest[-1]
    per_step, _, tail, columns = out_ref.shape
    heads = columns // DH
    sequences = row_ref.shape[0]
    step = pl.program_id(0)

    @pl.when(step == 0)
    def _():
        for i in range(sequences):
            for j, picked_ref in enumerate(picked_refs):
                picked_ref[i : i + 1, :] = odd_ref[pl.ds(slot_ref[i * neighbours + j], 1), :]
        for h in range(heads):
            lo, hi = h * DH, (h + 1) * DH
            maxima = [p[:, columns + h : columns + h + 1] for p in picked_refs]
            sums = [p[:, columns + DH // 2 + h : columns + DH // 2 + h + 1] for p in picked_refs]
            top = functools.reduce(jnp.maximum, maxima)
            each = [jnp.exp(m - top) for m in maxima]
            under = sum(e * t for e, t in zip(each, sums))
            over = sum(e * p[:, lo:hi] for e, p in zip(each, picked_refs))
            row_ref[:, lo:hi] = over / under

    last = lax.broadcasted_iota(jnp.int32, (tail, columns), 0) == tail - 1
    for i in range(per_step):
        row = row_ref[pl.ds(step * per_step + i, 1), :]
        out_ref[i, 0] = jnp.where(last, row, out_in_ref[i, 0].astype(F32)).astype(BF16)


def patch(slots, out, odd):
    tokens, columns = out.shape
    sequences = tokens // SEQ
    neighbours = slots.shape[0] // sequences
    per_step = math.gcd(sequences, 4)
    blocks = SEQ // TAIL
    tail = pl.BlockSpec((per_step, 1, TAIL, columns), lambda i, s: (i, blocks - 1, 0, 0))
    shape = (sequences, blocks, TAIL, columns)
    return pl.pallas_call(
        functools.partial(patch_body, neighbours=neighbours),
        out_shape=jax.ShapeDtypeStruct(shape, BF16),
        grid_spec=pltpu.PrefetchScalarGridSpec(
            num_scalar_prefetch=1,
            grid=(sequences // per_step,),
            in_specs=[tail, pl.BlockSpec(odd.shape, lambda i, s: (0, 0))],
            out_specs=tail,
            scratch_shapes=[pltpu.VMEM((sequences, odd.shape[1]), F32)] * neighbours
            + [pltpu.VMEM((sequences, columns), F32)],
        ),
        input_output_aliases={1: 0},
        name="patch",
    )(slots, out.reshape(shape), odd).reshape(out.shape)


def gather_body(index_ref, *refs, count):
    sources, out_ref, stage_ref, sem_ref = refs[:count], refs[count], refs[count + 1], refs[count + 2]
    copies, wanted = out_ref.shape[1:3]
    starts = [sum(s.shape[0] for s in sources[:k]) for k in range(count)]
    base = pl.program_id(0) * wanted

    @pl.when(pl.program_id(0) == 0)
    def _():
        moves = [
            pltpu.make_async_copy(source, stage_ref.at[pl.ds(starts[k], source.shape[0])], sem_ref.at[k])
            for k, source in enumerate(sources)
        ]
        for move in moves:
            move.start()
        for move in moves:
            move.wait()

    def step(i, carry):
        row = stage_ref[index_ref[base + i]]
        for c in range(copies):
            out_ref[0, c, i] = row
        return carry

    lax.fori_loop(0, wanted, step, 0, unroll=8)


def gather_rows(index, sources, groups, copies):
    wanted = index.shape[0] // groups
    piece, width = sources[0].shape[1:]
    out = pl.pallas_call(
        functools.partial(gather_body, count=len(sources)),
        out_shape=jax.ShapeDtypeStruct((groups, copies, wanted, piece, width), sources[0].dtype),
        grid_spec=pltpu.PrefetchScalarGridSpec(
            num_scalar_prefetch=1,
            grid=(groups,),
            in_specs=[pl.BlockSpec(memory_space=pl.ANY) for _ in sources],
            out_specs=pl.BlockSpec((1, copies, wanted, piece, width), lambda i, s: (i, 0, 0, 0, 0)),
            scratch_shapes=[
                pltpu.VMEM((sum(s.shape[0] for s in sources), piece, width), sources[0].dtype),
                pltpu.SemaphoreType.DMA((len(sources),)),
            ],
        ),
        name="gather_rows",
    )(index, *sources)
    return out.reshape(groups * copies * wanted, piece, width)


def select_body(index_ref, source_ref, *out_refs):
    fast = out_refs[0].shape[0]

    def step(i, carry):
        for k, out_ref in enumerate(out_refs):
            out_ref[i] = source_ref[index_ref[k * fast + i]]
        return carry

    lax.fori_loop(0, fast, step, 0, unroll=2)


def select_rows(index, source):
    count, fast = index.shape
    block = pl.BlockSpec((fast,) + source.shape[1:], lambda i, s: (0, 0, 0))
    return pl.pallas_call(
        select_body,
        out_shape=[jax.ShapeDtypeStruct((fast,) + source.shape[1:], source.dtype)] * count,
        grid_spec=pltpu.PrefetchScalarGridSpec(
            num_scalar_prefetch=1,
            grid=(1,),
            in_specs=[pl.BlockSpec(source.shape, lambda i, s: (0, 0, 0))],
            out_specs=[block] * count,
        ),
        name="select_rows",
    )(index.reshape(-1), source)


def odd_body(query_ref, want_ref, *refs):
    rows_refs, (weight_ref, prior_ref, out_ref) = refs[:-3], refs[-3:]
    columns = query_ref.shape[1]
    heads = columns // DH
    lanes, per_step, piece, width = rows_refs[0].shape
    tokens = len(rows_refs) * lanes * piece
    step = pl.program_id(0)

    @pl.when(step == 0)
    def _():
        out_ref[...] = prior_ref[...]

    pieces = [ref[...] for ref in rows_refs]
    stacked = jnp.concatenate(
        [p[:, r].reshape(lanes * piece, width) for r in range(per_step) for p in pieces], axis=0
    )
    projected = jnp.dot(stacked, weight_ref[...], preferred_element_type=F32).astype(BF16)
    want = want_ref[...] - step * per_step
    here = [want == r for r in range(per_step)]
    inside = (want >= 0) & (want < per_step)
    lane = lax.broadcasted_iota(jnp.int32, (want.shape[0], DH), 1)
    stats = out_ref[:, columns:]
    for h in range(heads):
        lo, hi = h * DH, (h + 1) * DH
        scores = (
            lax.dot_general(
                query_ref[:, lo:hi], projected[:, lo:hi], CONTRACT_LAST, preferred_element_type=F32
            )
            * SCALE
        )
        mine = jnp.zeros((want.shape[0], tokens), F32)
        for r in range(per_step):
            mine = jnp.where(here[r], scores[:, r * tokens : (r + 1) * tokens], mine)
        largest = jnp.max(mine, axis=1, keepdims=True)
        expscore = jnp.exp(mine - largest)
        total = jnp.sum(expscore, axis=1, keepdims=True)
        spread = jnp.concatenate([jnp.where(here[r], expscore, 0.0) for r in range(per_step)], axis=1)
        mixed = jnp.dot(spread.astype(BF16), projected[:, columns + lo : columns + hi], preferred_element_type=F32)
        out_ref[:, lo:hi] = jnp.where(inside, mixed, out_ref[:, lo:hi])
        stats = jnp.where(inside & (lane == h), largest, stats)
        stats = jnp.where(inside & (lane == DH // 2 + h), total, stats)
    out_ref[:, columns:] = stats


def odd_attention(queries, want, rows, weights, prior):
    slots, columns = queries.shape
    lanes, count, piece, width = rows[0].shape
    per_step = math.gcd(count, 4)
    row_spec = pl.BlockSpec((lanes, per_step, piece, width), lambda i: (0, i, 0, 0))
    return pl.pallas_call(
        odd_body,
        out_shape=jax.ShapeDtypeStruct(prior.shape, F32),
        grid=(count // per_step,),
        in_specs=[
            pl.BlockSpec((slots, columns), lambda i: (0, 0)),
            pl.BlockSpec((slots, DH), lambda i: (0, 0)),
            *[row_spec for _ in rows],
            pl.BlockSpec(weights.shape, lambda i: (0, 0)),
            pl.BlockSpec(prior.shape, lambda i: (0, 0)),
        ],
        out_specs=pl.BlockSpec(prior.shape, lambda i: (0, 0)),
        name="odd_attention",
    )(queries, want, *rows, weights, prior)


def local(queries, encodings, key_weight, value_weight, nbr_shard, nbr_row):
    shards = lax.axis_size("db")
    parts = lax.axis_size("mp")
    group = max(1, LANES // parts)
    lanes = group * parts
    planes = shards // group
    columns = queries.shape[1]
    held, tokens, width = encodings.shape
    piece = tokens // (lanes * CHUNKS)
    shard_rows = held * parts
    plane_rows = group * shard_rows
    span_count, neighbours = nbr_shard.shape
    sequences = queries.shape[0] // SEQ
    wanted = sequences * neighbours
    capacity = max(2, 4 * span_count // shards)
    most = min(plane_rows, group * wanted, group * group * capacity)
    fast = min(most, FAST_SLOTS)
    plane_groups = [[a * lanes + b for b in range(lanes)] for a in range(planes)]
    lane_groups = [[a * lanes + b for a in range(planes)] for b in range(lanes)]
    db_index = lax.axis_index("db")
    plane_index = db_index // group

    def swap(x, groups):
        return lax.all_to_all(x, BOTH, 0, 0, axis_index_groups=groups, tiled=True)

    def across(blocks):
        if planes > MOST_SHIFTS:
            stacked = jnp.stack(blocks)
            ordered = jnp.take(stacked, (jnp.arange(planes) - plane_index) % planes, axis=0, mode="clip")
            ordered = swap(ordered.reshape((-1,) + stacked.shape[2:]), lane_groups).reshape(stacked.shape)
            moved = jnp.take(ordered, (plane_index - jnp.arange(planes)) % planes, axis=0, mode="clip")
            return [moved.reshape((-1,) + stacked.shape[2:])]
        moved = [blocks[0]]
        for k in range(1, planes):
            pairs = [
                (a * lanes + b, (a + k) % planes * lanes + b) for a in range(planes) for b in range(lanes)
            ]
            moved.append(lax.ppermute(blocks[k], BOTH, pairs))
        return moved

    table = jnp.concatenate([nbr_shard.reshape(-1), nbr_row.reshape(-1)])
    table = jnp.broadcast_to(table[None, None], (shards, 1, table.shape[0]))
    table = lax.all_to_all(table, "db", 0, 0, tiled=True).reshape(
        shards, 2, sequences, SEQ // SPAN, neighbours
    )
    table_shard, table_row = table[:, 0], table[:, 1]

    weights = lax.all_gather(
        jnp.concatenate([key_weight, value_weight], axis=1), "db", axis=0, tiled=True
    )

    early_half, late_half = jnp.transpose(encodings.reshape(held, lanes, CHUNKS, piece, width), (2, 1, 0, 3, 4))
    first, _ = lax.optimization_barrier((early_half.reshape(lanes * held, piece, width), table))
    first = swap(first, plane_groups)

    odd_shard = table_shard[:, :, 1].reshape(shards, wanted)
    odd_row = table_row[:, :, 1].reshape(shards, wanted)
    earlier = jnp.arange(wanted)
    same = (odd_shard[:, :, None] == odd_shard[:, None, :]) & (earlier[None, None, :] < earlier[None, :, None])
    odd_rank = jnp.sum(same.astype(jnp.int32), axis=2)
    arriving = (odd_shard == db_index)[:, None, :] & (
        odd_rank[:, None, :] == jnp.arange(capacity, dtype=jnp.int32)[None, :, None]
    )
    slot_row = jnp.sum(jnp.where(arriving, odd_row[:, None, :] + 1, 0), axis=2) - 1
    my_slot = lax.dynamic_index_in_dim(odd_shard * capacity + odd_rank, db_index, 0, keepdims=False)
    slots = jnp.arange(shards * capacity, dtype=jnp.int32)
    chosen = my_slot[None, :] == slots[:, None]
    sender = jnp.sum(jnp.where(chosen, (earlier // neighbours).astype(jnp.int32)[None, :], 0), axis=1)
    last_rows = queries.reshape(sequences, SEQ, columns)[:, SEQ - 1]
    odd_query = jnp.take(last_rows, sender, axis=0, mode="clip").reshape(shards, capacity, columns)
    odd_query, _ = lax.optimization_barrier((odd_query, first))
    odd_query = lax.all_to_all(odd_query, "db", 0, 0, tiled=True)
    odd_query = odd_query.reshape(shards * capacity, columns)

    part_index = lax.axis_index("mp")

    def share(half, after):
        half, _ = lax.optimization_barrier((half, after))
        shared = [half]
        for k in range(1, parts):
            shared.append(lax.ppermute(half, "mp", [(m, (m + k) % parts) for m in range(parts)]))
        return shared

    late_shared = share(late_half, table)
    second = [
        lax.dynamic_index_in_dim(
            half.reshape(group, parts, held, piece, width), part_index, 1, keepdims=False
        )
        for half in late_shared
    ]
    second = jnp.concatenate(second, axis=1).reshape(group * shard_rows, piece, width)
    part_groups = [
        [a * lanes + g * parts + m for g in range(group)] for a in range(planes) for m in range(parts)
    ]
    second, _ = lax.optimization_barrier((second, odd_query))
    if group > 1:
        second = swap(second, part_groups)
    early_shared = share(early_half, late_shared)
    plane_pieces = [first, second]

    def stepped(row):
        step = (part_index + parts - row % shard_rows // held) % parts
        return row // shard_rows * shard_rows + step * held + row % held

    even_id = (table_shard[:, :, 0] * shard_rows + table_row[:, :, 0]).reshape(planes, group * wanted)
    ids = jnp.arange(planes * plane_rows, dtype=jnp.int32)
    want = jnp.any(even_id[:, :, None] == ids[None, None, :], axis=1).reshape(planes, planes, plane_rows)
    below = jnp.arange(plane_rows)
    before = (below[:, None] < below[None, :]).astype(BF16)
    rank = jnp.dot(want.astype(BF16), before, preferred_element_type=F32).astype(jnp.int32)
    loads = jnp.sum(want.astype(jnp.int32), axis=2)
    if planes <= MOST_SHIFTS:
        loads = jnp.where(jnp.eye(planes, dtype=jnp.bool_), 0, loads)
    fits = jnp.max(loads) <= fast
    mine_want = lax.dynamic_index_in_dim(want, plane_index, 1, keepdims=False)
    mine_rank = lax.dynamic_index_in_dim(rank, plane_index, 1, keepdims=False)
    picks = mine_want[:, None, :] & (
        mine_rank[:, None, :] == jnp.arange(fast, dtype=jnp.int32)[None, :, None]
    )
    send_rows = jnp.sum(jnp.where(picks, below[None, None, :].astype(jnp.int32), 0), axis=2)
    steps = jnp.arange(planes, dtype=jnp.int32)
    upward = (plane_index + steps) % planes
    send_rows = jnp.sum(
        jnp.where(upward[:, None, None] == steps[None, :, None], send_rows[None], 0), axis=1
    )
    my_ids = lax.dynamic_index_in_dim(even_id, plane_index, 0, keepdims=False)
    my_rank = lax.dynamic_index_in_dim(rank, plane_index, 0, keepdims=False).reshape(-1)
    place = jnp.sum(jnp.where(my_ids[:, None] == ids[None, :], my_rank[None, :], 0), axis=1)
    my_step = (plane_index + planes - my_ids // plane_rows) % planes

    def exact(source, chunk):
        rows = stepped(send_rows) if chunk else send_rows
        if planes > MOST_SHIFTS:
            return [jnp.take(source, rows[k], axis=0, mode="clip") for k in range(planes)]
        return [source, *select_rows(rows[1:], source)]

    def whole(source, chunk):
        return [source] * planes

    def exchange(sources, select, index):
        received, arrived = [], []
        for chunk, source in enumerate(sources):
            sending = select(source, chunk)
            if received:
                sending, _ = lax.optimization_barrier((sending, received[-1]))
            received.append(across(sending))
            outgoing = gather_rows(index[chunk], received[-1], group, parts)
            outgoing, _ = lax.optimization_barrier((outgoing, arrived[-1] if arrived else odd_query))
            arrived.append(swap(outgoing, plane_groups))
        return [a.reshape(lanes, wanted, piece, width) for a in arrived]

    odd_part = jnp.zeros((shards * capacity, columns + DH), F32)
    for k in range(parts):
        slot_want = slot_row - (part_index + parts - k) % parts * held
        slot_want = jnp.broadcast_to(slot_want.reshape(-1, 1), (shards * capacity, DH))
        odd_part = odd_attention(
            odd_query, slot_want, (early_shared[k], late_shared[k]), weights, odd_part
        )

    def attend(select, index):
        *early, late = exchange(plane_pieces, select, index)
        early = [project(e, weights) for e in early]
        return even_attention(queries, late, weights, early), late

    own_rows = [my_ids % plane_rows, stepped(my_ids % plane_rows)]
    fast_index = my_step * fast + jnp.minimum(place, fast - 1)
    fast_index = [fast_index] * CHUNKS
    if planes <= MOST_SHIFTS:
        fast_index = [
            jnp.where(my_step == 0, row, index + plane_rows - fast) for row, index in zip(own_rows, fast_index)
        ]
    result, last = attend(exact, fast_index)
    odd_part, _ = lax.optimization_barrier((odd_part, last))
    odd_part = lax.all_to_all(odd_part.reshape(shards, capacity, columns + DH), "db", 0, 0, tiled=True)
    odd_part = odd_part.reshape(shards * capacity, columns + DH)
    if fast < most:
        result, odd_part = lax.optimization_barrier((result, odd_part))
        result = lax.cond(
            fits,
            lambda done: done,
            lambda done: attend(whole, [my_step * plane_rows + row for row in own_rows])[0],
            result,
        )
    return patch(my_slot, result, odd_part)


def solution(mesh):
    placed = (
        P("db", "mp"),
        P(("db", "mp"), None, None),
        P("db", "mp"),
        P("db", "mp"),
        P("db", None),
        P("db", None),
    )

    return jax.shard_map(local, mesh=mesh, in_specs=placed, out_specs=P("db", "mp"), check_vma=False)
```

```python
import functools
import math

import jax
import jax.numpy as jnp
from jax import lax
from jax.experimental import pallas as pl
from jax.experimental.pallas import tpu as pltpu
from jax.sharding import PartitionSpec as P


DH = 128
SPAN = 64
SEQ = 128
LANES = 8
CHUNKS = 2
MOST_SHIFTS = 8
LOW = (SPAN - 1) // 16 * 16
FAST_SLOTS = 46
BF16 = jnp.bfloat16
F32 = jnp.float32
SCALE = 1.0 / math.sqrt(DH)
BOTH = ("db", "mp")
CONTRACT_LAST = (((1,), (1,)), ((), ()))


def project_rows(rows_ref, weight_ref):
    lanes, count, piece, width = rows_ref.shape
    rows = rows_ref[...]
    stacked = jnp.concatenate([rows[:, j].reshape(lanes * piece, width) for j in range(count)], axis=0)
    return jnp.dot(stacked, weight_ref[...], preferred_element_type=F32).astype(BF16)


def attend_head(query, keys, values):
    scores = lax.dot_general(query, keys, CONTRACT_LAST, preferred_element_type=F32) * SCALE
    largest = jnp.max(scores, axis=1, keepdims=True)
    expscore = jnp.exp(scores - largest)
    total = jnp.sum(expscore, axis=1, keepdims=True)
    return jnp.dot(expscore.astype(BF16), values, preferred_element_type=F32), largest, total


def early_body(query_ref, rows_ref, weight_ref, mixed_ref, stats_ref, *, per_step):
    columns = query_ref.shape[1]
    projected = project_rows(rows_ref, weight_ref)
    span = projected.shape[0] // per_step
    lane = lax.broadcasted_iota(jnp.int32, (SEQ - LOW, DH), 1)
    for s in range(per_step):
        own = projected[s * span : (s + 1) * span]
        at = slice(s * (SEQ - LOW), (s + 1) * (SEQ - LOW))
        stats = jnp.zeros((SEQ - LOW, DH), F32)
        for h in range(columns // DH):
            lo, hi = h * DH, (h + 1) * DH
            query = query_ref[s * SEQ + LOW : (s + 1) * SEQ, lo:hi]
            mixed, largest, total = attend_head(query, own[:, lo:hi], own[:, columns + lo : columns + hi])
            mixed_ref[at, lo:hi] = mixed
            stats = jnp.where(lane == h, largest, stats)
            stats = jnp.where(lane == DH // 2 + h, total, stats)
        stats_ref[at, :] = stats


def late_body(query_ref, rows_ref, weight_ref, mixed_ref, stats_ref, odd_ref, out_ref, *, per_step):
    columns = query_ref.shape[1]
    projected = project_rows(rows_ref, weight_ref)
    span = projected.shape[0] // per_step
    first = SPAN - 1
    position = LOW + lax.broadcasted_iota(jnp.int32, (SEQ - LOW, DH), 0)
    for s in range(per_step):
        own = projected[s * span : (s + 1) * span]
        at = slice(s * (SEQ - LOW), (s + 1) * (SEQ - LOW))
        stats = stats_ref[at, :]
        odd = odd_ref[pl.ds(pl.program_id(0) * per_step + s, 1), :]
        out_ref[s * SEQ : s * SEQ + LOW, :] = jnp.zeros((LOW, columns), BF16)
        for h in range(columns // DH):
            lo, hi = h * DH, (h + 1) * DH
            query = query_ref[s * SEQ + LOW : (s + 1) * SEQ, lo:hi]
            mixed, largest, total = attend_head(query, own[:, lo:hi], own[:, columns + lo : columns + hi])
            before = stats[:, h : h + 1]
            top = jnp.maximum(largest, before)
            here, there = jnp.exp(largest - top), jnp.exp(before - top)
            under = total * here + stats[:, DH // 2 + h : DH // 2 + h + 1] * there
            attended = mixed * (here / under) + mixed_ref[at, lo:hi] * (there / under)
            attended = jnp.where(position == SEQ - 1, odd[:, lo:hi], attended)
            attended = jnp.where(position < first, 0.0, attended)
            out_ref[s * SEQ + LOW : (s + 1) * SEQ, lo:hi] = attended.astype(BF16)


def even_specs(queries, rows, weights):
    columns = queries.shape[1]
    sequences = queries.shape[0] // SEQ
    lanes, count, piece, width = rows.shape
    per_step = math.gcd(sequences, 2)
    specs = [
        pl.BlockSpec((per_step * SEQ, columns), lambda i: (i, 0)),
        pl.BlockSpec((lanes, per_step * count // sequences, piece, width), lambda i: (0, i, 0, 0)),
        pl.BlockSpec(weights.shape, lambda i: (0, 0)),
    ]
    halves = [
        pl.BlockSpec((per_step * (SEQ - LOW), columns), lambda i: (i, 0)),
        pl.BlockSpec((per_step * (SEQ - LOW), DH), lambda i: (i, 0)),
    ]
    return sequences, per_step, specs, halves


def early_attention(queries, rows, weights):
    sequences, per_step, specs, halves = even_specs(queries, rows, weights)
    return pl.pallas_call(
        functools.partial(early_body, per_step=per_step),
        out_shape=[
            jax.ShapeDtypeStruct((sequences * (SEQ - LOW), width), F32) for width in (queries.shape[1], DH)
        ],
        grid=(sequences // per_step,),
        in_specs=specs,
        out_specs=halves,
        name="early_attention",
    )(queries, rows, weights)


def late_attention(queries, rows, weights, mixed, stats, odd):
    sequences, per_step, specs, halves = even_specs(queries, rows, weights)
    return pl.pallas_call(
        functools.partial(late_body, per_step=per_step),
        out_shape=jax.ShapeDtypeStruct(queries.shape, BF16),
        grid=(sequences // per_step,),
        in_specs=[*specs, *halves, pl.BlockSpec(odd.shape, lambda i: (0, 0))],
        out_specs=specs[0],
        name="late_attention",
    )(queries, rows, weights, mixed, stats, odd)


def combine_body(slot_ref, odd_ref, row_ref, *picked_refs):
    sequences, columns = row_ref.shape
    for i in range(sequences):
        for j, picked_ref in enumerate(picked_refs):
            picked_ref[i : i + 1, :] = odd_ref[pl.ds(slot_ref[i * len(picked_refs) + j], 1), :]
    for h in range(columns // DH):
        lo, hi = h * DH, (h + 1) * DH
        maxima = [p[:, columns + h : columns + h + 1] for p in picked_refs]
        sums = [p[:, columns + DH // 2 + h : columns + DH // 2 + h + 1] for p in picked_refs]
        top = functools.reduce(jnp.maximum, maxima)
        each = [jnp.exp(m - top) for m in maxima]
        under = sum(e * t for e, t in zip(each, sums))
        over = sum(e * p[:, lo:hi] for e, p in zip(each, picked_refs))
        row_ref[:, lo:hi] = over / under


def combine(slots, odd, sequences):
    columns = odd.shape[1] - DH
    return pl.pallas_call(
        combine_body,
        out_shape=jax.ShapeDtypeStruct((sequences, columns), F32),
        grid_spec=pltpu.PrefetchScalarGridSpec(
            num_scalar_prefetch=1,
            grid=(1,),
            in_specs=[pl.BlockSpec(odd.shape, lambda i, s: (0, 0))],
            out_specs=pl.BlockSpec((sequences, columns), lambda i, s: (0, 0)),
            scratch_shapes=[pltpu.VMEM((sequences, odd.shape[1]), F32)] * (slots.shape[0] // sequences),
        ),
        name="combine",
    )(slots, odd)


def gather_body(index_ref, *refs, count):
    sources, out_ref, stage_ref, sem_ref = refs[:count], refs[count], refs[count + 1], refs[count + 2]
    copies, wanted = out_ref.shape[1:3]
    starts = [sum(s.shape[0] for s in sources[:k]) for k in range(count)]
    base = pl.program_id(0) * wanted

    @pl.when(pl.program_id(0) == 0)
    def _():
        moves = [
            pltpu.make_async_copy(source, stage_ref.at[pl.ds(starts[k], source.shape[0])], sem_ref.at[k])
            for k, source in enumerate(sources)
        ]
        for move in moves:
            move.start()
        for move in moves:
            move.wait()

    def step(i, carry):
        row = stage_ref[index_ref[base + i]]
        for c in range(copies):
            out_ref[0, c, i] = row
        return carry

    lax.fori_loop(0, wanted, step, 0, unroll=8)


def gather_rows(index, sources, groups, copies):
    wanted = index.shape[0] // groups
    piece, width = sources[0].shape[1:]
    out = pl.pallas_call(
        functools.partial(gather_body, count=len(sources)),
        out_shape=jax.ShapeDtypeStruct((groups, copies, wanted, piece, width), sources[0].dtype),
        grid_spec=pltpu.PrefetchScalarGridSpec(
            num_scalar_prefetch=1,
            grid=(groups,),
            in_specs=[pl.BlockSpec(memory_space=pl.ANY) for _ in sources],
            out_specs=pl.BlockSpec((1, copies, wanted, piece, width), lambda i, s: (i, 0, 0, 0, 0)),
            scratch_shapes=[
                pltpu.VMEM((sum(s.shape[0] for s in sources), piece, width), sources[0].dtype),
                pltpu.SemaphoreType.DMA((len(sources),)),
            ],
        ),
        name="gather_rows",
    )(index, *sources)
    return out.reshape(groups * copies * wanted, piece, width)


def select_body(index_ref, source_ref, *out_refs):
    fast = out_refs[0].shape[0]

    def step(i, carry):
        for k, out_ref in enumerate(out_refs):
            out_ref[i] = source_ref[index_ref[k * fast + i]]
        return carry

    lax.fori_loop(0, fast, step, 0, unroll=2)


def select_rows(index, source):
    count, fast = index.shape
    block = pl.BlockSpec((fast,) + source.shape[1:], lambda i, s: (0, 0, 0))
    return pl.pallas_call(
        select_body,
        out_shape=[jax.ShapeDtypeStruct((fast,) + source.shape[1:], source.dtype)] * count,
        grid_spec=pltpu.PrefetchScalarGridSpec(
            num_scalar_prefetch=1,
            grid=(1,),
            in_specs=[pl.BlockSpec(source.shape, lambda i, s: (0, 0, 0))],
            out_specs=[block] * count,
        ),
        name="select_rows",
    )(index.reshape(-1), source)


def odd_body(query_ref, want_ref, *refs):
    rows_refs, (weight_ref, prior_ref, out_ref) = refs[:-3], refs[-3:]
    columns = query_ref.shape[1]
    heads = columns // DH
    lanes, per_step, piece, width = rows_refs[0].shape
    tokens = len(rows_refs) * lanes * piece
    step = pl.program_id(0)

    @pl.when(step == 0)
    def _():
        out_ref[...] = prior_ref[...]

    pieces = [ref[...] for ref in rows_refs]
    stacked = jnp.concatenate(
        [p[:, r].reshape(lanes * piece, width) for r in range(per_step) for p in pieces], axis=0
    )
    projected = jnp.dot(stacked, weight_ref[...], preferred_element_type=F32).astype(BF16)
    want = want_ref[...] - step * per_step
    here = [want == r for r in range(per_step)]
    inside = (want >= 0) & (want < per_step)
    lane = lax.broadcasted_iota(jnp.int32, (want.shape[0], DH), 1)
    stats = out_ref[:, columns:]
    for h in range(heads):
        lo, hi = h * DH, (h + 1) * DH
        scores = (
            lax.dot_general(
                query_ref[:, lo:hi], projected[:, lo:hi], CONTRACT_LAST, preferred_element_type=F32
            )
            * SCALE
        )
        mine = jnp.zeros((want.shape[0], tokens), F32)
        for r in range(per_step):
            mine = jnp.where(here[r], scores[:, r * tokens : (r + 1) * tokens], mine)
        largest = jnp.max(mine, axis=1, keepdims=True)
        expscore = jnp.exp(mine - largest)
        total = jnp.sum(expscore, axis=1, keepdims=True)
        spread = jnp.concatenate([jnp.where(here[r], expscore, 0.0) for r in range(per_step)], axis=1)
        mixed = jnp.dot(spread.astype(BF16), projected[:, columns + lo : columns + hi], preferred_element_type=F32)
        out_ref[:, lo:hi] = jnp.where(inside, mixed, out_ref[:, lo:hi])
        stats = jnp.where(inside & (lane == h), largest, stats)
        stats = jnp.where(inside & (lane == DH // 2 + h), total, stats)
    out_ref[:, columns:] = stats


def odd_attention(queries, want, rows, weights, prior):
    slots, columns = queries.shape
    lanes, count, piece, width = rows[0].shape
    per_step = math.gcd(count, 4)
    row_spec = pl.BlockSpec((lanes, per_step, piece, width), lambda i: (0, i, 0, 0))
    return pl.pallas_call(
        odd_body,
        out_shape=jax.ShapeDtypeStruct(prior.shape, F32),
        grid=(count // per_step,),
        in_specs=[
            pl.BlockSpec((slots, columns), lambda i: (0, 0)),
            pl.BlockSpec((slots, DH), lambda i: (0, 0)),
            *[row_spec for _ in rows],
            pl.BlockSpec(weights.shape, lambda i: (0, 0)),
            pl.BlockSpec(prior.shape, lambda i: (0, 0)),
        ],
        out_specs=pl.BlockSpec(prior.shape, lambda i: (0, 0)),
        name="odd_attention",
    )(queries, want, *rows, weights, prior)


def local(queries, encodings, key_weight, value_weight, nbr_shard, nbr_row):
    shards = lax.axis_size("db")
    parts = lax.axis_size("mp")
    group = max(1, LANES // parts)
    lanes = group * parts
    planes = shards // group
    columns = queries.shape[1]
    held, tokens, width = encodings.shape
    piece = tokens // (lanes * CHUNKS)
    shard_rows = held * parts
    plane_rows = group * shard_rows
    span_count, neighbours = nbr_shard.shape
    sequences = queries.shape[0] // SEQ
    wanted = sequences * neighbours
    capacity = max(2, 4 * span_count // shards)
    most = min(plane_rows, group * wanted, group * group * capacity)
    fast = min(most, FAST_SLOTS)
    plane_groups = [[a * lanes + b for b in range(lanes)] for a in range(planes)]
    lane_groups = [[a * lanes + b for a in range(planes)] for b in range(lanes)]
    db_index = lax.axis_index("db")
    plane_index = db_index // group

    def swap(x, groups):
        return lax.all_to_all(x, BOTH, 0, 0, axis_index_groups=groups, tiled=True)

    def across(blocks):
        if planes > MOST_SHIFTS:
            stacked = jnp.stack(blocks)
            ordered = jnp.take(stacked, (jnp.arange(planes) - plane_index) % planes, axis=0, mode="clip")
            ordered = swap(ordered.reshape((-1,) + stacked.shape[2:]), lane_groups).reshape(stacked.shape)
            moved = jnp.take(ordered, (plane_index - jnp.arange(planes)) % planes, axis=0, mode="clip")
            return [moved.reshape((-1,) + stacked.shape[2:])]
        moved = [blocks[0]]
        for k in range(1, planes):
            pairs = [
                (a * lanes + b, (a + k) % planes * lanes + b) for a in range(planes) for b in range(lanes)
            ]
            moved.append(lax.ppermute(blocks[k], BOTH, pairs))
        return moved

    table = jnp.concatenate([nbr_shard.reshape(-1), nbr_row.reshape(-1)])
    table = jnp.broadcast_to(table[None, None], (shards, 1, table.shape[0]))
    table = lax.all_to_all(table, "db", 0, 0, tiled=True).reshape(
        shards, 2, sequences, SEQ // SPAN, neighbours
    )
    table_shard, table_row = table[:, 0], table[:, 1]

    weights = lax.all_gather(
        jnp.concatenate([key_weight, value_weight], axis=1), "db", axis=0, tiled=True
    )

    early_half, late_half = jnp.transpose(encodings.reshape(held, lanes, CHUNKS, piece, width), (2, 1, 0, 3, 4))
    first, _ = lax.optimization_barrier((early_half.reshape(lanes * held, piece, width), table))
    first = swap(first, plane_groups)

    odd_shard = table_shard[:, :, 1].reshape(shards, wanted)
    odd_row = table_row[:, :, 1].reshape(shards, wanted)
    earlier = jnp.arange(wanted)
    same = (odd_shard[:, :, None] == odd_shard[:, None, :]) & (earlier[None, None, :] < earlier[None, :, None])
    odd_rank = jnp.sum(same.astype(jnp.int32), axis=2)
    arriving = (odd_shard == db_index)[:, None, :] & (
        odd_rank[:, None, :] == jnp.arange(capacity, dtype=jnp.int32)[None, :, None]
    )
    slot_row = jnp.sum(jnp.where(arriving, odd_row[:, None, :] + 1, 0), axis=2) - 1
    my_slot = lax.dynamic_index_in_dim(odd_shard * capacity + odd_rank, db_index, 0, keepdims=False)
    slots = jnp.arange(shards * capacity, dtype=jnp.int32)
    chosen = my_slot[None, :] == slots[:, None]
    sender = jnp.sum(jnp.where(chosen, (earlier // neighbours).astype(jnp.int32)[None, :], 0), axis=1)
    last_rows = queries.reshape(sequences, SEQ, columns)[:, SEQ - 1]
    odd_query = jnp.take(last_rows, sender, axis=0, mode="clip").reshape(shards, capacity, columns)
    odd_query, _ = lax.optimization_barrier((odd_query, first))
    odd_query = lax.all_to_all(odd_query, "db", 0, 0, tiled=True)
    odd_query = odd_query.reshape(shards * capacity, columns)

    part_index = lax.axis_index("mp")

    def share(half, after):
        half, _ = lax.optimization_barrier((half, after))
        shared = [half]
        for k in range(1, parts):
            shared.append(lax.ppermute(half, "mp", [(m, (m + k) % parts) for m in range(parts)]))
        return shared

    late_shared = share(late_half, table)
    second = [
        lax.dynamic_index_in_dim(
            half.reshape(group, parts, held, piece, width), part_index, 1, keepdims=False
        )
        for half in late_shared
    ]
    second = jnp.concatenate(second, axis=1).reshape(group * shard_rows, piece, width)
    part_groups = [
        [a * lanes + g * parts + m for g in range(group)] for a in range(planes) for m in range(parts)
    ]
    second, _ = lax.optimization_barrier((second, odd_query))
    if group > 1:
        second = swap(second, part_groups)
    early_shared = share(early_half, late_shared)
    plane_pieces = [first, second]

    def stepped(row):
        step = (part_index + parts - row % shard_rows // held) % parts
        return row // shard_rows * shard_rows + step * held + row % held

    even_id = (table_shard[:, :, 0] * shard_rows + table_row[:, :, 0]).reshape(planes, group * wanted)
    ids = jnp.arange(planes * plane_rows, dtype=jnp.int32)
    want = jnp.any(even_id[:, :, None] == ids[None, None, :], axis=1).reshape(planes, planes, plane_rows)
    below = jnp.arange(plane_rows)
    before = (below[:, None] < below[None, :]).astype(BF16)
    rank = jnp.dot(want.astype(BF16), before, preferred_element_type=F32).astype(jnp.int32)
    loads = jnp.sum(want.astype(jnp.int32), axis=2)
    if planes <= MOST_SHIFTS:
        loads = jnp.where(jnp.eye(planes, dtype=jnp.bool_), 0, loads)
    fits = jnp.max(loads) <= fast
    mine_want = lax.dynamic_index_in_dim(want, plane_index, 1, keepdims=False)
    mine_rank = lax.dynamic_index_in_dim(rank, plane_index, 1, keepdims=False)
    picks = mine_want[:, None, :] & (
        mine_rank[:, None, :] == jnp.arange(fast, dtype=jnp.int32)[None, :, None]
    )
    send_rows = jnp.sum(jnp.where(picks, below[None, None, :].astype(jnp.int32), 0), axis=2)
    steps = jnp.arange(planes, dtype=jnp.int32)
    upward = (plane_index + steps) % planes
    send_rows = jnp.sum(
        jnp.where(upward[:, None, None] == steps[None, :, None], send_rows[None], 0), axis=1
    )
    my_ids = lax.dynamic_index_in_dim(even_id, plane_index, 0, keepdims=False)
    my_rank = lax.dynamic_index_in_dim(rank, plane_index, 0, keepdims=False).reshape(-1)
    place = jnp.sum(jnp.where(my_ids[:, None] == ids[None, :], my_rank[None, :], 0), axis=1)
    my_step = (plane_index + planes - my_ids // plane_rows) % planes

    def exact(source, chunk):
        rows = stepped(send_rows) if chunk else send_rows
        if planes > MOST_SHIFTS:
            return [jnp.take(source, rows[k], axis=0, mode="clip") for k in range(planes)]
        return [source, *select_rows(rows[1:], source)]

    def whole(source, chunk):
        return [source] * planes

    def exchange(sources, select, index, between):
        received, arrived = [], []
        for chunk, source in enumerate(sources):
            sending = select(source, chunk)
            if received:
                sending, _ = lax.optimization_barrier((sending, received[-1]))
            received.append(across(sending))
            outgoing = gather_rows(index[chunk], received[-1], group, parts)
            outgoing, _ = lax.optimization_barrier((outgoing, after if arrived else odd_query))
            arrived.append(swap(outgoing, plane_groups))
            after = arrived[-1] if chunk else between(arrived[-1])
        return [a.reshape(lanes, wanted, piece, width) for a in arrived]

    odd_part = jnp.zeros((shards * capacity, columns + DH), F32)
    for k in range(parts):
        slot_want = slot_row - (part_index + parts - k) % parts * held
        slot_want = jnp.broadcast_to(slot_want.reshape(-1, 1), (shards * capacity, DH))
        odd_part = odd_attention(
            odd_query, slot_want, (early_shared[k], late_shared[k]), weights, odd_part
        )

    returned = []

    def send_back(after):
        part, _ = lax.optimization_barrier((odd_part, after))
        part = lax.all_to_all(part.reshape(shards, capacity, columns + DH), "db", 0, 0, tiled=True)
        returned.append(part)
        return part

    def attend(select, index, between, odd_rows):
        early, late = exchange(plane_pieces, select, index, between)
        early = early_attention(queries, early, weights)
        return late_attention(queries, late, weights, *early, odd_rows())

    def odd_rows():
        return combine(my_slot, returned[0].reshape(shards * capacity, columns + DH), sequences)

    own_rows = [my_ids % plane_rows, stepped(my_ids % plane_rows)]
    fast_index = my_step * fast + jnp.minimum(place, fast - 1)
    fast_index = [fast_index] * CHUNKS
    if planes <= MOST_SHIFTS:
        fast_index = [
            jnp.where(my_step == 0, row, index + plane_rows - fast) for row, index in zip(own_rows, fast_index)
        ]
    result = attend(exact, fast_index, send_back, odd_rows)
    if fast < most:
        result = lax.cond(
            fits,
            lambda done: done,
            lambda done: attend(
                whole, [my_step * plane_rows + row for row in own_rows], lambda arrived: arrived, odd_rows
            ),
            result,
        )
    return result


def solution(mesh):
    placed = (
        P("db", "mp"),
        P(("db", "mp"), None, None),
        P("db", "mp"),
        P("db", "mp"),
        P("db", None),
        P("db", None),
    )

    return jax.shard_map(local, mesh=mesh, in_specs=placed, out_specs=P("db", "mp"), check_vma=False)
```

```python
import functools
import math

import jax
import jax.numpy as jnp
from jax import lax
from jax.experimental import pallas as pl
from jax.experimental.pallas import tpu as pltpu
from jax.sharding import PartitionSpec as P


DH = 128
SPAN = 64
SEQ = 128
LANES = 8
CHUNKS = 2
MOST_SHIFTS = 8
LOW = (SPAN - 1) // 16 * 16
FAST_SLOTS = 46
BF16 = jnp.bfloat16
F32 = jnp.float32
SCALE = 1.0 / math.sqrt(DH)
BOTH = ("db", "mp")
CONTRACT_LAST = (((1,), (1,)), ((), ()))


def project_rows(rows_ref, weight_ref):
    lanes, count, piece, width = rows_ref.shape
    rows = rows_ref[...]
    stacked = jnp.concatenate([rows[:, j].reshape(lanes * piece, width) for j in range(count)], axis=0)
    return jnp.dot(stacked, weight_ref[...], preferred_element_type=F32).astype(BF16)


def project_body(rows_ref, weight_ref, out_ref):
    out_ref[...] = project_rows(rows_ref, weight_ref)


def project(rows, weights):
    lanes, count, piece, width = rows.shape
    per_step = math.gcd(count, 8)
    tokens = lanes * piece
    return pl.pallas_call(
        project_body,
        out_shape=jax.ShapeDtypeStruct((count * tokens, weights.shape[1]), BF16),
        grid=(count // per_step,),
        in_specs=[
            pl.BlockSpec((lanes, per_step, piece, width), lambda i: (0, i, 0, 0)),
            pl.BlockSpec(weights.shape, lambda i: (0, 0)),
        ],
        out_specs=pl.BlockSpec((per_step * tokens, weights.shape[1]), lambda i: (i, 0)),
        name="project",
    )(rows, weights)


def even_body(query_ref, rows_ref, weight_ref, early_ref, odd_ref, out_ref, *, per_step):
    columns = query_ref.shape[1]
    late = project_rows(rows_ref, weight_ref)
    span = late.shape[0] // per_step
    first = SPAN - 1
    position = LOW + lax.broadcasted_iota(jnp.int32, (SEQ - LOW, DH), 0)
    odd = [odd_ref[pl.ds(pl.program_id(0) * per_step + s, 1), :] for s in range(per_step)]
    blocks = [(s, h * DH) for s in range(per_step) for h in range(columns // DH)]

    def both(s, lo):
        at = slice(s * span, (s + 1) * span)
        return jnp.concatenate([early_ref[at, lo : lo + DH], late[at, lo : lo + DH]], axis=0)

    scores = [
        lax.dot_general(
            query_ref[s * SEQ + LOW : (s + 1) * SEQ, lo : lo + DH],
            both(s, lo),
            CONTRACT_LAST,
            preferred_element_type=F32,
        )
        * SCALE
        for s, lo in blocks
    ]
    largest = [jnp.max(x, axis=1, keepdims=True) for x in scores]
    expscore = [jnp.exp(x - m) for x, m in zip(scores, largest)]
    total = [jnp.sum(e, axis=1, keepdims=True) for e in expscore]
    mixed = [
        jnp.dot(e.astype(BF16), both(s, columns + lo), preferred_element_type=F32)
        for e, (s, lo) in zip(expscore, blocks)
    ]
    for s in range(per_step):
        out_ref[s * SEQ : s * SEQ + LOW, :] = jnp.zeros((LOW, columns), BF16)
    for (s, lo), over, under in zip(blocks, mixed, total):
        attended = over * (1.0 / under)
        attended = jnp.where(position == SEQ - 1, odd[s][:, lo : lo + DH], attended)
        attended = jnp.where(position < first, 0.0, attended)
        out_ref[s * SEQ + LOW : (s + 1) * SEQ, lo : lo + DH] = attended.astype(BF16)


def even_attention(queries, rows, weights, early, odd):
    columns = queries.shape[1]
    sequences = queries.shape[0] // SEQ
    lanes, count, piece, width = rows.shape
    per_step = math.gcd(sequences, 2)
    rows_step = per_step * count // sequences
    query_spec = pl.BlockSpec((per_step * SEQ, columns), lambda i: (i, 0))
    return pl.pallas_call(
        functools.partial(even_body, per_step=per_step),
        out_shape=jax.ShapeDtypeStruct(queries.shape, BF16),
        grid=(sequences // per_step,),
        in_specs=[
            query_spec,
            pl.BlockSpec((lanes, rows_step, piece, width), lambda i: (0, i, 0, 0)),
            pl.BlockSpec(weights.shape, lambda i: (0, 0)),
            pl.BlockSpec((rows_step * lanes * piece, weights.shape[1]), lambda i: (i, 0)),
            pl.BlockSpec(odd.shape, lambda i: (0, 0)),
        ],
        out_specs=query_spec,
        name="even_attention",
    )(queries, rows, weights, early, odd)


def combine_body(slot_ref, odd_ref, row_ref, *picked_refs):
    sequences, columns = row_ref.shape
    for i in range(sequences):
        for j, picked_ref in enumerate(picked_refs):
            picked_ref[i : i + 1, :] = odd_ref[pl.ds(slot_ref[i * len(picked_refs) + j], 1), :]
    for h in range(columns // DH):
        lo, hi = h * DH, (h + 1) * DH
        maxima = [p[:, columns + h : columns + h + 1] for p in picked_refs]
        sums = [p[:, columns + DH // 2 + h : columns + DH // 2 + h + 1] for p in picked_refs]
        top = functools.reduce(jnp.maximum, maxima)
        each = [jnp.exp(m - top) for m in maxima]
        under = sum(e * t for e, t in zip(each, sums))
        over = sum(e * p[:, lo:hi] for e, p in zip(each, picked_refs))
        row_ref[:, lo:hi] = over / under


def combine(slots, odd, sequences):
    columns = odd.shape[1] - DH
    return pl.pallas_call(
        combine_body,
        out_shape=jax.ShapeDtypeStruct((sequences, columns), F32),
        grid_spec=pltpu.PrefetchScalarGridSpec(
            num_scalar_prefetch=1,
            grid=(1,),
            in_specs=[pl.BlockSpec(odd.shape, lambda i, s: (0, 0))],
            out_specs=pl.BlockSpec((sequences, columns), lambda i, s: (0, 0)),
            scratch_shapes=[pltpu.VMEM((sequences, odd.shape[1]), F32)] * (slots.shape[0] // sequences),
        ),
        name="combine",
    )(slots, odd)


def gather_body(index_ref, *refs, count):
    sources, out_ref, stage_ref, sem_ref = refs[:count], refs[count], refs[count + 1], refs[count + 2]
    copies, wanted = out_ref.shape[1:3]
    starts = [sum(s.shape[0] for s in sources[:k]) for k in range(count)]
    base = pl.program_id(0) * wanted

    @pl.when(pl.program_id(0) == 0)
    def _():
        moves = [
            pltpu.make_async_copy(source, stage_ref.at[pl.ds(starts[k], source.shape[0])], sem_ref.at[k])
            for k, source in enumerate(sources)
        ]
        for move in moves:
            move.start()
        for move in moves:
            move.wait()

    def step(i, carry):
        row = stage_ref[index_ref[base + i]]
        for c in range(copies):
            out_ref[0, c, i] = row
        return carry

    lax.fori_loop(0, wanted, step, 0, unroll=8)


def gather_rows(index, sources, groups, copies):
    wanted = index.shape[0] // groups
    piece, width = sources[0].shape[1:]
    out = pl.pallas_call(
        functools.partial(gather_body, count=len(sources)),
        out_shape=jax.ShapeDtypeStruct((groups, copies, wanted, piece, width), sources[0].dtype),
        grid_spec=pltpu.PrefetchScalarGridSpec(
            num_scalar_prefetch=1,
            grid=(groups,),
            in_specs=[pl.BlockSpec(memory_space=pl.ANY) for _ in sources],
            out_specs=pl.BlockSpec((1, copies, wanted, piece, width), lambda i, s: (i, 0, 0, 0, 0)),
            scratch_shapes=[
                pltpu.VMEM((sum(s.shape[0] for s in sources), piece, width), sources[0].dtype),
                pltpu.SemaphoreType.DMA((len(sources),)),
            ],
        ),
        name="gather_rows",
    )(index, *sources)
    return out.reshape(groups * copies * wanted, piece, width)


def select_body(index_ref, source_ref, *out_refs):
    fast = out_refs[0].shape[0]

    def step(i, carry):
        for k, out_ref in enumerate(out_refs):
            out_ref[i] = source_ref[index_ref[k * fast + i]]
        return carry

    lax.fori_loop(0, fast, step, 0, unroll=2)


def select_rows(index, source):
    count, fast = index.shape
    block = pl.BlockSpec((fast,) + source.shape[1:], lambda i, s: (0, 0, 0))
    return pl.pallas_call(
        select_body,
        out_shape=[jax.ShapeDtypeStruct((fast,) + source.shape[1:], source.dtype)] * count,
        grid_spec=pltpu.PrefetchScalarGridSpec(
            num_scalar_prefetch=1,
            grid=(1,),
            in_specs=[pl.BlockSpec(source.shape, lambda i, s: (0, 0, 0))],
            out_specs=[block] * count,
        ),
        name="select_rows",
    )(index.reshape(-1), source)


def odd_body(query_ref, want_ref, *refs):
    rows_refs, (weight_ref, prior_ref, out_ref) = refs[:-3], refs[-3:]
    columns = query_ref.shape[1]
    heads = columns // DH
    lanes, per_step, piece, width = rows_refs[0].shape
    tokens = len(rows_refs) * lanes * piece
    step = pl.program_id(0)

    @pl.when(step == 0)
    def _():
        out_ref[...] = prior_ref[...]

    pieces = [ref[...] for ref in rows_refs]
    stacked = jnp.concatenate(
        [p[:, r].reshape(lanes * piece, width) for r in range(per_step) for p in pieces], axis=0
    )
    projected = jnp.dot(stacked, weight_ref[...], preferred_element_type=F32).astype(BF16)
    want = want_ref[...] - step * per_step
    here = [want == r for r in range(per_step)]
    inside = (want >= 0) & (want < per_step)
    lane = lax.broadcasted_iota(jnp.int32, (want.shape[0], DH), 1)
    spans = [(h * DH, (h + 1) * DH) for h in range(heads)]
    scores = [
        lax.dot_general(
            query_ref[:, lo:hi], projected[:, lo:hi], CONTRACT_LAST, preferred_element_type=F32
        )
        * SCALE
        for lo, hi in spans
    ]
    mine = []
    for x in scores:
        chosen = jnp.zeros((want.shape[0], tokens), F32)
        for r in range(per_step):
            chosen = jnp.where(here[r], x[:, r * tokens : (r + 1) * tokens], chosen)
        mine.append(chosen)
    largest = [jnp.max(x, axis=1, keepdims=True) for x in mine]
    expscore = [jnp.exp(x - m) for x, m in zip(mine, largest)]
    total = [jnp.sum(e, axis=1, keepdims=True) for e in expscore]
    spread = [
        jnp.concatenate([jnp.where(here[r], e, 0.0) for r in range(per_step)], axis=1).astype(BF16)
        for e in expscore
    ]
    mixed = [
        jnp.dot(p, projected[:, columns + lo : columns + hi], preferred_element_type=F32)
        for p, (lo, hi) in zip(spread, spans)
    ]
    stats = out_ref[:, columns:]
    for h, (lo, hi) in enumerate(spans):
        out_ref[:, lo:hi] = jnp.where(inside, mixed[h], out_ref[:, lo:hi])
        stats = jnp.where(inside & (lane == h), largest[h], stats)
        stats = jnp.where(inside & (lane == DH // 2 + h), total[h], stats)
    out_ref[:, columns:] = stats


def odd_attention(queries, want, rows, weights, prior):
    slots, columns = queries.shape
    lanes, count, piece, width = rows[0].shape
    per_step = math.gcd(count, 4)
    row_spec = pl.BlockSpec((lanes, per_step, piece, width), lambda i: (0, i, 0, 0))
    return pl.pallas_call(
        odd_body,
        out_shape=jax.ShapeDtypeStruct(prior.shape, F32),
        grid=(count // per_step,),
        in_specs=[
            pl.BlockSpec((slots, columns), lambda i: (0, 0)),
            pl.BlockSpec((slots, DH), lambda i: (0, 0)),
            *[row_spec for _ in rows],
            pl.BlockSpec(weights.shape, lambda i: (0, 0)),
            pl.BlockSpec(prior.shape, lambda i: (0, 0)),
        ],
        out_specs=pl.BlockSpec(prior.shape, lambda i: (0, 0)),
        name="odd_attention",
    )(queries, want, *rows, weights, prior)


def local(queries, encodings, key_weight, value_weight, nbr_shard, nbr_row):
    shards = lax.axis_size("db")
    parts = lax.axis_size("mp")
    group = max(1, LANES // parts)
    lanes = group * parts
    planes = shards // group
    columns = queries.shape[1]
    held, tokens, width = encodings.shape
    piece = tokens // (lanes * CHUNKS)
    shard_rows = held * parts
    plane_rows = group * shard_rows
    span_count, neighbours = nbr_shard.shape
    sequences = queries.shape[0] // SEQ
    wanted = sequences * neighbours
    capacity = max(2, 4 * span_count // shards)
    most = min(plane_rows, group * wanted, group * group * capacity)
    fast = min(most, FAST_SLOTS)
    plane_groups = [[a * lanes + b for b in range(lanes)] for a in range(planes)]
    lane_groups = [[a * lanes + b for a in range(planes)] for b in range(lanes)]
    db_index = lax.axis_index("db")
    plane_index = db_index // group

    def swap(x, groups):
        return lax.all_to_all(x, BOTH, 0, 0, axis_index_groups=groups, tiled=True)

    def across(blocks):
        if planes > MOST_SHIFTS:
            stacked = jnp.stack(blocks)
            ordered = jnp.take(stacked, (jnp.arange(planes) - plane_index) % planes, axis=0, mode="clip")
            ordered = swap(ordered.reshape((-1,) + stacked.shape[2:]), lane_groups).reshape(stacked.shape)
            moved = jnp.take(ordered, (plane_index - jnp.arange(planes)) % planes, axis=0, mode="clip")
            return [moved.reshape((-1,) + stacked.shape[2:])]
        moved = [blocks[0]]
        for k in range(1, planes):
            pairs = [
                (a * lanes + b, (a + k) % planes * lanes + b) for a in range(planes) for b in range(lanes)
            ]
            moved.append(lax.ppermute(blocks[k], BOTH, pairs))
        return moved

    table = jnp.concatenate([nbr_shard.reshape(-1), nbr_row.reshape(-1)])
    table = jnp.broadcast_to(table[None, None], (shards, 1, table.shape[0]))
    table = lax.all_to_all(table, "db", 0, 0, tiled=True).reshape(
        shards, 2, sequences, SEQ // SPAN, neighbours
    )
    table_shard, table_row = table[:, 0], table[:, 1]

    weights = lax.all_gather(
        jnp.concatenate([key_weight, value_weight], axis=1), "db", axis=0, tiled=True
    )

    early_half, late_half = jnp.transpose(encodings.reshape(held, lanes, CHUNKS, piece, width), (2, 1, 0, 3, 4))
    first, _ = lax.optimization_barrier((early_half.reshape(lanes * held, piece, width), table))
    first = swap(first, plane_groups)

    odd_shard = table_shard[:, :, 1].reshape(shards, wanted)
    odd_row = table_row[:, :, 1].reshape(shards, wanted)
    earlier = jnp.arange(wanted)
    same = (odd_shard[:, :, None] == odd_shard[:, None, :]) & (earlier[None, None, :] < earlier[None, :, None])
    odd_rank = jnp.sum(same.astype(jnp.int32), axis=2)
    arriving = (odd_shard == db_index)[:, None, :] & (
        odd_rank[:, None, :] == jnp.arange(capacity, dtype=jnp.int32)[None, :, None]
    )
    slot_row = jnp.sum(jnp.where(arriving, odd_row[:, None, :] + 1, 0), axis=2) - 1
    my_slot = lax.dynamic_index_in_dim(odd_shard * capacity + odd_rank, db_index, 0, keepdims=False)
    slots = jnp.arange(shards * capacity, dtype=jnp.int32)
    chosen = my_slot[None, :] == slots[:, None]
    sender = jnp.sum(jnp.where(chosen, (earlier // neighbours).astype(jnp.int32)[None, :], 0), axis=1)
    last_rows = queries.reshape(sequences, SEQ, columns)[:, SEQ - 1]
    odd_query = jnp.take(last_rows, sender, axis=0, mode="clip").reshape(shards, capacity, columns)
    odd_query, _ = lax.optimization_barrier((odd_query, first))
    odd_query = lax.all_to_all(odd_query, "db", 0, 0, tiled=True)
    odd_query = odd_query.reshape(shards * capacity, columns)

    part_index = lax.axis_index("mp")

    def share(half, after):
        half, _ = lax.optimization_barrier((half, after))
        shared = [half]
        for k in range(1, parts):
            shared.append(lax.ppermute(half, "mp", [(m, (m + k) % parts) for m in range(parts)]))
        return shared

    late_shared = share(late_half, table)
    second = [
        lax.dynamic_index_in_dim(
            half.reshape(group, parts, held, piece, width), part_index, 1, keepdims=False
        )
        for half in late_shared
    ]
    second = jnp.concatenate(second, axis=1).reshape(group * shard_rows, piece, width)
    part_groups = [
        [a * lanes + g * parts + m for g in range(group)] for a in range(planes) for m in range(parts)
    ]
    second, _ = lax.optimization_barrier((second, odd_query))
    if group > 1:
        second = swap(second, part_groups)
    early_shared = share(early_half, late_shared)
    plane_pieces = [first, second]

    def stepped(row):
        step = (part_index + parts - row % shard_rows // held) % parts
        return row // shard_rows * shard_rows + step * held + row % held

    even_id = (table_shard[:, :, 0] * shard_rows + table_row[:, :, 0]).reshape(planes, group * wanted)
    ids = jnp.arange(planes * plane_rows, dtype=jnp.int32)
    want = jnp.any(even_id[:, :, None] == ids[None, None, :], axis=1).reshape(planes, planes, plane_rows)
    below = jnp.arange(plane_rows)
    before = (below[:, None] < below[None, :]).astype(BF16)
    rank = jnp.dot(want.astype(BF16), before, preferred_element_type=F32).astype(jnp.int32)
    loads = jnp.sum(want.astype(jnp.int32), axis=2)
    if planes <= MOST_SHIFTS:
        loads = jnp.where(jnp.eye(planes, dtype=jnp.bool_), 0, loads)
    fits = jnp.max(loads) <= fast
    mine_want = lax.dynamic_index_in_dim(want, plane_index, 1, keepdims=False)
    mine_rank = lax.dynamic_index_in_dim(rank, plane_index, 1, keepdims=False)
    picks = mine_want[:, None, :] & (
        mine_rank[:, None, :] == jnp.arange(fast, dtype=jnp.int32)[None, :, None]
    )
    send_rows = jnp.sum(jnp.where(picks, below[None, None, :].astype(jnp.int32), 0), axis=2)
    steps = jnp.arange(planes, dtype=jnp.int32)
    upward = (plane_index + steps) % planes
    send_rows = jnp.sum(
        jnp.where(upward[:, None, None] == steps[None, :, None], send_rows[None], 0), axis=1
    )
    my_ids = lax.dynamic_index_in_dim(even_id, plane_index, 0, keepdims=False)
    my_rank = lax.dynamic_index_in_dim(rank, plane_index, 0, keepdims=False).reshape(-1)
    place = jnp.sum(jnp.where(my_ids[:, None] == ids[None, :], my_rank[None, :], 0), axis=1)
    my_step = (plane_index + planes - my_ids // plane_rows) % planes

    def exact(source, chunk):
        rows = stepped(send_rows) if chunk else send_rows
        if planes > MOST_SHIFTS:
            return [jnp.take(source, rows[k], axis=0, mode="clip") for k in range(planes)]
        return [source, *select_rows(rows[1:], source)]

    def whole(source, chunk):
        return [source] * planes

    def exchange(sources, select, index, between):
        received, arrived = [], []
        for chunk, source in enumerate(sources):
            sending = select(source, chunk)
            if received:
                sending, _ = lax.optimization_barrier((sending, received[-1]))
            received.append(across(sending))
            outgoing = gather_rows(index[chunk], received[-1], group, parts)
            outgoing, _ = lax.optimization_barrier((outgoing, after if arrived else odd_query))
            arrived.append(swap(outgoing, plane_groups))
            after = arrived[-1] if chunk else between(arrived[-1])
        return [a.reshape(lanes, wanted, piece, width) for a in arrived]

    odd_part = jnp.zeros((shards * capacity, columns + DH), F32)
    for k in range(parts):
        slot_want = slot_row - (part_index + parts - k) % parts * held
        slot_want = jnp.broadcast_to(slot_want.reshape(-1, 1), (shards * capacity, DH))
        odd_part = odd_attention(
            odd_query, slot_want, (early_shared[k], late_shared[k]), weights, odd_part
        )

    returned = []

    def send_back(after):
        part, _ = lax.optimization_barrier((odd_part, after))
        part = lax.all_to_all(part.reshape(shards, capacity, columns + DH), "db", 0, 0, tiled=True)
        returned.append(part)
        return part

    def attend(select, index, between, odd_rows):
        early, late = exchange(plane_pieces, select, index, between)
        early = project(early, weights)
        return even_attention(queries, late, weights, early, odd_rows())

    def odd_rows():
        return combine(my_slot, returned[0].reshape(shards * capacity, columns + DH), sequences)

    own_rows = [my_ids % plane_rows, stepped(my_ids % plane_rows)]
    fast_index = my_step * fast + jnp.minimum(place, fast - 1)
    fast_index = [fast_index] * CHUNKS
    if planes <= MOST_SHIFTS:
        fast_index = [
            jnp.where(my_step == 0, row, index + plane_rows - fast) for row, index in zip(own_rows, fast_index)
        ]
    result = attend(exact, fast_index, send_back, odd_rows)
    if fast < most:
        result = lax.cond(
            fits,
            lambda done: done,
            lambda done: attend(
                whole, [my_step * plane_rows + row for row in own_rows], lambda arrived: arrived, odd_rows
            ),
            result,
        )
    return result


def solution(mesh):
    placed = (
        P("db", "mp"),
        P(("db", "mp"), None, None),
        P("db", "mp"),
        P("db", "mp"),
        P("db", None),
        P("db", None),
    )

    return jax.shard_map(local, mesh=mesh, in_specs=placed, out_specs=P("db", "mp"), check_vma=False)
```

```python
import functools
import math

import jax
import jax.numpy as jnp
from jax import lax
from jax.experimental import pallas as pl
from jax.experimental.pallas import tpu as pltpu
from jax.sharding import PartitionSpec as P


DH = 128
SPAN = 64
SEQ = 128
LANES = 8
CHUNKS = 2
MOST_SHIFTS = 8
LOW = (SPAN - 1) // 16 * 16
FAST_SLOTS = 46
BF16 = jnp.bfloat16
F32 = jnp.float32
SCALE = 1.0 / math.sqrt(DH)
BOTH = ("db", "mp")
CONTRACT_LAST = (((1,), (1,)), ((), ()))


def project_rows(rows_refs, weight_ref):
    lanes, count, piece, _ = rows_refs[0].shape
    rows = [ref[...] for ref in rows_refs]
    stacked = jnp.concatenate(
        [
            jnp.concatenate([r[:, j].reshape(lanes * piece, r.shape[3]) for r in rows], axis=1)
            for j in range(count)
        ],
        axis=0,
    )
    return jnp.dot(stacked, weight_ref[...], preferred_element_type=F32).astype(BF16)


def project_body(rows_ref, weight_ref, out_ref):
    out_ref[...] = project_rows([rows_ref], weight_ref)


def project(rows, weights):
    lanes, count, piece, width = rows.shape
    per_step = math.gcd(count, 8)
    tokens = lanes * piece
    return pl.pallas_call(
        project_body,
        out_shape=jax.ShapeDtypeStruct((count * tokens, weights.shape[1]), BF16),
        grid=(count // per_step,),
        in_specs=[
            pl.BlockSpec((lanes, per_step, piece, width), lambda i: (0, i, 0, 0)),
            pl.BlockSpec(weights.shape, lambda i: (0, 0)),
        ],
        out_specs=pl.BlockSpec((per_step * tokens, weights.shape[1]), lambda i: (i, 0)),
        name="project",
    )(rows, weights)


def even_body(query_ref, *refs, per_step):
    rows_refs, (weight_ref, early_ref, odd_ref, out_ref) = refs[:-4], refs[-4:]
    columns = query_ref.shape[1]
    late = project_rows(rows_refs, weight_ref)
    span = late.shape[0] // per_step
    first = SPAN - 1
    position = LOW + lax.broadcasted_iota(jnp.int32, (SEQ - LOW, DH), 0)
    odd = [odd_ref[pl.ds(pl.program_id(0) * per_step + s, 1), :] for s in range(per_step)]
    blocks = [(s, h * DH) for s in range(per_step) for h in range(columns // DH)]

    def both(s, lo):
        at = slice(s * span, (s + 1) * span)
        return jnp.concatenate([early_ref[at, lo : lo + DH], late[at, lo : lo + DH]], axis=0)

    scores = [
        lax.dot_general(
            query_ref[s * SEQ + LOW : (s + 1) * SEQ, lo : lo + DH],
            both(s, lo),
            CONTRACT_LAST,
            preferred_element_type=F32,
        )
        * SCALE
        for s, lo in blocks
    ]
    largest = [jnp.max(x, axis=1, keepdims=True) for x in scores]
    expscore = [jnp.exp(x - m) for x, m in zip(scores, largest)]
    total = [jnp.sum(e, axis=1, keepdims=True) for e in expscore]
    mixed = [
        jnp.dot(e.astype(BF16), both(s, columns + lo), preferred_element_type=F32)
        for e, (s, lo) in zip(expscore, blocks)
    ]
    for s in range(per_step):
        out_ref[s * SEQ : s * SEQ + LOW, :] = jnp.zeros((LOW, columns), BF16)
    for (s, lo), over, under in zip(blocks, mixed, total):
        attended = over * (1.0 / under)
        attended = jnp.where(position == SEQ - 1, odd[s][:, lo : lo + DH], attended)
        attended = jnp.where(position < first, 0.0, attended)
        out_ref[s * SEQ + LOW : (s + 1) * SEQ, lo : lo + DH] = attended.astype(BF16)


def even_attention(queries, rows, weights, early, odd):
    columns = queries.shape[1]
    sequences = queries.shape[0] // SEQ
    lanes, count, piece, _ = rows[0].shape
    per_step = math.gcd(sequences, 2)
    rows_step = per_step * count // sequences
    query_spec = pl.BlockSpec((per_step * SEQ, columns), lambda i: (i, 0))
    return pl.pallas_call(
        functools.partial(even_body, per_step=per_step),
        out_shape=jax.ShapeDtypeStruct(queries.shape, BF16),
        grid=(sequences // per_step,),
        in_specs=[
            query_spec,
            *[pl.BlockSpec((lanes, rows_step, piece, r.shape[3]), lambda i: (0, i, 0, 0)) for r in rows],
            pl.BlockSpec(weights.shape, lambda i: (0, 0)),
            pl.BlockSpec((rows_step * lanes * piece, weights.shape[1]), lambda i: (i, 0)),
            pl.BlockSpec(odd.shape, lambda i: (0, 0)),
        ],
        out_specs=query_spec,
        name="even_attention",
    )(queries, *rows, weights, early, odd)


def combine_body(slot_ref, odd_ref, row_ref, *picked_refs):
    sequences, columns = row_ref.shape
    for i in range(sequences):
        for j, picked_ref in enumerate(picked_refs):
            picked_ref[i : i + 1, :] = odd_ref[pl.ds(slot_ref[i * len(picked_refs) + j], 1), :]
    for h in range(columns // DH):
        lo, hi = h * DH, (h + 1) * DH
        maxima = [p[:, columns + h : columns + h + 1] for p in picked_refs]
        sums = [p[:, columns + DH // 2 + h : columns + DH // 2 + h + 1] for p in picked_refs]
        top = functools.reduce(jnp.maximum, maxima)
        each = [jnp.exp(m - top) for m in maxima]
        under = sum(e * t for e, t in zip(each, sums))
        over = sum(e * p[:, lo:hi] for e, p in zip(each, picked_refs))
        row_ref[:, lo:hi] = over / under


def combine(slots, odd, sequences):
    columns = odd.shape[1] - DH
    return pl.pallas_call(
        combine_body,
        out_shape=jax.ShapeDtypeStruct((sequences, columns), F32),
        grid_spec=pltpu.PrefetchScalarGridSpec(
            num_scalar_prefetch=1,
            grid=(1,),
            in_specs=[pl.BlockSpec(odd.shape, lambda i, s: (0, 0))],
            out_specs=pl.BlockSpec((sequences, columns), lambda i, s: (0, 0)),
            scratch_shapes=[pltpu.VMEM((sequences, odd.shape[1]), F32)] * (slots.shape[0] // sequences),
        ),
        name="combine",
    )(slots, odd)


def gather_body(index_ref, *refs, count):
    sources, out_ref, stage_ref, sem_ref = refs[:count], refs[count], refs[count + 1], refs[count + 2]
    copies, wanted = out_ref.shape[1:3]
    starts = [sum(s.shape[0] for s in sources[:k]) for k in range(count)]
    base = pl.program_id(0) * wanted

    @pl.when(pl.program_id(0) == 0)
    def _():
        moves = [
            pltpu.make_async_copy(source, stage_ref.at[pl.ds(starts[k], source.shape[0])], sem_ref.at[k])
            for k, source in enumerate(sources)
        ]
        for move in moves:
            move.start()
        for move in moves:
            move.wait()

    def step(i, carry):
        row = stage_ref[index_ref[base + i]]
        for c in range(copies):
            out_ref[0, c, i] = row
        return carry

    lax.fori_loop(0, wanted, step, 0, unroll=8)


def gather_rows(index, sources, groups, copies):
    wanted = index.shape[0] // groups
    piece, width = sources[0].shape[1:]
    out = pl.pallas_call(
        functools.partial(gather_body, count=len(sources)),
        out_shape=jax.ShapeDtypeStruct((groups, copies, wanted, piece, width), sources[0].dtype),
        grid_spec=pltpu.PrefetchScalarGridSpec(
            num_scalar_prefetch=1,
            grid=(groups,),
            in_specs=[pl.BlockSpec(memory_space=pl.ANY) for _ in sources],
            out_specs=pl.BlockSpec((1, copies, wanted, piece, width), lambda i, s: (i, 0, 0, 0, 0)),
            scratch_shapes=[
                pltpu.VMEM((sum(s.shape[0] for s in sources), piece, width), sources[0].dtype),
                pltpu.SemaphoreType.DMA((len(sources),)),
            ],
        ),
        name="gather_rows",
    )(index, *sources)
    return out.reshape(groups * copies * wanted, piece, width)


def select_body(index_ref, source_ref, *out_refs):
    fast = out_refs[0].shape[0]

    def step(i, carry):
        for k, out_ref in enumerate(out_refs):
            out_ref[i] = source_ref[index_ref[k * fast + i]]
        return carry

    lax.fori_loop(0, fast, step, 0, unroll=2)


def select_rows(index, source):
    count, fast = index.shape
    block = pl.BlockSpec((fast,) + source.shape[1:], lambda i, s: (0, 0, 0))
    return pl.pallas_call(
        select_body,
        out_shape=[jax.ShapeDtypeStruct((fast,) + source.shape[1:], source.dtype)] * count,
        grid_spec=pltpu.PrefetchScalarGridSpec(
            num_scalar_prefetch=1,
            grid=(1,),
            in_specs=[pl.BlockSpec(source.shape, lambda i, s: (0, 0, 0))],
            out_specs=[block] * count,
        ),
        name="select_rows",
    )(index.reshape(-1), source)


def odd_body(query_ref, want_ref, *refs):
    rows_refs, (weight_ref, prior_ref, out_ref) = refs[:-3], refs[-3:]
    columns = query_ref.shape[1]
    heads = columns // DH
    lanes, per_step, piece, width = rows_refs[0].shape
    tokens = len(rows_refs) * lanes * piece
    step = pl.program_id(0)

    @pl.when(step == 0)
    def _():
        out_ref[...] = prior_ref[...]

    pieces = [ref[...] for ref in rows_refs]
    stacked = jnp.concatenate(
        [p[:, r].reshape(lanes * piece, width) for r in range(per_step) for p in pieces], axis=0
    )
    projected = jnp.dot(stacked, weight_ref[...], preferred_element_type=F32).astype(BF16)
    want = want_ref[...] - step * per_step
    here = [want == r for r in range(per_step)]
    inside = (want >= 0) & (want < per_step)
    lane = lax.broadcasted_iota(jnp.int32, (want.shape[0], DH), 1)
    spans = [(h * DH, (h + 1) * DH) for h in range(heads)]
    scores = [
        lax.dot_general(
            query_ref[:, lo:hi], projected[:, lo:hi], CONTRACT_LAST, preferred_element_type=F32
        )
        * SCALE
        for lo, hi in spans
    ]
    mine = []
    for x in scores:
        chosen = jnp.zeros((want.shape[0], tokens), F32)
        for r in range(per_step):
            chosen = jnp.where(here[r], x[:, r * tokens : (r + 1) * tokens], chosen)
        mine.append(chosen)
    largest = [jnp.max(x, axis=1, keepdims=True) for x in mine]
    expscore = [jnp.exp(x - m) for x, m in zip(mine, largest)]
    total = [jnp.sum(e, axis=1, keepdims=True) for e in expscore]
    spread = [
        jnp.concatenate([jnp.where(here[r], e, 0.0) for r in range(per_step)], axis=1).astype(BF16)
        for e in expscore
    ]
    mixed = [
        jnp.dot(p, projected[:, columns + lo : columns + hi], preferred_element_type=F32)
        for p, (lo, hi) in zip(spread, spans)
    ]
    stats = out_ref[:, columns:]
    for h, (lo, hi) in enumerate(spans):
        out_ref[:, lo:hi] = jnp.where(inside, mixed[h], out_ref[:, lo:hi])
        stats = jnp.where(inside & (lane == h), largest[h], stats)
        stats = jnp.where(inside & (lane == DH // 2 + h), total[h], stats)
    out_ref[:, columns:] = stats


def odd_attention(queries, want, rows, weights, prior):
    slots, columns = queries.shape
    lanes, count, piece, width = rows[0].shape
    per_step = math.gcd(count, 4)
    row_spec = pl.BlockSpec((lanes, per_step, piece, width), lambda i: (0, i, 0, 0))
    return pl.pallas_call(
        odd_body,
        out_shape=jax.ShapeDtypeStruct(prior.shape, F32),
        grid=(count // per_step,),
        in_specs=[
            pl.BlockSpec((slots, columns), lambda i: (0, 0)),
            pl.BlockSpec((slots, DH), lambda i: (0, 0)),
            *[row_spec for _ in rows],
            pl.BlockSpec(weights.shape, lambda i: (0, 0)),
            pl.BlockSpec(prior.shape, lambda i: (0, 0)),
        ],
        out_specs=pl.BlockSpec(prior.shape, lambda i: (0, 0)),
        name="odd_attention",
    )(queries, want, *rows, weights, prior)


def local(queries, encodings, key_weight, value_weight, nbr_shard, nbr_row):
    shards = lax.axis_size("db")
    parts = lax.axis_size("mp")
    group = max(1, LANES // parts)
    lanes = group * parts
    planes = shards // group
    columns = queries.shape[1]
    held, tokens, width = encodings.shape
    piece = tokens // (lanes * CHUNKS)
    shard_rows = held * parts
    plane_rows = group * shard_rows
    span_count, neighbours = nbr_shard.shape
    sequences = queries.shape[0] // SEQ
    wanted = sequences * neighbours
    capacity = max(2, 4 * span_count // shards)
    most = min(plane_rows, group * wanted, group * group * capacity)
    fast = min(most, FAST_SLOTS)
    plane_groups = [[a * lanes + b for b in range(lanes)] for a in range(planes)]
    lane_groups = [[a * lanes + b for a in range(planes)] for b in range(lanes)]
    db_index = lax.axis_index("db")
    plane_index = db_index // group

    def swap(x, groups):
        return lax.all_to_all(x, BOTH, 0, 0, axis_index_groups=groups, tiled=True)

    def across(blocks):
        if planes > MOST_SHIFTS:
            stacked = jnp.stack(blocks)
            ordered = jnp.take(stacked, (jnp.arange(planes) - plane_index) % planes, axis=0, mode="clip")
            ordered = swap(ordered.reshape((-1,) + stacked.shape[2:]), lane_groups).reshape(stacked.shape)
            moved = jnp.take(ordered, (plane_index - jnp.arange(planes)) % planes, axis=0, mode="clip")
            return [moved.reshape((-1,) + stacked.shape[2:])]
        moved = [blocks[0]]
        for k in range(1, planes):
            pairs = [
                (a * lanes + b, (a + k) % planes * lanes + b) for a in range(planes) for b in range(lanes)
            ]
            moved.append(lax.ppermute(blocks[k], BOTH, pairs))
        return moved

    table = jnp.concatenate([nbr_shard.reshape(-1), nbr_row.reshape(-1)])
    table = jnp.broadcast_to(table[None, None], (shards, 1, table.shape[0]))
    table = lax.all_to_all(table, "db", 0, 0, tiled=True)
    table = table.reshape(shards, 2, sequences, SEQ // SPAN, neighbours)
    table_shard, table_row = table[:, 0], table[:, 1]

    weights = lax.all_gather(
        jnp.concatenate([key_weight, value_weight], axis=1), "db", axis=0, tiled=True
    )

    early_half, late_half = jnp.transpose(encodings.reshape(held, lanes, CHUNKS, piece, width), (2, 1, 0, 3, 4))
    first, _ = lax.optimization_barrier((early_half.reshape(lanes * held, piece, width), table))
    first = swap(first, plane_groups)

    odd_shard = table_shard[:, :, 1].reshape(shards, wanted)
    odd_row = table_row[:, :, 1].reshape(shards, wanted)
    earlier = jnp.arange(wanted)
    same = (odd_shard[:, :, None] == odd_shard[:, None, :]) & (earlier[None, None, :] < earlier[None, :, None])
    odd_rank = jnp.sum(same.astype(jnp.int32), axis=2)
    arriving = (odd_shard == db_index)[:, None, :] & (
        odd_rank[:, None, :] == jnp.arange(capacity, dtype=jnp.int32)[None, :, None]
    )
    slot_row = jnp.sum(jnp.where(arriving, odd_row[:, None, :] + 1, 0), axis=2) - 1
    my_slot = lax.dynamic_index_in_dim(odd_shard * capacity + odd_rank, db_index, 0, keepdims=False)
    slots = jnp.arange(shards * capacity, dtype=jnp.int32)
    chosen = my_slot[None, :] == slots[:, None]
    sender = jnp.sum(jnp.where(chosen, (earlier // neighbours).astype(jnp.int32)[None, :], 0), axis=1)
    last_rows = queries.reshape(sequences, SEQ, columns)[:, SEQ - 1]
    odd_query = jnp.take(last_rows, sender, axis=0, mode="clip").reshape(shards, capacity, columns)

    part_index = lax.axis_index("mp")

    def share(half, after):
        half, _ = lax.optimization_barrier((half, after))
        shared = [half]
        for k in range(1, parts):
            shared.append(lax.ppermute(half, "mp", [(m, (m + k) % parts) for m in range(parts)]))
        return shared

    late_shared = share(late_half, table)
    second = [
        lax.dynamic_index_in_dim(
            half.reshape(group, parts, held, piece, width), part_index, 1, keepdims=False
        )
        for half in late_shared
    ]
    second = jnp.concatenate(second, axis=1).reshape(group * shard_rows, piece, width)
    part_groups = [
        [a * lanes + g * parts + m for g in range(group)] for a in range(planes) for m in range(parts)
    ]
    second, _ = lax.optimization_barrier((second, first))
    if group > 1:
        second = swap(second, part_groups)
    early_shared = share(early_half, late_shared)
    odd_query, _ = lax.optimization_barrier((odd_query, second))
    odd_query = lax.all_to_all(odd_query, "db", 0, 0, tiled=True)
    odd_query = odd_query.reshape(shards * capacity, columns)
    cut = (width // DH + 1) // 2 * DH
    plane_pieces = [first, second[:, :, :cut], second[:, :, cut:]]

    def stepped(row):
        step = (part_index + parts - row % shard_rows // held) % parts
        return row // shard_rows * shard_rows + step * held + row % held

    even_id = (table_shard[:, :, 0] * shard_rows + table_row[:, :, 0]).reshape(planes, group * wanted)
    ids = jnp.arange(planes * plane_rows, dtype=jnp.int32)
    want = jnp.any(even_id[:, :, None] == ids[None, None, :], axis=1).reshape(planes, planes, plane_rows)
    below = jnp.arange(plane_rows)
    before = (below[:, None] < below[None, :]).astype(BF16)
    rank = jnp.dot(want.astype(BF16), before, preferred_element_type=F32).astype(jnp.int32)
    loads = jnp.sum(want.astype(jnp.int32), axis=2)
    if planes <= MOST_SHIFTS:
        loads = jnp.where(jnp.eye(planes, dtype=jnp.bool_), 0, loads)
    fits = jnp.max(loads) <= fast
    mine_want = lax.dynamic_index_in_dim(want, plane_index, 1, keepdims=False)
    mine_rank = lax.dynamic_index_in_dim(rank, plane_index, 1, keepdims=False)
    picks = mine_want[:, None, :] & (
        mine_rank[:, None, :] == jnp.arange(fast, dtype=jnp.int32)[None, :, None]
    )
    send_rows = jnp.sum(jnp.where(picks, below[None, None, :].astype(jnp.int32), 0), axis=2)
    steps = jnp.arange(planes, dtype=jnp.int32)
    upward = (plane_index + steps) % planes
    send_rows = jnp.sum(
        jnp.where(upward[:, None, None] == steps[None, :, None], send_rows[None], 0), axis=1
    )
    my_ids = lax.dynamic_index_in_dim(even_id, plane_index, 0, keepdims=False)
    my_rank = lax.dynamic_index_in_dim(rank, plane_index, 0, keepdims=False).reshape(-1)
    place = jnp.sum(jnp.where(my_ids[:, None] == ids[None, :], my_rank[None, :], 0), axis=1)
    my_step = (plane_index + planes - my_ids // plane_rows) % planes

    def exact(source, chunk):
        rows = stepped(send_rows) if chunk else send_rows
        if planes > MOST_SHIFTS:
            return [jnp.take(source, rows[k], axis=0, mode="clip") for k in range(planes)]
        return [source, *select_rows(rows[1:], source)]

    def whole(source, chunk):
        return [source] * planes

    def exchange(sources, select, index, between):
        received, arrived = [], []
        for chunk, source in enumerate(sources):
            sending = select(source, chunk)
            if received:
                sending, _ = lax.optimization_barrier((sending, received[-1]))
            received.append(across(sending))
            outgoing = gather_rows(index[min(chunk, 1)], received[-1], group, parts)
            outgoing, _ = lax.optimization_barrier((outgoing, after if arrived else odd_query))
            arrived.append(swap(outgoing, plane_groups))
            after = arrived[-1] if chunk else between(arrived[-1])
        return [a.reshape(lanes, wanted, piece, a.shape[2]) for a in arrived]

    odd_part = jnp.zeros((shards * capacity, columns + DH), F32)
    for k in range(parts):
        slot_want = slot_row - (part_index + parts - k) % parts * held
        slot_want = jnp.broadcast_to(slot_want.reshape(-1, 1), (shards * capacity, DH))
        odd_part = odd_attention(
            odd_query, slot_want, (early_shared[k], late_shared[k]), weights, odd_part
        )

    returned = []

    def send_back(after):
        part, _ = lax.optimization_barrier((odd_part, after))
        part = lax.all_to_all(part.reshape(shards, capacity, columns + DH), "db", 0, 0, tiled=True)
        returned.append(part)
        return part

    def attend(select, index, between, odd_rows):
        early, *late = exchange(plane_pieces, select, index, between)
        early = project(early, weights)
        return even_attention(queries, late, weights, early, odd_rows())

    def odd_rows():
        return combine(my_slot, returned[0].reshape(shards * capacity, columns + DH), sequences)

    own_rows = [my_ids % plane_rows, stepped(my_ids % plane_rows)]
    fast_index = my_step * fast + jnp.minimum(place, fast - 1)
    fast_index = [fast_index] * CHUNKS
    if planes <= MOST_SHIFTS:
        fast_index = [
            jnp.where(my_step == 0, row, index + plane_rows - fast) for row, index in zip(own_rows, fast_index)
        ]
    result = attend(exact, fast_index, send_back, odd_rows)
    if fast < most:
        result = lax.cond(
            fits,
            lambda done: done,
            lambda done: attend(
                whole, [my_step * plane_rows + row for row in own_rows], lambda arrived: arrived, odd_rows
            ),
            result,
        )
    return result


def solution(mesh):
    placed = (
        P("db", "mp"),
        P(("db", "mp"), None, None),
        P("db", "mp"),
        P("db", "mp"),
        P("db", None),
        P("db", None),
    )

    return jax.shard_map(local, mesh=mesh, in_specs=placed, out_specs=P("db", "mp"), check_vma=False)
```

```python
import functools
import math

import jax
import jax.numpy as jnp
from jax import lax
from jax.experimental import pallas as pl
from jax.experimental.pallas import tpu as pltpu
from jax.sharding import PartitionSpec as P


DH = 128
SPAN = 64
SEQ = 128
LANES = 8
CHUNKS = 2
MOST_SHIFTS = 8
LOW = (SPAN - 1) // 16 * 16
FAST_SLOTS = 46
BF16 = jnp.bfloat16
F32 = jnp.float32
SCALE = 1.0 / math.sqrt(DH)
BOTH = ("db", "mp")
CONTRACT_LAST = (((1,), (1,)), ((), ()))


def project_rows(rows_refs, weight_ref):
    lanes, count, piece, _ = rows_refs[0].shape
    rows = [ref[...] for ref in rows_refs]
    stacked = jnp.concatenate(
        [
            jnp.concatenate([r[:, j].reshape(lanes * piece, r.shape[3]) for r in rows], axis=1)
            for j in range(count)
        ],
        axis=0,
    )
    return jnp.dot(stacked, weight_ref[...], preferred_element_type=F32).astype(BF16)


def project_body(rows_ref, weight_ref, out_ref):
    out_ref[...] = project_rows([rows_ref], weight_ref)


def project(rows, weights):
    lanes, count, piece, width = rows.shape
    per_step = math.gcd(count, 8)
    tokens = lanes * piece
    return pl.pallas_call(
        project_body,
        out_shape=jax.ShapeDtypeStruct((count * tokens, weights.shape[1]), BF16),
        grid=(count // per_step,),
        in_specs=[
            pl.BlockSpec((lanes, per_step, piece, width), lambda i: (0, i, 0, 0)),
            pl.BlockSpec(weights.shape, lambda i: (0, 0)),
        ],
        out_specs=pl.BlockSpec((per_step * tokens, weights.shape[1]), lambda i: (i, 0)),
        name="project",
    )(rows, weights)


def even_body(query_ref, *refs, per_step):
    rows_refs, (weight_ref, early_ref, odd_ref, out_ref) = refs[:-4], refs[-4:]
    columns = query_ref.shape[1]
    late = project_rows(rows_refs, weight_ref)
    span = late.shape[0] // per_step
    first = SPAN - 1
    position = LOW + lax.broadcasted_iota(jnp.int32, (SEQ - LOW, DH), 0)
    odd = [odd_ref[pl.ds(pl.program_id(0) * per_step + s, 1), :] for s in range(per_step)]
    blocks = [(s, h * DH) for s in range(per_step) for h in range(columns // DH)]

    def both(s, lo):
        at = slice(s * span, (s + 1) * span)
        return jnp.concatenate([early_ref[at, lo : lo + DH], late[at, lo : lo + DH]], axis=0)

    scores = [
        lax.dot_general(
            query_ref[s * SEQ + LOW : (s + 1) * SEQ, lo : lo + DH],
            both(s, lo),
            CONTRACT_LAST,
            preferred_element_type=F32,
        )
        * SCALE
        for s, lo in blocks
    ]
    largest = [jnp.max(x, axis=1, keepdims=True) for x in scores]
    expscore = [jnp.exp(x - m) for x, m in zip(scores, largest)]
    total = [jnp.sum(e, axis=1, keepdims=True) for e in expscore]
    mixed = [
        jnp.dot(e.astype(BF16), both(s, columns + lo), preferred_element_type=F32)
        for e, (s, lo) in zip(expscore, blocks)
    ]
    for s in range(per_step):
        out_ref[s * SEQ : s * SEQ + LOW, :] = jnp.zeros((LOW, columns), BF16)
    for (s, lo), over, under in zip(blocks, mixed, total):
        attended = over * (1.0 / under)
        attended = jnp.where(position == SEQ - 1, odd[s][:, lo : lo + DH], attended)
        attended = jnp.where(position < first, 0.0, attended)
        out_ref[s * SEQ + LOW : (s + 1) * SEQ, lo : lo + DH] = attended.astype(BF16)


def even_attention(queries, rows, weights, early, odd):
    columns = queries.shape[1]
    sequences = queries.shape[0] // SEQ
    lanes, count, piece, _ = rows[0].shape
    per_step = math.gcd(sequences, 2)
    rows_step = per_step * count // sequences
    query_spec = pl.BlockSpec((per_step * SEQ, columns), lambda i: (i, 0))
    return pl.pallas_call(
        functools.partial(even_body, per_step=per_step),
        out_shape=jax.ShapeDtypeStruct(queries.shape, BF16),
        grid=(sequences // per_step,),
        in_specs=[
            query_spec,
            *[pl.BlockSpec((lanes, rows_step, piece, r.shape[3]), lambda i: (0, i, 0, 0)) for r in rows],
            pl.BlockSpec(weights.shape, lambda i: (0, 0)),
            pl.BlockSpec((rows_step * lanes * piece, weights.shape[1]), lambda i: (i, 0)),
            pl.BlockSpec(odd.shape, lambda i: (0, 0)),
        ],
        out_specs=query_spec,
        name="even_attention",
    )(queries, *rows, weights, early, odd)


def combine_body(slot_ref, odd_ref, row_ref, *picked_refs):
    sequences, columns = row_ref.shape
    for i in range(sequences):
        for j, picked_ref in enumerate(picked_refs):
            picked_ref[i : i + 1, :] = odd_ref[pl.ds(slot_ref[i * len(picked_refs) + j], 1), :]
    for h in range(columns // DH):
        lo, hi = h * DH, (h + 1) * DH
        maxima = [p[:, columns + h : columns + h + 1] for p in picked_refs]
        sums = [p[:, columns + DH // 2 + h : columns + DH // 2 + h + 1] for p in picked_refs]
        top = functools.reduce(jnp.maximum, maxima)
        each = [jnp.exp(m - top) for m in maxima]
        under = sum(e * t for e, t in zip(each, sums))
        over = sum(e * p[:, lo:hi] for e, p in zip(each, picked_refs))
        row_ref[:, lo:hi] = over / under


def combine(slots, odd, sequences):
    columns = odd.shape[1] - DH
    return pl.pallas_call(
        combine_body,
        out_shape=jax.ShapeDtypeStruct((sequences, columns), F32),
        grid_spec=pltpu.PrefetchScalarGridSpec(
            num_scalar_prefetch=1,
            grid=(1,),
            in_specs=[pl.BlockSpec(odd.shape, lambda i, s: (0, 0))],
            out_specs=pl.BlockSpec((sequences, columns), lambda i, s: (0, 0)),
            scratch_shapes=[pltpu.VMEM((sequences, odd.shape[1]), F32)] * (slots.shape[0] // sequences),
        ),
        name="combine",
    )(slots, odd)


def gather_body(index_ref, *refs, count):
    sources, out_ref, stage_ref, sem_ref = refs[:count], refs[count], refs[count + 1], refs[count + 2]
    copies, wanted = out_ref.shape[1:3]
    starts = [sum(s.shape[0] for s in sources[:k]) for k in range(count)]
    base = pl.program_id(0) * wanted

    @pl.when(pl.program_id(0) == 0)
    def _():
        moves = [
            pltpu.make_async_copy(source, stage_ref.at[pl.ds(starts[k], source.shape[0])], sem_ref.at[k])
            for k, source in enumerate(sources)
        ]
        for move in moves:
            move.start()
        for move in moves:
            move.wait()

    def step(i, carry):
        row = stage_ref[index_ref[base + i]]
        for c in range(copies):
            out_ref[0, c, i] = row
        return carry

    lax.fori_loop(0, wanted, step, 0, unroll=8)


def gather_rows(index, sources, groups, copies):
    wanted = index.shape[0] // groups
    piece, width = sources[0].shape[1:]
    out = pl.pallas_call(
        functools.partial(gather_body, count=len(sources)),
        out_shape=jax.ShapeDtypeStruct((groups, copies, wanted, piece, width), sources[0].dtype),
        grid_spec=pltpu.PrefetchScalarGridSpec(
            num_scalar_prefetch=1,
            grid=(groups,),
            in_specs=[pl.BlockSpec(memory_space=pl.ANY) for _ in sources],
            out_specs=pl.BlockSpec((1, copies, wanted, piece, width), lambda i, s: (i, 0, 0, 0, 0)),
            scratch_shapes=[
                pltpu.VMEM((sum(s.shape[0] for s in sources), piece, width), sources[0].dtype),
                pltpu.SemaphoreType.DMA((len(sources),)),
            ],
        ),
        name="gather_rows",
    )(index, *sources)
    return out.reshape(groups * copies * wanted, piece, width)


def select_body(index_ref, source_ref, *out_refs):
    fast = out_refs[0].shape[0]

    def step(i, carry):
        for k, out_ref in enumerate(out_refs):
            out_ref[i] = source_ref[index_ref[k * fast + i]]
        return carry

    lax.fori_loop(0, fast, step, 0, unroll=2)


def select_rows(index, source):
    count, fast = index.shape
    block = pl.BlockSpec((fast,) + source.shape[1:], lambda i, s: (0, 0, 0))
    return pl.pallas_call(
        select_body,
        out_shape=[jax.ShapeDtypeStruct((fast,) + source.shape[1:], source.dtype)] * count,
        grid_spec=pltpu.PrefetchScalarGridSpec(
            num_scalar_prefetch=1,
            grid=(1,),
            in_specs=[pl.BlockSpec(source.shape, lambda i, s: (0, 0, 0))],
            out_specs=[block] * count,
        ),
        name="select_rows",
    )(index.reshape(-1), source)


def odd_body(query_ref, want_ref, *refs):
    rows_refs, (weight_ref, prior_ref, out_ref) = refs[:-3], refs[-3:]
    columns = query_ref.shape[1]
    heads = columns // DH
    _, per_step, piece, width = rows_refs[0].shape
    tokens = sum(ref.shape[0] for ref in rows_refs) * piece
    step = pl.program_id(0)

    @pl.when(step == 0)
    def _():
        out_ref[...] = prior_ref[...]

    pieces = [ref[...] for ref in rows_refs]
    stacked = jnp.concatenate(
        [p[:, r].reshape(p.shape[0] * piece, width) for r in range(per_step) for p in pieces], axis=0
    )
    projected = jnp.dot(stacked, weight_ref[...], preferred_element_type=F32).astype(BF16)
    want = want_ref[...] - step * per_step
    here = [want == r for r in range(per_step)]
    inside = (want >= 0) & (want < per_step)
    lane = lax.broadcasted_iota(jnp.int32, (want.shape[0], DH), 1)
    spans = [(h * DH, (h + 1) * DH) for h in range(heads)]
    scores = [
        lax.dot_general(
            query_ref[:, lo:hi], projected[:, lo:hi], CONTRACT_LAST, preferred_element_type=F32
        )
        * SCALE
        for lo, hi in spans
    ]
    mine = []
    for x in scores:
        chosen = jnp.zeros((want.shape[0], tokens), F32)
        for r in range(per_step):
            chosen = jnp.where(here[r], x[:, r * tokens : (r + 1) * tokens], chosen)
        mine.append(chosen)
    largest = [jnp.max(x, axis=1, keepdims=True) for x in mine]
    expscore = [jnp.exp(x - m) for x, m in zip(mine, largest)]
    total = [jnp.sum(e, axis=1, keepdims=True) for e in expscore]
    spread = [
        jnp.concatenate([jnp.where(here[r], e, 0.0) for r in range(per_step)], axis=1).astype(BF16)
        for e in expscore
    ]
    mixed = [
        jnp.dot(p, projected[:, columns + lo : columns + hi], preferred_element_type=F32)
        for p, (lo, hi) in zip(spread, spans)
    ]
    stats = out_ref[:, columns:]
    for h, (lo, hi) in enumerate(spans):
        out_ref[:, lo:hi] = jnp.where(inside, mixed[h], out_ref[:, lo:hi])
        stats = jnp.where(inside & (lane == h), largest[h], stats)
        stats = jnp.where(inside & (lane == DH // 2 + h), total[h], stats)
    out_ref[:, columns:] = stats


def odd_attention(queries, want, rows, weights, prior):
    slots, columns = queries.shape
    _, count, piece, width = rows[0].shape
    per_step = math.gcd(count, 4)
    return pl.pallas_call(
        odd_body,
        out_shape=jax.ShapeDtypeStruct(prior.shape, F32),
        grid=(count // per_step,),
        in_specs=[
            pl.BlockSpec((slots, columns), lambda i: (0, 0)),
            pl.BlockSpec((slots, DH), lambda i: (0, 0)),
            *[pl.BlockSpec((r.shape[0], per_step, piece, width), lambda i: (0, i, 0, 0)) for r in rows],
            pl.BlockSpec(weights.shape, lambda i: (0, 0)),
            pl.BlockSpec(prior.shape, lambda i: (0, 0)),
        ],
        out_specs=pl.BlockSpec(prior.shape, lambda i: (0, 0)),
        name="odd_attention",
    )(queries, want, *rows, weights, prior)


def local(queries, encodings, key_weight, value_weight, nbr_shard, nbr_row):
    shards = lax.axis_size("db")
    parts = lax.axis_size("mp")
    group = max(1, LANES // parts)
    lanes = group * parts
    planes = shards // group
    columns = queries.shape[1]
    held, tokens, width = encodings.shape
    piece = tokens // (lanes * CHUNKS)
    shard_rows = held * parts
    plane_rows = group * shard_rows
    span_count, neighbours = nbr_shard.shape
    sequences = queries.shape[0] // SEQ
    wanted = sequences * neighbours
    capacity = max(2, 4 * span_count // shards)
    most = min(plane_rows, group * wanted, group * group * capacity)
    fast = min(most, FAST_SLOTS)
    plane_groups = [[a * lanes + b for b in range(lanes)] for a in range(planes)]
    lane_groups = [[a * lanes + b for a in range(planes)] for b in range(lanes)]
    db_index = lax.axis_index("db")
    plane_index = db_index // group

    def swap(x, groups):
        return lax.all_to_all(x, BOTH, 0, 0, axis_index_groups=groups, tiled=True)

    def across(blocks):
        if planes > MOST_SHIFTS:
            stacked = jnp.stack(blocks)
            ordered = jnp.take(stacked, (jnp.arange(planes) - plane_index) % planes, axis=0, mode="clip")
            ordered = swap(ordered.reshape((-1,) + stacked.shape[2:]), lane_groups).reshape(stacked.shape)
            moved = jnp.take(ordered, (plane_index - jnp.arange(planes)) % planes, axis=0, mode="clip")
            return [moved.reshape((-1,) + stacked.shape[2:])]
        moved = [blocks[0]]
        for k in range(1, planes):
            pairs = [
                (a * lanes + b, (a + k) % planes * lanes + b) for a in range(planes) for b in range(lanes)
            ]
            moved.append(lax.ppermute(blocks[k], BOTH, pairs))
        return moved

    table = jnp.concatenate([nbr_shard.reshape(-1), nbr_row.reshape(-1)])
    table = jnp.broadcast_to(table[None, None], (shards, 1, table.shape[0]))
    table = lax.all_to_all(table, "db", 0, 0, tiled=True)
    table = table.reshape(shards, 2, sequences, SEQ // SPAN, neighbours)
    table_shard, table_row = table[:, 0], table[:, 1]

    weights = lax.all_gather(
        jnp.concatenate([key_weight, value_weight], axis=1), "db", axis=0, tiled=True
    )

    early_half, late_half = jnp.transpose(encodings.reshape(held, lanes, CHUNKS, piece, width), (2, 1, 0, 3, 4))
    first, _ = lax.optimization_barrier((early_half.reshape(lanes * held, piece, width), table))
    first = swap(first, plane_groups)

    odd_shard = table_shard[:, :, 1].reshape(shards, wanted)
    odd_row = table_row[:, :, 1].reshape(shards, wanted)
    earlier = jnp.arange(wanted)
    same = (odd_shard[:, :, None] == odd_shard[:, None, :]) & (earlier[None, None, :] < earlier[None, :, None])
    odd_rank = jnp.sum(same.astype(jnp.int32), axis=2)
    arriving = (odd_shard == db_index)[:, None, :] & (
        odd_rank[:, None, :] == jnp.arange(capacity, dtype=jnp.int32)[None, :, None]
    )
    slot_row = jnp.sum(jnp.where(arriving, odd_row[:, None, :] + 1, 0), axis=2) - 1
    my_slot = lax.dynamic_index_in_dim(odd_shard * capacity + odd_rank, db_index, 0, keepdims=False)
    slots = jnp.arange(shards * capacity, dtype=jnp.int32)
    chosen = my_slot[None, :] == slots[:, None]
    sender = jnp.sum(jnp.where(chosen, (earlier // neighbours).astype(jnp.int32)[None, :], 0), axis=1)
    last_rows = queries.reshape(sequences, SEQ, columns)[:, SEQ - 1]
    odd_query = jnp.take(last_rows, sender, axis=0, mode="clip").reshape(shards, capacity, columns)

    part_index = lax.axis_index("mp")

    def share(half, after):
        half, _ = lax.optimization_barrier((half, after))
        shared = [half]
        for k in range(1, parts):
            shared.append(lax.ppermute(half, "mp", [(m, (m + k) % parts) for m in range(parts)]))
        return shared

    by_lane = late_half.reshape(group, parts, held, piece, width)
    near = lax.dynamic_index_in_dim(by_lane, part_index, 1, keepdims=False)
    if parts == 2:
        other = lax.dynamic_index_in_dim(by_lane, 1 - part_index, 1, keepdims=False)
        ahead = share(other, table)[1]
        behind = share(near, ahead)[1]
        late_rows = [(late_half,), (ahead, behind)]
        second = [near, ahead]
    else:
        ahead = share(late_half, table)
        late_rows = [(half,) for half in ahead]
        second = [
            lax.dynamic_index_in_dim(
                half.reshape(group, parts, held, piece, width), part_index, 1, keepdims=False
            )
            for half in ahead
        ]
    second = jnp.concatenate(second, axis=1).reshape(group * shard_rows, piece, width)
    part_groups = [
        [a * lanes + g * parts + m for g in range(group)] for a in range(planes) for m in range(parts)
    ]
    second, _ = lax.optimization_barrier((second, first))
    if group > 1:
        second = swap(second, part_groups)
    early_shared = share(early_half, ahead)
    odd_query, _ = lax.optimization_barrier((odd_query, second))
    odd_query = lax.all_to_all(odd_query, "db", 0, 0, tiled=True)
    odd_query = odd_query.reshape(shards * capacity, columns)
    plane_pieces = [first, second]

    def stepped(row):
        step = (part_index + parts - row % shard_rows // held) % parts
        return row // shard_rows * shard_rows + step * held + row % held

    even_id = (table_shard[:, :, 0] * shard_rows + table_row[:, :, 0]).reshape(planes, group * wanted)
    ids = jnp.arange(planes * plane_rows, dtype=jnp.int32)
    want = jnp.any(even_id[:, :, None] == ids[None, None, :], axis=1).reshape(planes, planes, plane_rows)
    below = jnp.arange(plane_rows)
    before = (below[:, None] < below[None, :]).astype(BF16)
    rank = jnp.dot(want.astype(BF16), before, preferred_element_type=F32).astype(jnp.int32)
    loads = jnp.sum(want.astype(jnp.int32), axis=2)
    if planes <= MOST_SHIFTS:
        loads = jnp.where(jnp.eye(planes, dtype=jnp.bool_), 0, loads)
    fits = jnp.max(loads) <= fast
    mine_want = lax.dynamic_index_in_dim(want, plane_index, 1, keepdims=False)
    mine_rank = lax.dynamic_index_in_dim(rank, plane_index, 1, keepdims=False)
    picks = mine_want[:, None, :] & (
        mine_rank[:, None, :] == jnp.arange(fast, dtype=jnp.int32)[None, :, None]
    )
    send_rows = jnp.sum(jnp.where(picks, below[None, None, :].astype(jnp.int32), 0), axis=2)
    steps = jnp.arange(planes, dtype=jnp.int32)
    upward = (plane_index + steps) % planes
    send_rows = jnp.sum(
        jnp.where(upward[:, None, None] == steps[None, :, None], send_rows[None], 0), axis=1
    )
    my_ids = lax.dynamic_index_in_dim(even_id, plane_index, 0, keepdims=False)
    my_rank = lax.dynamic_index_in_dim(rank, plane_index, 0, keepdims=False).reshape(-1)
    place = jnp.sum(jnp.where(my_ids[:, None] == ids[None, :], my_rank[None, :], 0), axis=1)
    my_step = (plane_index + planes - my_ids // plane_rows) % planes

    def exact(source, chunk):
        rows = stepped(send_rows) if chunk else send_rows
        if planes > MOST_SHIFTS:
            return [jnp.take(source, rows[k], axis=0, mode="clip") for k in range(planes)]
        return [source, *select_rows(rows[1:], source)]

    def whole(source, chunk):
        return [source] * planes

    def exchange(sources, select, index, between):
        received, arrived = [], []
        for chunk, source in enumerate(sources):
            sending = select(source, chunk)
            if received:
                sending, _ = lax.optimization_barrier((sending, received[-1]))
            received.append(across(sending))
            outgoing = gather_rows(index[min(chunk, 1)], received[-1], group, parts)
            outgoing, _ = lax.optimization_barrier((outgoing, after if arrived else odd_query))
            arrived.append(swap(outgoing, plane_groups))
            after = arrived[-1] if chunk else between(arrived[-1])
        return [a.reshape(lanes, wanted, piece, a.shape[2]) for a in arrived]

    odd_part = jnp.zeros((shards * capacity, columns + DH), F32)
    for k in range(parts):
        slot_want = slot_row - (part_index + parts - k) % parts * held
        slot_want = jnp.broadcast_to(slot_want.reshape(-1, 1), (shards * capacity, DH))
        odd_part = odd_attention(
            odd_query, slot_want, (early_shared[k], *late_rows[k]), weights, odd_part
        )

    returned = []

    def send_back(after):
        part, _ = lax.optimization_barrier((odd_part, after))
        part = lax.all_to_all(part.reshape(shards, capacity, columns + DH), "db", 0, 0, tiled=True)
        returned.append(part)
        return part

    def attend(select, index, between, odd_rows):
        early, *late = exchange(plane_pieces, select, index, between)
        early = project(early, weights)
        return even_attention(queries, late, weights, early, odd_rows())

    def odd_rows():
        return combine(my_slot, returned[0].reshape(shards * capacity, columns + DH), sequences)

    own_rows = [my_ids % plane_rows, stepped(my_ids % plane_rows)]
    fast_index = my_step * fast + jnp.minimum(place, fast - 1)
    fast_index = [fast_index] * CHUNKS
    if planes <= MOST_SHIFTS:
        fast_index = [
            jnp.where(my_step == 0, row, index + plane_rows - fast) for row, index in zip(own_rows, fast_index)
        ]
    result = attend(exact, fast_index, send_back, odd_rows)
    if fast < most:
        result = lax.cond(
            fits,
            lambda done: done,
            lambda done: attend(
                whole, [my_step * plane_rows + row for row in own_rows], lambda arrived: arrived, odd_rows
            ),
            result,
        )
    return result


def solution(mesh):
    placed = (
        P("db", "mp"),
        P(("db", "mp"), None, None),
        P("db", "mp"),
        P("db", "mp"),
        P("db", None),
        P("db", None),
    )

    return jax.shard_map(local, mesh=mesh, in_specs=placed, out_specs=P("db", "mp"), check_vma=False)
```

```python
import functools
import math

import jax
import jax.numpy as jnp
from jax import lax
from jax.experimental import pallas as pl
from jax.experimental.pallas import tpu as pltpu
from jax.sharding import PartitionSpec as P


DH = 128
SPAN = 64
SEQ = 128
LANES = 8
CHUNKS = 2
MOST_SHIFTS = 8
MOST_DEALS = 16
LOW = (SPAN - 1) // 16 * 16
FAST_SLOTS = 46
BF16 = jnp.bfloat16
F32 = jnp.float32
SCALE = 1.0 / math.sqrt(DH)
BOTH = ("db", "mp")
CONTRACT_LAST = (((1,), (1,)), ((), ()))


def project_rows(rows_refs, weight_ref):
    lanes, count, piece, _ = rows_refs[0].shape
    rows = [ref[...] for ref in rows_refs]
    stacked = jnp.concatenate(
        [
            jnp.concatenate([r[:, j].reshape(lanes * piece, r.shape[3]) for r in rows], axis=1)
            for j in range(count)
        ],
        axis=0,
    )
    return jnp.dot(stacked, weight_ref[...], preferred_element_type=F32).astype(BF16)


def project_body(rows_ref, weight_ref, out_ref):
    out_ref[...] = project_rows([rows_ref], weight_ref)


def project(rows, weights):
    lanes, count, piece, width = rows.shape
    per_step = math.gcd(count, 8)
    tokens = lanes * piece
    return pl.pallas_call(
        project_body,
        out_shape=jax.ShapeDtypeStruct((count * tokens, weights.shape[1]), BF16),
        grid=(count // per_step,),
        in_specs=[
            pl.BlockSpec((lanes, per_step, piece, width), lambda i: (0, i, 0, 0)),
            pl.BlockSpec(weights.shape, lambda i: (0, 0)),
        ],
        out_specs=pl.BlockSpec((per_step * tokens, weights.shape[1]), lambda i: (i, 0)),
        name="project",
    )(rows, weights)


def even_body(query_ref, *refs, per_step):
    rows_refs, (weight_ref, early_ref, odd_ref, out_ref) = refs[:-4], refs[-4:]
    columns = query_ref.shape[1]
    late = project_rows(rows_refs, weight_ref)
    span = late.shape[0] // per_step
    first = SPAN - 1
    position = LOW + lax.broadcasted_iota(jnp.int32, (SEQ - LOW, DH), 0)
    odd = [odd_ref[pl.ds(pl.program_id(0) * per_step + s, 1), :] for s in range(per_step)]
    blocks = [(s, h * DH) for s in range(per_step) for h in range(columns // DH)]

    def both(s, lo):
        at = slice(s * span, (s + 1) * span)
        return jnp.concatenate([early_ref[at, lo : lo + DH], late[at, lo : lo + DH]], axis=0)

    scores = [
        lax.dot_general(
            query_ref[s * SEQ + LOW : (s + 1) * SEQ, lo : lo + DH],
            both(s, lo),
            CONTRACT_LAST,
            preferred_element_type=F32,
        )
        * SCALE
        for s, lo in blocks
    ]
    largest = [jnp.max(x, axis=1, keepdims=True) for x in scores]
    expscore = [jnp.exp(x - m) for x, m in zip(scores, largest)]
    total = [jnp.sum(e, axis=1, keepdims=True) for e in expscore]
    mixed = [
        jnp.dot(e.astype(BF16), both(s, columns + lo), preferred_element_type=F32)
        for e, (s, lo) in zip(expscore, blocks)
    ]
    for s in range(per_step):
        out_ref[s * SEQ : s * SEQ + LOW, :] = jnp.zeros((LOW, columns), BF16)
    for (s, lo), over, under in zip(blocks, mixed, total):
        attended = over * (1.0 / under)
        attended = jnp.where(position == SEQ - 1, odd[s][:, lo : lo + DH], attended)
        attended = jnp.where(position < first, 0.0, attended)
        out_ref[s * SEQ + LOW : (s + 1) * SEQ, lo : lo + DH] = attended.astype(BF16)


def even_attention(queries, rows, weights, early, odd):
    columns = queries.shape[1]
    sequences = queries.shape[0] // SEQ
    lanes, count, piece, _ = rows[0].shape
    per_step = math.gcd(sequences, 2)
    rows_step = per_step * count // sequences
    query_spec = pl.BlockSpec((per_step * SEQ, columns), lambda i: (i, 0))
    return pl.pallas_call(
        functools.partial(even_body, per_step=per_step),
        out_shape=jax.ShapeDtypeStruct(queries.shape, BF16),
        grid=(sequences // per_step,),
        in_specs=[
            query_spec,
            *[pl.BlockSpec((lanes, rows_step, piece, r.shape[3]), lambda i: (0, i, 0, 0)) for r in rows],
            pl.BlockSpec(weights.shape, lambda i: (0, 0)),
            pl.BlockSpec((rows_step * lanes * piece, weights.shape[1]), lambda i: (i, 0)),
            pl.BlockSpec(odd.shape, lambda i: (0, 0)),
        ],
        out_specs=query_spec,
        name="even_attention",
    )(queries, *rows, weights, early, odd)


def combine_body(slot_ref, odd_ref, row_ref, *picked_refs):
    sequences, columns = row_ref.shape
    for i in range(sequences):
        for j, picked_ref in enumerate(picked_refs):
            picked_ref[i : i + 1, :] = odd_ref[pl.ds(slot_ref[i * len(picked_refs) + j], 1), :]
    for h in range(columns // DH):
        lo, hi = h * DH, (h + 1) * DH
        maxima = [p[:, columns + h : columns + h + 1] for p in picked_refs]
        sums = [p[:, columns + DH // 2 + h : columns + DH // 2 + h + 1] for p in picked_refs]
        top = functools.reduce(jnp.maximum, maxima)
        each = [jnp.exp(m - top) for m in maxima]
        under = sum(e * t for e, t in zip(each, sums))
        over = sum(e * p[:, lo:hi] for e, p in zip(each, picked_refs))
        row_ref[:, lo:hi] = over / under


def combine(slots, odd, sequences):
    columns = odd.shape[1] - DH
    return pl.pallas_call(
        combine_body,
        out_shape=jax.ShapeDtypeStruct((sequences, columns), F32),
        grid_spec=pltpu.PrefetchScalarGridSpec(
            num_scalar_prefetch=1,
            grid=(1,),
            in_specs=[pl.BlockSpec(odd.shape, lambda i, s: (0, 0))],
            out_specs=pl.BlockSpec((sequences, columns), lambda i, s: (0, 0)),
            scratch_shapes=[pltpu.VMEM((sequences, odd.shape[1]), F32)] * (slots.shape[0] // sequences),
        ),
        name="combine",
    )(slots, odd)


def gather_body(index_ref, *refs, count):
    sources, out_ref, stage_ref, sem_ref = refs[:count], refs[count], refs[count + 1], refs[count + 2]
    copies, wanted = out_ref.shape[1:3]
    starts = [sum(s.shape[0] for s in sources[:k]) for k in range(count)]
    base = pl.program_id(0) * wanted

    @pl.when(pl.program_id(0) == 0)
    def _():
        moves = [
            pltpu.make_async_copy(source, stage_ref.at[pl.ds(starts[k], source.shape[0])], sem_ref.at[k])
            for k, source in enumerate(sources)
        ]
        for move in moves:
            move.start()
        for move in moves:
            move.wait()

    def step(i, carry):
        row = stage_ref[index_ref[base + i]]
        for c in range(copies):
            out_ref[0, c, i] = row
        return carry

    lax.fori_loop(0, wanted, step, 0, unroll=8)


def gather_rows(index, sources, groups, copies):
    wanted = index.shape[0] // groups
    piece, width = sources[0].shape[1:]
    out = pl.pallas_call(
        functools.partial(gather_body, count=len(sources)),
        out_shape=jax.ShapeDtypeStruct((groups, copies, wanted, piece, width), sources[0].dtype),
        grid_spec=pltpu.PrefetchScalarGridSpec(
            num_scalar_prefetch=1,
            grid=(groups,),
            in_specs=[pl.BlockSpec(memory_space=pl.ANY) for _ in sources],
            out_specs=pl.BlockSpec((1, copies, wanted, piece, width), lambda i, s: (i, 0, 0, 0, 0)),
            scratch_shapes=[
                pltpu.VMEM((sum(s.shape[0] for s in sources), piece, width), sources[0].dtype),
                pltpu.SemaphoreType.DMA((len(sources),)),
            ],
        ),
        name="gather_rows",
    )(index, *sources)
    return out.reshape(groups * copies * wanted, piece, width)


def select_body(index_ref, source_ref, *out_refs):
    fast = out_refs[0].shape[0]

    def step(i, carry):
        for k, out_ref in enumerate(out_refs):
            out_ref[i] = source_ref[index_ref[k * fast + i]]
        return carry

    lax.fori_loop(0, fast, step, 0, unroll=2)


def select_rows(index, source):
    count, fast = index.shape
    block = pl.BlockSpec((fast,) + source.shape[1:], lambda i, s: (0, 0, 0))
    return pl.pallas_call(
        select_body,
        out_shape=[jax.ShapeDtypeStruct((fast,) + source.shape[1:], source.dtype)] * count,
        grid_spec=pltpu.PrefetchScalarGridSpec(
            num_scalar_prefetch=1,
            grid=(1,),
            in_specs=[pl.BlockSpec(source.shape, lambda i, s: (0, 0, 0))],
            out_specs=[block] * count,
        ),
        name="select_rows",
    )(index.reshape(-1), source)


def odd_body(query_ref, want_ref, *refs):
    rows_refs, (weight_ref, prior_ref, out_ref) = refs[:-3], refs[-3:]
    columns = query_ref.shape[1]
    heads = columns // DH
    _, per_step, piece, width = rows_refs[0].shape
    tokens = sum(ref.shape[0] for ref in rows_refs) * piece
    step = pl.program_id(0)

    @pl.when(step == 0)
    def _():
        out_ref[...] = prior_ref[...]

    pieces = [ref[...] for ref in rows_refs]
    stacked = jnp.concatenate(
        [p[:, r].reshape(p.shape[0] * piece, width) for r in range(per_step) for p in pieces], axis=0
    )
    projected = jnp.dot(stacked, weight_ref[...], preferred_element_type=F32).astype(BF16)
    want = want_ref[...] - step * per_step
    here = [want == r for r in range(per_step)]
    inside = (want >= 0) & (want < per_step)
    lane = lax.broadcasted_iota(jnp.int32, (want.shape[0], DH), 1)
    spans = [(h * DH, (h + 1) * DH) for h in range(heads)]
    scores = [
        lax.dot_general(
            query_ref[:, lo:hi], projected[:, lo:hi], CONTRACT_LAST, preferred_element_type=F32
        )
        * SCALE
        for lo, hi in spans
    ]
    mine = []
    for x in scores:
        chosen = jnp.zeros((want.shape[0], tokens), F32)
        for r in range(per_step):
            chosen = jnp.where(here[r], x[:, r * tokens : (r + 1) * tokens], chosen)
        mine.append(chosen)
    largest = [jnp.max(x, axis=1, keepdims=True) for x in mine]
    expscore = [jnp.exp(x - m) for x, m in zip(mine, largest)]
    total = [jnp.sum(e, axis=1, keepdims=True) for e in expscore]
    spread = [
        jnp.concatenate([jnp.where(here[r], e, 0.0) for r in range(per_step)], axis=1).astype(BF16)
        for e in expscore
    ]
    mixed = [
        jnp.dot(p, projected[:, columns + lo : columns + hi], preferred_element_type=F32)
        for p, (lo, hi) in zip(spread, spans)
    ]
    stats = out_ref[:, columns:]
    for h, (lo, hi) in enumerate(spans):
        out_ref[:, lo:hi] = jnp.where(inside, mixed[h], out_ref[:, lo:hi])
        stats = jnp.where(inside & (lane == h), largest[h], stats)
        stats = jnp.where(inside & (lane == DH // 2 + h), total[h], stats)
    out_ref[:, columns:] = stats


def odd_attention(queries, want, rows, weights, prior):
    slots, columns = queries.shape
    _, count, piece, width = rows[0].shape
    per_step = math.gcd(count, 4)
    return pl.pallas_call(
        odd_body,
        out_shape=jax.ShapeDtypeStruct(prior.shape, F32),
        grid=(count // per_step,),
        in_specs=[
            pl.BlockSpec((slots, columns), lambda i: (0, 0)),
            pl.BlockSpec((slots, DH), lambda i: (0, 0)),
            *[pl.BlockSpec((r.shape[0], per_step, piece, width), lambda i: (0, i, 0, 0)) for r in rows],
            pl.BlockSpec(weights.shape, lambda i: (0, 0)),
            pl.BlockSpec(prior.shape, lambda i: (0, 0)),
        ],
        out_specs=pl.BlockSpec(prior.shape, lambda i: (0, 0)),
        name="odd_attention",
    )(queries, want, *rows, weights, prior)


def local(queries, encodings, key_weight, value_weight, nbr_shard, nbr_row):
    shards = lax.axis_size("db")
    parts = lax.axis_size("mp")
    group = max(1, LANES // parts)
    lanes = group * parts
    planes = shards // group
    columns = queries.shape[1]
    held, tokens, width = encodings.shape
    piece = tokens // (lanes * CHUNKS)
    shard_rows = held * parts
    plane_rows = group * shard_rows
    span_count, neighbours = nbr_shard.shape
    sequences = queries.shape[0] // SEQ
    wanted = sequences * neighbours
    capacity = max(2, 4 * span_count // shards)
    most = min(plane_rows, group * wanted, group * group * capacity)
    fast = min(most, FAST_SLOTS)
    plane_groups = [[a * lanes + b for b in range(lanes)] for a in range(planes)]
    lane_groups = [[a * lanes + b for a in range(planes)] for b in range(lanes)]
    db_index = lax.axis_index("db")
    plane_index = db_index // group

    def swap(x, groups):
        return lax.all_to_all(x, BOTH, 0, 0, axis_index_groups=groups, tiled=True)

    def across(blocks):
        if planes > MOST_SHIFTS:
            stacked = jnp.stack(blocks)
            ordered = jnp.take(stacked, (jnp.arange(planes) - plane_index) % planes, axis=0, mode="clip")
            ordered = swap(ordered.reshape((-1,) + stacked.shape[2:]), lane_groups).reshape(stacked.shape)
            moved = jnp.take(ordered, (plane_index - jnp.arange(planes)) % planes, axis=0, mode="clip")
            return [moved.reshape((-1,) + stacked.shape[2:])]
        moved = [blocks[0]]
        for k in range(1, planes):
            pairs = [
                (a * lanes + b, (a + k) % planes * lanes + b) for a in range(planes) for b in range(lanes)
            ]
            moved.append(lax.ppermute(blocks[k], BOTH, pairs))
        return moved

    def deal(blocks, sign):
        if shards > MOST_DEALS:
            return lax.all_to_all(blocks, "db", 0, 0, tiled=True)
        dealt = [blocks[:1]]
        for k in range(1, shards):
            pairs = [(d, (d + sign * k) % shards) for d in range(shards)]
            dealt.append(lax.ppermute(blocks[k : k + 1], "db", pairs))
        return jnp.concatenate(dealt, axis=0)

    table = jnp.concatenate([nbr_shard.reshape(-1), nbr_row.reshape(-1)])
    table = jnp.broadcast_to(table[None, None], (shards, 1, table.shape[0]))
    table = lax.all_to_all(table, "db", 0, 0, tiled=True)
    table = table.reshape(shards, 2, sequences, SEQ // SPAN, neighbours)
    table_shard, table_row = table[:, 0], table[:, 1]

    weights = lax.all_gather(
        jnp.concatenate([key_weight, value_weight], axis=1), "db", axis=0, tiled=True
    )

    early_half, late_half = jnp.transpose(encodings.reshape(held, lanes, CHUNKS, piece, width), (2, 1, 0, 3, 4))
    first, _ = lax.optimization_barrier((early_half.reshape(lanes * held, piece, width), table))
    first = swap(first, plane_groups)

    odd_shard = table_shard[:, :, 1].reshape(shards, wanted)
    odd_row = table_row[:, :, 1].reshape(shards, wanted)
    earlier = jnp.arange(wanted)
    same = (odd_shard[:, :, None] == odd_shard[:, None, :]) & (earlier[None, None, :] < earlier[None, :, None])
    odd_rank = jnp.sum(same.astype(jnp.int32), axis=2)
    arriving = (odd_shard == db_index)[:, None, :] & (
        odd_rank[:, None, :] == jnp.arange(capacity, dtype=jnp.int32)[None, :, None]
    )
    slot_row = jnp.sum(jnp.where(arriving, odd_row[:, None, :] + 1, 0), axis=2) - 1
    place_of = odd_shard
    if shards <= MOST_DEALS:
        place_of = (odd_shard + shards - db_index) % shards
        slot_row = jnp.take(slot_row, (db_index + shards - jnp.arange(shards)) % shards, axis=0, mode="clip")
    my_slot = lax.dynamic_index_in_dim(place_of * capacity + odd_rank, db_index, 0, keepdims=False)
    slots = jnp.arange(shards * capacity, dtype=jnp.int32)
    chosen = my_slot[None, :] == slots[:, None]
    sender = jnp.sum(jnp.where(chosen, (earlier // neighbours).astype(jnp.int32)[None, :], 0), axis=1)
    last_rows = queries.reshape(sequences, SEQ, columns)[:, SEQ - 1]
    odd_query = jnp.take(last_rows, sender, axis=0, mode="clip").reshape(shards, capacity, columns)

    part_index = lax.axis_index("mp")

    def share(half, after):
        half, _ = lax.optimization_barrier((half, after))
        shared = [half]
        for k in range(1, parts):
            shared.append(lax.ppermute(half, "mp", [(m, (m + k) % parts) for m in range(parts)]))
        return shared

    by_lane = late_half.reshape(group, parts, held, piece, width)
    near = lax.dynamic_index_in_dim(by_lane, part_index, 1, keepdims=False)
    if parts == 2:
        other = lax.dynamic_index_in_dim(by_lane, 1 - part_index, 1, keepdims=False)
        ahead = share(other, table)[1]
        behind = share(near, ahead)[1]
        late_rows = [(late_half,), (ahead, behind)]
        second = [near, ahead]
    else:
        ahead = share(late_half, table)
        late_rows = [(half,) for half in ahead]
        second = [
            lax.dynamic_index_in_dim(
                half.reshape(group, parts, held, piece, width), part_index, 1, keepdims=False
            )
            for half in ahead
        ]
    second = jnp.concatenate(second, axis=1).reshape(group * shard_rows, piece, width)
    part_groups = [
        [a * lanes + g * parts + m for g in range(group)] for a in range(planes) for m in range(parts)
    ]
    second, _ = lax.optimization_barrier((second, first))
    if group > 1:
        second = swap(second, part_groups)
    early_shared = share(early_half, ahead)
    odd_query, _ = lax.optimization_barrier((odd_query, second if shards > MOST_DEALS else first))
    odd_query = deal(odd_query, 1)
    odd_query = odd_query.reshape(shards * capacity, columns)
    plane_pieces = [first, second]

    def stepped(row):
        step = (part_index + parts - row % shard_rows // held) % parts
        return row // shard_rows * shard_rows + step * held + row % held

    even_id = (table_shard[:, :, 0] * shard_rows + table_row[:, :, 0]).reshape(planes, group * wanted)
    ids = jnp.arange(planes * plane_rows, dtype=jnp.int32)
    want = jnp.any(even_id[:, :, None] == ids[None, None, :], axis=1).reshape(planes, planes, plane_rows)
    below = jnp.arange(plane_rows)
    before = (below[:, None] < below[None, :]).astype(BF16)
    rank = jnp.dot(want.astype(BF16), before, preferred_element_type=F32).astype(jnp.int32)
    loads = jnp.sum(want.astype(jnp.int32), axis=2)
    if planes <= MOST_SHIFTS:
        loads = jnp.where(jnp.eye(planes, dtype=jnp.bool_), 0, loads)
    fits = jnp.max(loads) <= fast
    mine_want = lax.dynamic_index_in_dim(want, plane_index, 1, keepdims=False)
    mine_rank = lax.dynamic_index_in_dim(rank, plane_index, 1, keepdims=False)
    picks = mine_want[:, None, :] & (
        mine_rank[:, None, :] == jnp.arange(fast, dtype=jnp.int32)[None, :, None]
    )
    send_rows = jnp.sum(jnp.where(picks, below[None, None, :].astype(jnp.int32), 0), axis=2)
    steps = jnp.arange(planes, dtype=jnp.int32)
    upward = (plane_index + steps) % planes
    send_rows = jnp.sum(
        jnp.where(upward[:, None, None] == steps[None, :, None], send_rows[None], 0), axis=1
    )
    my_ids = lax.dynamic_index_in_dim(even_id, plane_index, 0, keepdims=False)
    my_rank = lax.dynamic_index_in_dim(rank, plane_index, 0, keepdims=False).reshape(-1)
    place = jnp.sum(jnp.where(my_ids[:, None] == ids[None, :], my_rank[None, :], 0), axis=1)
    my_step = (plane_index + planes - my_ids // plane_rows) % planes

    def exact(source, chunk):
        rows = stepped(send_rows) if chunk else send_rows
        if planes > MOST_SHIFTS:
            return [jnp.take(source, rows[k], axis=0, mode="clip") for k in range(planes)]
        return [source, *select_rows(rows[1:], source)]

    def whole(source, chunk):
        return [source] * planes

    def exchange(sources, select, index, between):
        received, arrived = [], []
        for chunk, source in enumerate(sources):
            sending = select(source, chunk)
            if received:
                sending, _ = lax.optimization_barrier((sending, received[-1]))
            received.append(across(sending))
            outgoing = gather_rows(index[min(chunk, 1)], received[-1], group, parts)
            outgoing, _ = lax.optimization_barrier((outgoing, after if arrived else first))
            arrived.append(swap(outgoing, plane_groups))
            after = arrived[-1] if chunk else between(arrived[-1])
        return [a.reshape(lanes, wanted, piece, a.shape[2]) for a in arrived]

    odd_part = jnp.zeros((shards * capacity, columns + DH), F32)
    for k in range(parts):
        slot_want = slot_row - (part_index + parts - k) % parts * held
        slot_want = jnp.broadcast_to(slot_want.reshape(-1, 1), (shards * capacity, DH))
        odd_part = odd_attention(
            odd_query, slot_want, (early_shared[k], *late_rows[k]), weights, odd_part
        )

    returned = []

    def send_back(after):
        part = odd_part.reshape(shards, capacity, columns + DH)
        if shards > MOST_DEALS:
            part, _ = lax.optimization_barrier((part, after))
        part = deal(part, -1)
        returned.append(part)
        return part if shards > MOST_DEALS else after

    def attend(select, index, between, odd_rows):
        early, *late = exchange(plane_pieces, select, index, between)
        early = project(early, weights)
        return even_attention(queries, late, weights, early, odd_rows())

    def odd_rows():
        return combine(my_slot, returned[0].reshape(shards * capacity, columns + DH), sequences)

    own_rows = [my_ids % plane_rows, stepped(my_ids % plane_rows)]
    fast_index = my_step * fast + jnp.minimum(place, fast - 1)
    fast_index = [fast_index] * CHUNKS
    if planes <= MOST_SHIFTS:
        fast_index = [
            jnp.where(my_step == 0, row, index + plane_rows - fast) for row, index in zip(own_rows, fast_index)
        ]
    result = attend(exact, fast_index, send_back, odd_rows)
    if fast < most:
        result = lax.cond(
            fits,
            lambda done: done,
            lambda done: attend(
                whole, [my_step * plane_rows + row for row in own_rows], lambda arrived: arrived, odd_rows
            ),
            result,
        )
    return result


def solution(mesh):
    placed = (
        P("db", "mp"),
        P(("db", "mp"), None, None),
        P("db", "mp"),
        P("db", "mp"),
        P("db", None),
        P("db", None),
    )

    return jax.shard_map(local, mesh=mesh, in_specs=placed, out_specs=P("db", "mp"), check_vma=False)
```
